128 devices in a mesh: req: 16 (over z, y), mlp: 8 (over x, core).
Axes of the slice: x: 4, y: 4, z: 4, core: 2. Of those that a mesh axis runs over, the one named last changes fastest.
Arguments:
- tokens: bfloat16 [4096, 2048], P('req', 'mlp'), may hold values from -5 to 5
- attn_gain: float32 [2048], replicated, may hold values from 0.5 to 1.5
- mlp_gain: float32 [2048], replicated, may hold values from 0.5 to 1.5
- final_gain: float32 [2048], replicated, may hold values from 0.25 to 4
- q_gain: float32 [64], replicated, may hold values from 0.5 to 1.5
- k_gain: float32 [64], replicated, may hold values from 0.25 to 4
- w_query: bfloat16 [2048, 2048], P(None, 'mlp'), may hold values from -0.125 to 0.125
- w_keyval: bfloat16 [2048, 1024], P(None, 'mlp'), may hold values from -0.125 to 0.125
- w_out: bfloat16 [2048, 2048], P('mlp'), may hold values from -0.125 to 0.125
- w_gate: bfloat16 [2048, 8192], P(None, 'mlp'), may hold values from -0.125 to 0.125
- w_up: bfloat16 [2048, 8192], P(None, 'mlp'), may hold values from -0.125 to 0.125
- w_down: bfloat16 [8192, 2048], P('mlp'), may hold values from -0.0625 to 0.0625
- w_head: bfloat16 [2048, 65536], P('req', 'mlp'), may hold values from -0.42 to 0.42
- targets: int32 [4096], P('req'), may hold values from 0 to 65535
- req_lengths: int32 [16, 4], P('req'), may hold values from 1 to 128, 256 in all within a row
- req_tenant: int32 [16, 4], P('req'), may hold values from 0 to 3
- prefix_piece: int32 [16], replicated, may hold values from 0 to 15, each once
- prefix_kv: bfloat16 [16, 1024, 1024], P('req', None, 'mlp'), may hold values from -160 to 160
Outputs:
- hidden_out: bfloat16 [4096, 2048], P('req', 'mlp')
- logprob: float32 [4096], P('req')
The draws below stay inside these ranges and needn't reach their ends.
Inputs may be any that keep to these rules, and one draw needn't show every extreme that they name: `req_lengths`: each row sums to 256; its longest request has exactly 128 tokens. `prefix_piece`: every piece number appears once; piece n is part n % 4 of the prefix of tenant n // 4.
All inputs are finite; a program needn't handle non-finite values.
Results may differ from the reference program's by a relative error of at most 0.023.
Values may be sent and summed in bfloat16 or wider, within the bound.
A program may use at most 128 MiB of HBM per device.

```python
import math
import jax
import jax.numpy as jnp
import numpy as np
from jax import lax

D = 2048
H = 32
KVH = 8
HD = 64
FF = 8192
VOCAB = 65536
TENANTS = 4
PLEN = 4096
RPG = 4
TOK_GRP = 256
LMOST = 128
PSPLIT = 4
PSLAB = 1024
TOKENS = 4096
N_REQ = 16


def draw_prefix_kv(key, part):
    key_base = jax.random.fold_in(key, 0)
    full_shape = (N_REQ, PSLAB, 2 * HD * KVH)
    return jnp.clip(jax.random.normal(key_base, full_shape, jnp.float32), -4.0, 4.0).astype(jnp.bfloat16)


def draw_tokens(key, part):
    key_base = jax.random.fold_in(key, 1)
    return jnp.clip(jax.random.normal(key_base, (TOKENS, D), jnp.float32), -5.0, 5.0).astype(jnp.bfloat16)


def draw_w_head(key, part):
    key_base = jax.random.fold_in(key, 3)
    return jnp.clip(0.07 * jax.random.normal(key_base, (D, VOCAB), jnp.float32), -0.42, 0.42).astype(jnp.bfloat16)


def plant(result, own_key, low, largest):
    shape = result.shape
    index_at = [jax.random.randint(jax.random.fold_in(own_key, axis), (), 0, shape[axis]) for axis in range(len(shape))]
    result = result.at[tuple(index_at)].set(low)
    longest = shape.index(max(shape))
    index_at[longest] = (index_at[longest] + 1) % shape[longest]
    return result.at[tuple(index_at)].set(largest)


def block_scale(own_key, dims, shards, least, high):
    factor_of, own = 1.0, jax.random.fold_in(own_key, 6)
    for dim, blocks in shards:
        draws = jnp.exp(jax.random.uniform(jax.random.fold_in(own, dim), (blocks,), jnp.float32, least / len(shards), high / len(shards)))
        factor_of = factor_of * jnp.repeat(draws, dims[dim] // blocks).reshape([-1 if axis == dim else 1 for axis in range(len(dims))])
    return factor_of


def profile(count, total, reach, slope):
    portions = [(1 << 20) // math.isqrt(standing ** slope) + 1 for standing in range(2, count + 1)]
    rest, counts = total - reach - (count - 1), [1] * (count - 1)
    while rest > 0:
        candidates = [i for i in range(count - 1) if counts[i] < reach]
        mass, remaining = sum([portions[i] for i in candidates]), rest
        for i in candidates:
            addition = min(reach - counts[i], max(1, remaining * portions[i] // mass), rest)
            counts[i] = counts[i] + addition
            rest = rest - addition
    return np.array([reach] + counts)


def uneven_parts(key, number_of, total, most, lean):
    if number_of == 2:
        one = jax.random.randint(key, (), max(1, total - most), min(most, total - 1) + 1)
        return jnp.stack([one, total - one])
    tallies = jnp.asarray(profile(number_of, total, most, lean), jnp.int32)
    couples = (number_of - 1) // 2
    source_of, taker = tallies[1:1 + 2 * couples:2], tallies[2:2 + 2 * couples:2]
    slack = jnp.minimum(source_of - 1, most - taker)
    moved = jax.random.randint(jax.random.fold_in(key, 1), (couples,), 0, 1 << 20) % (slack + 1)
    tallies = tallies.at[1:1 + 2 * couples:2].set(source_of - moved).at[2:2 + 2 * couples:2].set(taker + moved)
    return tallies[jax.random.permutation(jax.random.fold_in(key, 2), number_of)]


def scatter_about(key, shape, width, bound, cuts=(), kind=jnp.bfloat16):
    level = block_scale(key, shape, cuts, -0.22, 0.18) if cuts else 1.0
    values = jax.random.normal(key, shape, jnp.float32) * width * level
    return jnp.minimum(jnp.maximum(values, -bound), bound).astype(kind)


def setup_inputs(seed: int = 0) -> dict:
    splits = jax.random.split(jax.random.key(seed), 19)
    tokens = draw_tokens(jax.random.fold_in(splits[18], 71), 0)
    attn_gain = jnp.clip(1.0 + 0.1 * jax.random.normal(splits[1], (D,), jnp.float32), 0.5, 1.5)
    mlp_gain = jnp.clip(1.0 + 0.1 * jax.random.normal(splits[2], (D,), jnp.float32), 0.5, 1.5)
    final_gain = jnp.clip(jnp.exp(jax.random.uniform(splits[3], (D,), jnp.float32, math.log(0.25), math.log(4.0))), 0.25, 4.0)
    q_gain = jnp.clip(1.0 + 0.1 * jax.random.normal(splits[4], (HD,), jnp.float32), 0.5, 1.5)
    k_gain = jnp.clip(jnp.exp(jax.random.uniform(splits[5], (HD,), jnp.float32, math.log(0.25), math.log(4.0))), 0.25, 4.0)
    w_query = scatter_about(splits[6], (D, H * HD), D ** -0.5, 0.125, ((1, 8),))
    w_keyval = scatter_about(splits[7], (D, KVH * 2 * HD), D ** -0.5, 0.125, ((1, 8),))
    w_out = scatter_about(splits[8], (H * HD, D), (H * HD) ** -0.5, 0.125, ((0, 8),))
    w_gate = scatter_about(splits[9], (D, FF), D ** -0.5, 0.125, ((1, 8),))
    w_up = scatter_about(splits[10], (D, FF), D ** -0.5, 0.125, ((1, 8),))
    w_down = scatter_about(splits[11], (FF, D), FF ** -0.5, 0.0625, ((0, 8),))
    w_head = draw_w_head(jax.random.fold_in(splits[18], 71), 0)
    targets = plant(jax.random.randint(splits[13], (TOKENS,), 0, VOCAB), jax.random.fold_in(splits[13], 1), 0, VOCAB - 1).astype(jnp.int32)
    req_lengths = jax.vmap(lambda own: uneven_parts(own, RPG, TOK_GRP, LMOST, 2))(jax.random.split(splits[14], N_REQ)).reshape((N_REQ, RPG)).astype(jnp.int32)
    req_tenant = plant(jax.random.randint(splits[15], (N_REQ, RPG), 0, TENANTS), jax.random.fold_in(splits[15], 1), 0, TENANTS - 1).astype(jnp.int32)
    prefix_piece = jax.random.permutation(splits[16], N_REQ).astype(jnp.int32)
    prefix_kv = draw_prefix_kv(jax.random.fold_in(splits[18], 71), 0)
    return dict(tokens=tokens, attn_gain=attn_gain, mlp_gain=mlp_gain, final_gain=final_gain, q_gain=q_gain, k_gain=k_gain, w_query=w_query, w_keyval=w_keyval, w_out=w_out, w_gate=w_gate, w_up=w_up, w_down=w_down, w_head=w_head, targets=targets, req_lengths=req_lengths, req_tenant=req_tenant, prefix_piece=prefix_piece, prefix_kv=prefix_kv)


EPS = 1e-05
LOG_THETA = math.log(1000000.0)
NEG = -1e+30

def rms_norm(values, gain):
    return values * lax.rsqrt(lax.optimization_barrier(jnp.mean(values * values, axis=-1, keepdims=True)) + EPS) * gain

def rope_tables(position, size):
    half = size // 2
    freq = jnp.exp(jnp.arange(half, dtype=jnp.float32) * (-2.0 * LOG_THETA / size))
    angle = position[:, None] * freq[None, :]
    return (jnp.cos(angle), jnp.sin(angle))

def rotate(values, cosine, sine):
    half = values.shape[-1] // 2
    first = values[..., :half]
    second = values[..., half:]
    cosine = cosine[:, None, :]
    sine = sine[:, None, :]
    return jnp.concatenate([first * cosine - second * sine, first * sine + second * cosine], axis=-1)

def row_layout(lengths, tenants, count):
    ends = jnp.cumsum(lengths).astype(jnp.int32)
    row_ids = jnp.arange(count, dtype=jnp.int32)
    request = lax.optimization_barrier(jnp.sum((row_ids[:, None] >= ends[None, :]).astype(jnp.int32), axis=1)).astype(jnp.int32)
    onehot = (request[:, None] == jnp.arange(lengths.shape[0], dtype=jnp.int32)[None, :]).astype(jnp.int32)
    starts = (ends - lengths).astype(jnp.int32)
    offset = (row_ids - lax.optimization_barrier(jnp.sum(onehot * starts[None, :], axis=1))).astype(jnp.int32)
    tenant = lax.optimization_barrier(jnp.sum(onehot * tenants[None, :], axis=1)).astype(jnp.int32)
    return (request, offset, tenant)

def reference(tokens, attn_gain, mlp_gain, final_gain, q_gain, k_gain, w_query, w_keyval, w_out, w_gate, w_up, w_down, w_head, targets, req_lengths, req_tenant, prefix_piece, prefix_kv):
    group = H // KVH
    scale = HD ** (-0.5)
    prefix = prefix_kv.reshape(N_REQ * PSLAB, KVH, 2, HD)
    pre_keys = prefix[:, :, 0].transpose(1, 0, 2)
    pre_vals = prefix[:, :, 1].transpose(1, 0, 2)
    key_tenant = jnp.repeat((prefix_piece // PSPLIT).astype(jnp.int32), PSLAB)

    def one_group(index):
        stream = lax.dynamic_slice_in_dim(tokens, (index * TOK_GRP).astype(jnp.int32), TOK_GRP, 0)
        lengths = lax.dynamic_index_in_dim(req_lengths, index, 0, keepdims=False)
        tenants = lax.dynamic_index_in_dim(req_tenant, index, 0, keepdims=False)
        wanted = lax.dynamic_slice_in_dim(targets, (index * TOK_GRP).astype(jnp.int32), TOK_GRP, 0)
        stream_f = stream.astype(jnp.float32)
        normed = rms_norm(stream_f, attn_gain).astype(jnp.bfloat16)
        query = jnp.dot(normed, w_query, preferred_element_type=jnp.float32).reshape(TOK_GRP, H, HD)
        keyval = jnp.dot(normed, w_keyval, preferred_element_type=jnp.float32).reshape(TOK_GRP, KVH, 2, HD)
        request, offset, tenant = row_layout(lengths, tenants, TOK_GRP)
        cosine, sine = rope_tables((PLEN + offset).astype(jnp.float32), HD)
        query = rotate(rms_norm(query, q_gain), cosine, sine).astype(jnp.bfloat16)
        own_keys = rotate(rms_norm(keyval[:, :, 0], k_gain), cosine, sine).astype(jnp.bfloat16).transpose(1, 0, 2)
        own_vals = keyval[:, :, 1].astype(jnp.bfloat16).transpose(1, 0, 2)
        queries = query.reshape(TOK_GRP, KVH, group, HD).transpose(1, 2, 0, 3).reshape(KVH, group * TOK_GRP, HD)
        row_ids = jnp.arange(TOK_GRP, dtype=jnp.int32)
        causal = (request[:, None] == request[None, :]) & (row_ids[None, :] <= row_ids[:, None])
        seen_prefix = tenant[:, None] == key_tenant[None, :]
        seen = jnp.tile(jnp.concatenate([seen_prefix, causal], axis=1), (group, 1))

        def one_head(kv_index):
            qhead = lax.dynamic_index_in_dim(queries, kv_index, 0, keepdims=False)
            keys = jnp.concatenate([lax.dynamic_index_in_dim(pre_keys, kv_index, 0, keepdims=False), lax.dynamic_index_in_dim(own_keys, kv_index, 0, keepdims=False)], axis=0)
            vals = jnp.concatenate([lax.dynamic_index_in_dim(pre_vals, kv_index, 0, keepdims=False), lax.dynamic_index_in_dim(own_vals, kv_index, 0, keepdims=False)], axis=0)
            scores = jnp.dot(qhead, keys.T, preferred_element_type=jnp.float32) * scale
            scores = jnp.where(seen, scores, NEG)
            top = lax.optimization_barrier(jnp.max(scores, axis=1, keepdims=True))
            weights = jnp.where(seen, jnp.exp(scores - top), 0.0)
            total = lax.optimization_barrier(jnp.sum(weights, axis=1, keepdims=True))
            accum = jnp.dot(weights.astype(jnp.bfloat16), vals, preferred_element_type=jnp.float32)
            return accum / total
        heads = lax.map(one_head, jnp.arange(KVH, dtype=jnp.int32))
        attended = heads.reshape(KVH, group, TOK_GRP, HD).transpose(2, 0, 1, 3).reshape(TOK_GRP, H * HD).astype(jnp.bfloat16)
        mid = (stream_f + jnp.dot(attended, w_out, preferred_element_type=jnp.float32)).astype(jnp.bfloat16)
        mid_f = mid.astype(jnp.float32)
        normed_mid = rms_norm(mid_f, mlp_gain).astype(jnp.bfloat16)
        gate = jnp.dot(normed_mid, w_gate, preferred_element_type=jnp.float32)
        upper = jnp.dot(normed_mid, w_up, preferred_element_type=jnp.float32)
        inner = (jax.nn.silu(gate) * upper).astype(jnp.bfloat16)
        hidden = (mid_f + jnp.dot(inner, w_down, preferred_element_type=jnp.float32)).astype(jnp.bfloat16)
        normed_out = rms_norm(hidden.astype(jnp.float32), final_gain).astype(jnp.bfloat16)
        logits = jnp.dot(normed_out, w_head, preferred_element_type=jnp.float32)
        top = lax.optimization_barrier(jnp.max(logits, axis=1))
        total = lax.optimization_barrier(jnp.sum(jnp.exp(logits - top[:, None]), axis=1))
        picked = jnp.take_along_axis(logits, wanted[:, None].astype(jnp.int32), axis=1)[:, 0]
        return (hidden, picked - top - jnp.log(total))
    hidden_all, logprob_all = lax.map(one_group, jnp.arange(N_REQ, dtype=jnp.int32))
    return (hidden_all.reshape(TOKENS, D), logprob_all.reshape(TOKENS))
```

```python
import functools
import math

import jax
import jax.numpy as jnp
from jax import lax
from jax.experimental import pallas as pl
from jax.experimental.pallas import tpu as pltpu
from jax.sharding import Mesh
from jax.sharding import PartitionSpec as P

TENANTS = 4
PLEN = 4096
BLOCK = 64

EPS = 1e-05
LOG_THETA = math.log(1000000.0)
NEG = -1e30


def rms_norm(values, gain):
    return values * lax.rsqrt(jnp.mean(values * values, axis=-1, keepdims=True) + EPS) * gain


def rope_tables(position, size):
    half = size // 2
    freq = jnp.exp(jnp.arange(half, dtype=jnp.float32) * (-2.0 * LOG_THETA / size))
    angle = position[:, None] * freq[None, :]
    return (jnp.cos(angle), jnp.sin(angle))


def rotate(values, cosine, sine):
    half = values.shape[-1] // 2
    first = values[..., :half]
    second = values[..., half:]
    cosine = cosine[:, None, :]
    sine = sine[:, None, :]
    return jnp.concatenate(
        [first * cosine - second * sine, first * sine + second * cosine], axis=-1
    )


def row_layout(lengths, count):
    ends = jnp.cumsum(lengths)
    row_ids = jnp.arange(count, dtype=jnp.int32)
    request = jnp.sum((row_ids[:, None] >= ends[None, :]).astype(jnp.int32), axis=1)
    onehot = (request[:, None] == jnp.arange(lengths.shape[0], dtype=jnp.int32)[None, :]).astype(
        jnp.int32
    )
    starts = ends - lengths
    offset = row_ids - jnp.sum(onehot * starts[None, :], axis=1)
    return (starts, ends, offset)


def dot_nt(a, b):
    return lax.dot_general(a, b, (((1,), (1,)), ((), ())), preferred_element_type=jnp.float32)


def attention_kernel(requests, split, start_ref, end_ref, tenant_ref, slot_ref,
                     q_ref, own_ref, kv_ref, out_ref, best_ref, total_ref, accum_ref):
    block = pl.program_id(0)
    queries = q_ref[0]
    count = queries.shape[0]
    rows = own_ref.shape[0]
    row = (lax.broadcasted_iota(jnp.int32, (count, 1), 0) & (BLOCK - 1)) + block * BLOCK
    col = lax.broadcasted_iota(jnp.int32, (1, rows), 1)
    row_request = jnp.zeros((count, 1), jnp.int32)
    col_request = jnp.zeros((1, rows), jnp.int32)
    for r in range(requests):
        row_request += (row >= end_ref[r]).astype(jnp.int32)
        col_request += (col >= end_ref[r]).astype(jnp.int32)
    seen = (row_request == col_request) & (col <= row)
    own = own_ref[...]
    scores = jnp.where(seen, dot_nt(queries, own), NEG)
    best = jnp.max(scores, axis=1, keepdims=True)
    weights = jnp.where(seen, jnp.exp(scores - best), 0.0)
    best_ref[...] = best
    total_ref[...] = jnp.sum(weights, axis=1, keepdims=True)
    accum_ref[...] = jnp.dot(weights.astype(jnp.bfloat16), own, preferred_element_type=jnp.float32)
    for r in range(requests):

        @pl.when((end_ref[r] > block * BLOCK) & (start_ref[r] < block * BLOCK + BLOCK))
        def _():
            inside = row_request == r
            tenant = tenant_ref[r]

            def piece(index, carry):
                keyval = kv_ref[slot_ref[tenant * split + index]]
                part = dot_nt(queries, keyval)
                old = best_ref[...]
                new = jnp.where(inside, jnp.maximum(old, jnp.max(part, axis=1, keepdims=True)), old)
                keep = jnp.exp(old - new)
                piece_weights = jnp.exp(part - jnp.where(inside, new, -NEG))
                best_ref[...] = new
                total_ref[...] = total_ref[...] * keep + jnp.sum(piece_weights, axis=1, keepdims=True)
                accum_ref[...] = accum_ref[...] * keep + jnp.dot(
                    piece_weights.astype(jnp.bfloat16), keyval, preferred_element_type=jnp.float32
                )
                return carry

            lax.fori_loop(0, split, piece, 0)

    out_ref[0] = (accum_ref[...] / total_ref[...]).astype(jnp.bfloat16)


def attention(starts, ends, tenants, slots, queries, own, pieces):
    blocks, count, width = queries.shape
    smem = pl.BlockSpec(memory_space=pltpu.SMEM)
    return pl.pallas_call(
        functools.partial(attention_kernel, starts.shape[0], slots.shape[0] // TENANTS),
        grid=(blocks,),
        in_specs=[smem, smem, smem, smem,
                  pl.BlockSpec((1, count, width), lambda i: (i, 0, 0)),
                  pl.BlockSpec(own.shape, lambda i: (0, 0)),
                  pl.BlockSpec(pieces.shape, lambda i: (0, 0, 0), pipeline_mode=pl.Buffered(1))],
        out_specs=pl.BlockSpec((1, count, width), lambda i: (i, 0, 0)),
        out_shape=jax.ShapeDtypeStruct((blocks, count, width), jnp.bfloat16),
        scratch_shapes=[pltpu.VMEM((count, 1), jnp.float32), pltpu.VMEM((count, 1), jnp.float32),
                        pltpu.VMEM((count, width), jnp.float32)],
        cost_estimate=pl.CostEstimate(flops=4 * 1024 * 4096 * 128 * 2, bytes_accessed=5 << 20,
                                      transcendentals=1 << 23),
        name="attention",
    )(starts, ends, tenants, slots, queries, own, pieces)


def spread_head(w_head, ny):
    me = lax.axis_index("y")
    depth, vocab = w_head.shape
    part = vocab // ny
    mine = lax.dynamic_slice_in_dim(w_head, me * part, part, 1)
    slab = jnp.zeros((ny * depth, part), w_head.dtype)
    slab = lax.dynamic_update_slice_in_dim(slab, mine, me * depth, 0)
    for shift in range(1, ny):
        give = lax.dynamic_slice_in_dim(w_head, ((me + shift) % ny) * part, part, 1)
        got = lax.ppermute(give, "y", [(i, (i + shift) % ny) for i in range(ny)])
        slab = lax.dynamic_update_slice_in_dim(slab, got, ((me - shift) % ny) * depth, 0)
    return lax.all_gather(slab, "z", axis=0, tiled=True)


def body(
    tokens,
    attn_gain,
    mlp_gain,
    final_gain,
    q_gain,
    k_gain,
    w_query,
    w_keyval,
    w_out,
    w_gate,
    w_up,
    w_down,
    w_head,
    targets,
    req_lengths,
    req_tenant,
    prefix_piece,
    prefix_kv,
):
    rows = tokens.shape[0]
    head_size = q_gain.shape[0]
    local_q = w_query.shape[1] // head_size
    ny = lax.axis_size("y")
    scale = head_size ** (-0.5)
    blocks = rows // BLOCK
    stream = lax.all_gather(tokens, "mlp", axis=1, tiled=True)
    pieces = lax.all_gather(prefix_kv, ("z", "y"), axis=0, tiled=True)
    head = spread_head(w_head, ny)

    normed = rms_norm(stream.astype(jnp.float32), attn_gain).astype(jnp.bfloat16)
    query = jnp.dot(normed, w_query, preferred_element_type=jnp.float32).reshape(
        rows, local_q, head_size
    )
    keyval = jnp.dot(normed, w_keyval, preferred_element_type=jnp.float32).reshape(
        rows, 1, 2, head_size
    )
    starts, ends, offset = row_layout(req_lengths[0], rows)
    cosine, sine = rope_tables((PLEN + offset).astype(jnp.float32), head_size)
    query = rotate(rms_norm(query, q_gain), cosine, sine).astype(jnp.bfloat16) * jnp.bfloat16(scale)
    own = jnp.concatenate(
        [rotate(rms_norm(keyval[:, :, 0], k_gain), cosine, sine)[:, 0], keyval[:, 0, 1]], axis=-1
    ).astype(jnp.bfloat16)
    queries = (
        query.reshape(blocks, BLOCK, local_q, head_size)
        .transpose(0, 2, 1, 3)
        .reshape(blocks, local_q * BLOCK, head_size)
    )
    queries = jnp.pad(queries, ((0, 0), (0, 0), (0, head_size)))
    order = jnp.arange(prefix_piece.shape[0], dtype=jnp.int32)
    slots = jnp.sum(
        jnp.where(prefix_piece[None, :] == order[:, None], order[None, :], 0), axis=1
    ).astype(jnp.int32)
    out = attention(starts, ends, req_tenant[0], slots, queries, own, pieces)
    attended = (
        out[:, :, head_size:]
        .reshape(blocks, local_q, BLOCK, head_size)
        .transpose(0, 2, 1, 3)
        .reshape(rows, local_q * head_size)
    )
    attn_proj = jnp.dot(attended, w_out, preferred_element_type=jnp.float32)
    attn_part = lax.psum_scatter(
        attn_proj.astype(jnp.bfloat16), "mlp", scatter_dimension=1, tiled=True
    ).astype(jnp.float32)
    mid_share = (tokens.astype(jnp.float32) + attn_part).astype(jnp.bfloat16)
    middle = lax.all_gather(mid_share, "mlp", axis=1, tiled=True)
    normed_mid = rms_norm(middle.astype(jnp.float32), mlp_gain).astype(jnp.bfloat16)
    gate = jnp.dot(normed_mid, w_gate, preferred_element_type=jnp.float32)
    upper = jnp.dot(normed_mid, w_up, preferred_element_type=jnp.float32)
    inner = (jax.nn.silu(gate) * upper).astype(jnp.bfloat16)
    down = jnp.dot(inner, w_down, preferred_element_type=jnp.float32)
    down_part = lax.psum_scatter(
        down.astype(jnp.bfloat16), "mlp", scatter_dimension=1, tiled=True
    ).astype(jnp.float32)
    out_share = (mid_share.astype(jnp.float32) + down_part).astype(jnp.bfloat16)
    near = lax.all_gather(out_share, "y", axis=0, tiled=True)
    hidden_full = lax.all_gather(near, "mlp", axis=1, tiled=True)
    normed_out = rms_norm(hidden_full.astype(jnp.float32), final_gain).astype(jnp.bfloat16)
    wanted = lax.all_gather(targets, "y", axis=0, tiled=True)
    logits = jnp.dot(normed_out, head, preferred_element_type=jnp.float32)
    vocab_local = head.shape[1]
    vocab_start = (lax.axis_index("mlp") * ny + lax.axis_index("y")) * vocab_local
    top = jnp.max(logits, axis=1)
    hit = wanted[:, None] - vocab_start == jnp.arange(vocab_local, dtype=jnp.int32)[None, :]
    stats = jnp.stack(
        [
            top,
            jnp.sum(jnp.exp(logits - top[:, None]), axis=1),
            jnp.sum(jnp.where(hit, logits, 0.0), axis=1),
        ]
    )
    every = lax.all_gather(stats, ("y", "mlp"), axis=0)
    every = lax.dynamic_slice_in_dim(every, lax.axis_index("y") * rows, rows, 2)
    top = jnp.max(every[:, 0], axis=0)
    total = jnp.sum(every[:, 1] * jnp.exp(every[:, 0] - top[None, :]), axis=0)
    logprob = jnp.sum(every[:, 2], axis=0) - top - jnp.log(total)
    return (out_share, logprob)


def solution(mesh):
    req = ("z", "y")
    in_specs = (
        P(req, "mlp"),
        P(),
        P(),
        P(),
        P(),
        P(),
        P(None, "mlp"),
        P(None, "mlp"),
        P("mlp", None),
        P(None, "mlp"),
        P(None, "mlp"),
        P("mlp", None),
        P(req, "mlp"),
        P(req),
        P(req, None),
        P(req, None),
        P(),
        P(req, None, "mlp"),
    )
    out_specs = (P(req, "mlp"), P(req))
    split = Mesh(mesh.devices.reshape(4, 4, -1), ("z", "y", "mlp"))
    return jax.shard_map(body, mesh=split, in_specs=in_specs, out_specs=out_specs, check_vma=False)
```

```python
import functools
import math

import jax
import jax.numpy as jnp
from jax import lax
from jax.experimental import pallas as pl
from jax.experimental.pallas import tpu as pltpu
from jax.sharding import Mesh
from jax.sharding import PartitionSpec as P

TENANTS = 4
PLEN = 4096
BLOCK = 64
EPS = 1e-05
LOG_THETA = math.log(1000000.0)
NEG = -1e30
RING = 4
MESH = pl.DeviceIdType.MESH
F32 = jnp.float32
BF16 = jnp.bfloat16


def dot(a, b):
    return jnp.dot(a, b, preferred_element_type=F32)


def dot_nt(a, b):
    return lax.dot_general(a, b, (((1,), (1,)), ((), ())), preferred_element_type=F32)


def remote(src, dst, send_sem, recv_sem, **device):
    return pltpu.make_async_remote_copy(
        src_ref=src, dst_ref=dst, send_sem=send_sem, recv_sem=recv_sem,
        device_id=device, device_id_type=MESH,
    )


def arrived(ref, sem):
    pltpu.make_async_copy(ref, ref, sem).wait()


def greet(peers):
    barrier = pltpu.get_barrier_semaphore()
    for peer in peers:
        pl.semaphore_signal(barrier, inc=1, device_id=peer, device_id_type=MESH)
    pl.semaphore_wait(barrier, len(peers))


def ring_of(axis, core):
    me = lax.axis_index(axis)
    ahead = lax.rem(me + 1 + 2 * core, RING)
    back = lax.rem(me + 3 + 2 * core, RING)
    far = lax.rem(me + 2, RING)
    return (me, ahead, back, far)


class Gather:
    def __init__(self, slots, send, recv):
        self.slots, self.send, self.recv, self.sent = slots, send, recv, []
        self.core = lax.axis_index("c")
        self.x, self.ahead, self.back, self.far = ring_of("x", self.core)

    def push(self, at, core, src=None, **device):
        slot = 2 * at + core
        copy = remote(self.slots.at[slot] if src is None else src, self.slots.at[slot],
                      self.send.at[len(self.sent)], self.recv.at[slot], **device)
        copy.start()
        self.sent.append(copy)

    def wait(self, at, core):
        slot = 2 * at + core
        arrived(self.slots.at[slot], self.recv.at[slot])

    def open(self, src=None):
        self.push(self.x, self.core, src, x=self.ahead)
        self.push(self.x, self.core, src, x=self.back)
        self.push(self.x, self.core, src, c=1 - self.core)

    def relay(self):
        self.wait(self.back, self.core)
        self.push(self.back, self.core, x=self.ahead)
        self.push(self.back, self.core, c=1 - self.core)
        self.wait(self.ahead, self.core)
        self.push(self.ahead, self.core, c=1 - self.core)

    def close(self):
        self.wait(self.far, self.core)
        self.push(self.far, self.core, c=1 - self.core)
        for x in (self.x, self.back, self.ahead, self.far):
            self.wait(x, 1 - self.core)

    def finish(self):
        for copy in self.sent:
            copy.wait_send()


def scatter_sum(partial, stage, paired, inbox, send, pair_sem, in_sem):
    core = lax.axis_index("c")
    x, ahead, back, far = ring_of("x", core)
    sent = []

    def push(value, dst, recv, **device):
        index = len(sent)
        stage[index] = value.astype(BF16)
        copy = remote(stage.at[index], dst, send.at[index], recv, **device)
        copy.start()
        sent.append(copy)

    def chip(to):
        mine = partial(2 * to + core)
        arrived(paired.at[to], pair_sem.at[to])
        return mine + paired[to].astype(F32)

    for to in (far, back, ahead, x):
        push(partial(2 * to + 1 - core), paired.at[to], pair_sem.at[to], c=1 - core)
    push(chip(far), inbox.at[2], in_sem.at[2], x=ahead)
    push(chip(back), inbox.at[1], in_sem.at[1], x=back)
    value = chip(ahead)
    arrived(inbox.at[2], in_sem.at[2])
    push(value + inbox[2].astype(F32), inbox.at[0], in_sem.at[0], x=ahead)
    value = chip(x)
    for slot in (1, 0):
        arrived(inbox.at[slot], in_sem.at[slot])
        value += inbox[slot].astype(F32)
    for copy in sent:
        copy.wait_send()
    return value


def normalise(blocks, gain_ref, normed):
    count, rows, width = blocks.shape
    square = jnp.zeros((rows, 1), F32)
    for m in range(count):
        value = blocks[m].astype(F32)
        square += jnp.sum(value * value, axis=1, keepdims=True)
    factor = lax.rsqrt(square / (count * width) + EPS)
    for m in range(count):
        columns = slice(m * width, (m + 1) * width)
        normed[:, columns] = (blocks[m].astype(F32) * factor * gain_ref[:, columns]).astype(BF16)


def x_peers():
    core = lax.axis_index("c")
    _, ahead, back, _ = ring_of("x", core)
    return [dict(x=ahead), dict(x=back), dict(c=1 - core)]


def entry_kernel(requests, scale, length_ref, tok_ref, gain_ref, qgain_ref, kgain_ref, wq_ref,
                 wkv_ref, prefix_ref, q_out, own_out, pieces, stream, normed, send, recv,
                 psend, precv, local_sem):
    core = lax.axis_index("c")
    rows = tok_ref.shape[0]
    size = qgain_ref.shape[1]
    half = prefix_ref.shape[1] // 2
    y, y_ahead, y_back, y_far = ring_of("y", core)
    z, z_ahead, z_back, z_far = ring_of("z", core)
    greet(x_peers() + [dict(y=y_ahead), dict(y=y_back), dict(z=z_ahead), dict(z=z_back)])

    sent = []

    def view(part, pz, py):
        return pieces.at[pz * RING + py, pl.ds(part * half, half)]

    def push(part, pz, py, src=None, **device):
        slot = pz * RING + py
        copy = remote(view(part, pz, py) if src is None else src, view(part, pz, py),
                      psend.at[len(sent)], precv.at[part, slot], **device)
        copy.start()
        sent.append(copy)

    def wait(part, pz, py):
        arrived(view(part, pz, py), precv.at[part, pz * RING + py])

    first = [prefix_ref.at[0, pl.ds(part * half, half)] for part in range(2)]
    gather = Gather(stream, send, recv)
    gather.open(tok_ref)
    push(0, z, y, first[0], y=y_ahead)
    push(0, z, y, first[0], y=y_back)
    push(1, z, y, first[1], z=z_ahead)
    push(1, z, y, first[1], z=z_back)
    push(0, z, y, first[0], z=z_ahead)
    push(0, z, y, first[0], z=z_back)
    push(1, z, y, first[1], y=y_ahead)
    push(1, z, y, first[1], y=y_back)
    keep = [pltpu.make_async_copy(prefix_ref.at[0], pieces.at[z * RING + y], local_sem.at[0]),
            pltpu.make_async_copy(tok_ref, stream.at[2 * gather.x + core], local_sem.at[1])]
    for copy in keep:
        copy.start()

    wait(0, z, y_back)
    push(0, z, y_back, y=y_ahead)
    push(0, z, y_back, z=z_ahead)
    push(0, z, y_back, z=z_back)
    wait(1, z_back, y)
    push(1, z_back, y, z=z_ahead)
    push(1, z_back, y, y=y_ahead)
    push(1, z_back, y, y=y_back)
    wait(0, z, y_ahead)
    push(0, z, y_ahead, z=z_ahead)
    push(0, z, y_ahead, z=z_back)
    wait(1, z_ahead, y)
    push(1, z_ahead, y, y=y_ahead)
    push(1, z_ahead, y, y=y_back)
    gather.relay()
    wait(0, z, y_far)
    push(0, z, y_far, z=z_ahead)
    push(0, z, y_far, z=z_back)
    wait(1, z_far, y)
    push(1, z_far, y, y=y_ahead)
    push(1, z_far, y, y=y_back)

    row = lax.broadcasted_iota(jnp.int32, (rows, 1), 0)
    offset = row
    end = 0
    for r in range(requests):
        end = end + length_ref[0, r]
        offset = offset - jnp.where(row >= end, length_ref[0, r], 0)
    lane = lax.broadcasted_iota(jnp.int32, (1, size), 1)
    freq = jnp.exp((lane & (size // 2 - 1)).astype(F32) * (-2.0 * LOG_THETA / size))
    angle = (PLEN + offset).astype(F32) * freq
    cosine, sine = jnp.cos(angle), jnp.sin(angle)

    def turned(value, gain):
        value = value * lax.rsqrt(jnp.mean(value * value, axis=1, keepdims=True) + EPS) * gain
        other = jnp.concatenate([-value[:, size // 2:], value[:, : size // 2]], axis=1)
        return (value * cosine + other * sine).astype(BF16)

    keep[1].wait()
    gather.close()
    normalise(stream, gain_ref, normed)

    far_z = [(py, z_back, z_ahead) for py in (y, y_far)] + [(py, z_ahead, z_back) for py in (y_back, y_ahead)]
    far_y = [(pz, y_back, y_ahead) for pz in (z, z_far)] + [(pz, y_ahead, y_back) for pz in (z_back, z_ahead)]
    order = (0, 2, 3, 1)
    for i in order:
        py, come, go = far_z[i]
        wait(0, come, py)
        push(0, come, py, z=go)
        pz, come, go = far_y[i]
        wait(1, pz, come)
        push(1, pz, come, y=go)

    query = dot(normed[...], wq_ref[...])
    keyval = dot(normed[...], wkv_ref[...])
    heads = query.shape[1] // size
    zero = jnp.zeros((rows, size), BF16)
    for h in range(heads):
        value = turned(query[:, h * size:(h + 1) * size], qgain_ref[...])
        value = jnp.concatenate([value * jnp.asarray(scale, BF16), zero], axis=1)
        for i in range(rows // BLOCK):
            q_out[i, h * BLOCK:(h + 1) * BLOCK, :] = value[i * BLOCK:(i + 1) * BLOCK]
    own_out[...] = jnp.concatenate(
        [turned(keyval[:, :size], kgain_ref[...]), keyval[:, size:].astype(BF16)], axis=1
    )

    for py, come, go in far_z:
        wait(0, go, py)
    for pz, come, go in far_y:
        wait(1, pz, go)
    for py, come, go in far_z:
        wait(0, z_far, py)
    for pz, come, go in far_y:
        wait(1, pz, y_far)
    keep[0].wait()
    gather.finish()
    for copy in sent:
        copy.wait_send()


def vmem():
    return pl.BlockSpec(memory_space=pltpu.VMEM)


def hbm():
    return pl.BlockSpec(memory_space=pl.ANY)


def smem():
    return pl.BlockSpec(memory_space=pltpu.SMEM)


def entry(lengths, tokens, attn_gain, q_gain, k_gain, w_query, w_keyval, prefix_kv):
    rows, width = tokens.shape
    size = q_gain.shape[1]
    heads = w_query.shape[1] // size
    count = RING * RING
    return pl.pallas_call(
        functools.partial(entry_kernel, lengths.shape[1], size ** (-0.5)),
        in_specs=[smem()] + [vmem()] * 7,
        out_specs=[vmem(), vmem(), hbm()],
        out_shape=[jax.ShapeDtypeStruct((rows // BLOCK, heads * BLOCK, 2 * size), BF16),
                   jax.ShapeDtypeStruct((rows, 2 * size), BF16),
                   jax.ShapeDtypeStruct((count,) + prefix_kv.shape[1:], BF16)],
        scratch_shapes=[pltpu.VMEM((8, rows, width), BF16), pltpu.VMEM((rows, 8 * width), BF16),
                        pltpu.SemaphoreType.DMA((7,)), pltpu.SemaphoreType.DMA((8,)),
                        pltpu.SemaphoreType.DMA((30,)), pltpu.SemaphoreType.DMA((2, count)),
                        pltpu.SemaphoreType.DMA((2,))],
        compiler_params=pltpu.CompilerParams(collective_id=1, has_side_effects=True),
        cost_estimate=pl.CostEstimate(flops=30 << 30, bytes_accessed=8 << 20, transcendentals=0),
        name="entry",
    )(lengths, tokens, attn_gain, q_gain, k_gain, w_query, w_keyval, prefix_kv)


def attention_kernel(requests, split, length_ref, tenant_ref, piece_ref,
                     q_ref, own_ref, kv_ref, out_ref, best_ref, total_ref, accum_ref, slot_ref):
    block = pl.program_id(0)
    queries = q_ref[0]
    count = queries.shape[0]
    rows = own_ref.shape[0]
    size = own_ref.shape[1] // 2
    for j in range(kv_ref.shape[0]):
        slot_ref[piece_ref[j]] = j
    row = (lax.broadcasted_iota(jnp.int32, (count, 1), 0) & (BLOCK - 1)) + block * BLOCK
    col = lax.broadcasted_iota(jnp.int32, (1, rows), 1)
    row_request = jnp.zeros((count, 1), jnp.int32)
    col_request = jnp.zeros((1, rows), jnp.int32)
    ends = []
    for r in range(requests):
        ends.append(length_ref[0, r] + (ends[-1] if ends else 0))
        row_request += (row >= ends[r]).astype(jnp.int32)
        col_request += (col >= ends[r]).astype(jnp.int32)
    seen = (row_request == col_request) & (col <= row)
    own = own_ref[...]
    scores = jnp.where(seen, dot_nt(queries, own), NEG)
    best = jnp.max(scores, axis=1, keepdims=True)
    weights = jnp.where(seen, jnp.exp(scores - best), 0.0)
    best_ref[...] = best
    total_ref[...] = jnp.sum(weights, axis=1, keepdims=True)
    accum_ref[...] = dot(weights.astype(BF16), own)
    for r in range(requests):
        begin = ends[r] - length_ref[0, r]

        @pl.when((ends[r] > block * BLOCK) & (begin < block * BLOCK + BLOCK))
        def _():
            inside = row_request == r
            tenant = tenant_ref[0, r]

            def piece(index, carry):
                keyval = kv_ref[slot_ref[tenant * split + index]]
                part = dot_nt(queries, keyval)
                old = best_ref[...]
                new = jnp.where(inside, jnp.maximum(old, jnp.max(part, axis=1, keepdims=True)), old)
                keep = jnp.exp(old - new)
                piece_weights = jnp.exp(part - jnp.where(inside, new, -NEG))
                best_ref[...] = new
                total_ref[...] = total_ref[...] * keep + jnp.sum(piece_weights, axis=1, keepdims=True)
                accum_ref[...] = accum_ref[...] * keep + dot(piece_weights.astype(BF16), keyval)
                return carry

            lax.fori_loop(0, split, piece, 0)

    out = accum_ref[...] / total_ref[...]
    heads = [out[h * BLOCK:(h + 1) * BLOCK, size:] for h in range(count // BLOCK)]
    out_ref[...] = jnp.concatenate(heads, axis=1).astype(BF16)


def attention(lengths, tenants, prefix_piece, queries, own, pieces):
    blocks, count, width = queries.shape
    rows = own.shape[0]
    columns = count // BLOCK * width // 2
    return pl.pallas_call(
        functools.partial(attention_kernel, lengths.shape[1], pieces.shape[0] // TENANTS),
        grid=(blocks,),
        in_specs=[smem(), smem(), smem(),
                  pl.BlockSpec((1, count, width), lambda i: (i, 0, 0)),
                  pl.BlockSpec(own.shape, lambda i: (0, 0)),
                  pl.BlockSpec(pieces.shape, lambda i: (0, 0, 0), pipeline_mode=pl.Buffered(1))],
        out_specs=pl.BlockSpec((BLOCK, columns), lambda i: (i, 0)),
        out_shape=jax.ShapeDtypeStruct((rows, columns), BF16),
        scratch_shapes=[pltpu.VMEM((count, 1), F32), pltpu.VMEM((count, 1), F32),
                        pltpu.VMEM((count, width), F32), pltpu.SMEM((pieces.shape[0],), jnp.int32)],
        cost_estimate=pl.CostEstimate(flops=24 << 30, bytes_accessed=5 << 20, transcendentals=0),
        name="attention",
    )(lengths, tenants, prefix_piece, queries, own, pieces)


def layer_kernel(att_ref, tok_ref, gain_ref, wo_ref, wg_hbm, wu_hbm, wd_hbm, out_ref,
                 wg, wu, wd, stage, paired, inbox, stage2, paired2, inbox2, mid, normed, inner,
                 load, send, pair_sem, in_sem, send2, pair_sem2, in_sem2, gsend, grecv):
    width = tok_ref.shape[1]
    loads = [pltpu.make_async_copy(src, dst, load.at[i])
             for i, (src, dst) in enumerate(((wg_hbm, wg), (wu_hbm, wu), (wd_hbm, wd)))]
    for copy in loads:
        copy.start()
    greet(x_peers())

    def columns(index):
        return pl.ds(pl.multiple_of(index * width, width), width)

    att = att_ref[...]
    value = scatter_sum(lambda d: dot(att, wo_ref[:, columns(d)]),
                        stage, paired, inbox, send, pair_sem, in_sem)
    share = (tok_ref[...].astype(F32) + value).astype(BF16)
    gather = Gather(mid, gsend, grecv)
    mine = 2 * gather.x + gather.core
    mid[mine] = share
    gather.open()
    gather.relay()
    gather.close()
    normalise(mid, gain_ref, normed)
    loads[0].wait()
    loads[1].wait()
    for t in range(inner.shape[1] // width):
        tile = slice(t * width, (t + 1) * width)
        gate = dot(normed[...], wg[:, tile])
        upper = dot(normed[...], wu[:, tile])
        inner[:, tile] = (gate / (1.0 + jnp.exp(-gate)) * upper).astype(BF16)
    loads[2].wait()
    value = scatter_sum(lambda d: dot(inner[...], wd[:, columns(d)]),
                        stage2, paired2, inbox2, send2, pair_sem2, in_sem2)
    out_ref[...] = (mid[mine].astype(F32) + value).astype(BF16)
    gather.finish()


def layer(attended, tokens, mlp_gain, w_out, w_gate, w_up, w_down):
    rows, width = tokens.shape
    units = w_gate.shape[1]
    block = (rows, width)
    dma = pltpu.SemaphoreType.DMA

    def blocks(n):
        return pltpu.VMEM((n,) + block, BF16)

    return pl.pallas_call(
        layer_kernel,
        in_specs=[vmem()] * 4 + [hbm()] * 3,
        out_specs=vmem(),
        out_shape=jax.ShapeDtypeStruct(block, BF16),
        scratch_shapes=[pltpu.VMEM(w_gate.shape, BF16), pltpu.VMEM(w_up.shape, BF16),
                        pltpu.VMEM(w_down.shape, BF16),
                        blocks(7), blocks(4), blocks(3), blocks(7), blocks(4), blocks(3), blocks(8),
                        pltpu.VMEM((rows, 8 * width), BF16), pltpu.VMEM((rows, units), BF16),
                        dma((3,)), dma((7,)), dma((4,)), dma((3,)), dma((7,)), dma((4,)), dma((3,)),
                        dma((7,)), dma((8,))],
        compiler_params=pltpu.CompilerParams(collective_id=2, has_side_effects=True,
                                             vmem_limit_bytes=48 << 20),
        cost_estimate=pl.CostEstimate(flops=40 << 30, bytes_accessed=14 << 20, transcendentals=0),
        name="layer",
    )(attended, tokens, mlp_gain, w_out, w_gate, w_up, w_down)


def head_kernel(share_ref, gain_ref, target_ref, near_w, ahead_w, back_w, far_a, far_b, out_ref,
                weight, hidden, normed, logits, wanted, stat, stat_y, stat_m,
                load, gsend, grecv, ysend, yrecv, tsend, trecv, ssend, srecv, msend, mrecv):
    core = lax.axis_index("c")
    rows = share_ref.shape[0]
    vocab = weight.shape[1]
    depth = near_w.shape[0] // RING
    x, x_ahead, x_back, x_far = ring_of("x", core)
    y, y_ahead, y_back, y_far = ring_of("y", core)
    z = lax.axis_index("z")
    mine = 2 * x + core
    loads = []

    def fetch(src, row, from_z, shift):
        to = (from_z * RING + lax.rem(y + RING - shift, RING)) * depth
        copy = pltpu.make_async_copy(
            src.at[pl.ds(row, depth)], weight.at[pl.ds(pl.multiple_of(to, depth), depth)],
            load.at[len(loads)])
        copy.start()
        loads.append(copy)

    up, down, over = lax.rem(z + 1, RING), lax.rem(z + 3, RING), lax.rem(z + 2, RING)
    for s in range(RING):
        fetch(near_w, s * depth, z, s)
        fetch(ahead_w, s * depth, up, s)
        fetch(back_w, s * depth, down, s)
        fetch(far_a if s < 2 else far_b, (s % 2) * depth, over, s)

    others = [dict(x=lax.rem(x + i // 2, RING), c=lax.rem(core + i % 2, 2)) for i in range(1, 8)]
    greet([dict(y=y_ahead), dict(y=y_back), dict(y=y_far)] + others)
    sent = []

    def push(src, dst, sems, recv, **device):
        copy = remote(src, dst, sems, recv, **device)
        copy.start()
        sent.append(copy)

    gathers = {}

    def gather_of(index, group):
        gathers[index] = Gather(hidden.at[group], gsend.at[index], grecv.at[group])
        return gathers[index]

    first = gather_of(0, y)
    push(share_ref, hidden.at[y, mine], ysend.at[0], yrecv.at[0], y=y_ahead)
    push(share_ref, hidden.at[y, mine], ysend.at[1], yrecv.at[1], y=y_back)
    first.open(share_ref)
    for i, to in enumerate((y_ahead, y_back, y_far)):
        push(target_ref, wanted.at[y], tsend.at[i], trecv.at[i], y=to)
    hidden[y, mine] = share_ref[...]
    wanted[y] = target_ref[...]

    arrived(hidden.at[y_back, mine], yrecv.at[0])
    push(hidden.at[y_back, mine], hidden.at[y_back, mine], ysend.at[2], yrecv.at[2], y=y_ahead)
    arrived(hidden.at[y_ahead, mine], yrecv.at[1])
    y_down, y_up = lax.rem(y + 3, RING), lax.rem(y + 1, RING)
    gather_of(1, y_down).open()
    gather_of(2, y_up).open()
    first.relay()
    arrived(hidden.at[y_far, mine], yrecv.at[2])
    gather_of(3, y_far).open()
    first.close()
    for i, group in enumerate((y_back, y_ahead, y_far)):
        arrived(wanted.at[group], trecv.at[i])
    for copy in loads:
        copy.wait()

    tile = 512
    eye = (lax.broadcasted_iota(jnp.int32, (rows, rows), 0)
           == lax.broadcasted_iota(jnp.int32, (rows, rows), 1))
    start = (mine * RING + y) * vocab
    column = lax.broadcasted_iota(jnp.int32, (1, vocab), 1)

    def to_row(value):
        return jnp.sum(jnp.where(eye, value, 0.0), axis=0, keepdims=True)

    for index, group in enumerate((y, y_down, y_up, y_far)):
        if index:
            gathers[index].close()
        normalise(hidden.at[group], gain_ref, normed)
        if index < 3:
            gathers[index + 1].relay()
        for t in range(vocab // tile):
            logits[:, t * tile:(t + 1) * tile] = dot(normed[...], weight[:, t * tile:(t + 1) * tile])
        value = logits[...]
        top = jnp.max(value, axis=1, keepdims=True)
        total = jnp.sum(jnp.exp(value - top), axis=1, keepdims=True)
        target = jnp.sum(jnp.where(eye, wanted[group], 0), axis=1, keepdims=True)
        picked = jnp.sum(jnp.where(target - start == column, value, 0.0), axis=1, keepdims=True)
        stat[group, 0:1, :] = to_row(top)
        stat[group, 1:2, :] = to_row(total)
        stat[group, 2:3, :] = to_row(picked)
        if index:
            push(stat.at[group], stat_y.at[y], ssend.at[index - 1], srecv.at[y], y=group)

    stat_y[y] = stat[y]
    for group in (y_back, y_ahead, y_far):
        arrived(stat_y.at[group], srecv.at[group])

    def merge(parts, count):
        top = parts[0, 0:1, :]
        for i in range(1, count):
            top = jnp.maximum(top, parts[i, 0:1, :])
        total = jnp.zeros_like(top)
        picked = jnp.zeros_like(top)
        for i in range(count):
            total += parts[i, 1:2, :] * jnp.exp(parts[i, 0:1, :] - top)
            picked += parts[i, 2:3, :]
        return (top, total, picked)

    for i, value in enumerate(merge(stat_y, RING)):
        stat_m[mine, i:i + 1, :] = value
    for i, peer in enumerate(others):
        push(stat_m.at[mine], stat_m.at[mine], msend.at[i], mrecv.at[mine], **peer)
    for peer in others:
        slot = 2 * peer["x"] + peer["c"]
        arrived(stat_m.at[slot], mrecv.at[slot])
    top, total, picked = merge(stat_m, 8)
    out_ref[...] = picked - top - jnp.log(total)
    for gather in gathers.values():
        gather.finish()
    for copy in sent:
        copy.wait_send()


def head(share, final_gain, targets, slabs):
    rows, width = share.shape
    vocab = slabs[0].shape[1]
    dma = pltpu.SemaphoreType.DMA
    stats = (8, rows)
    return pl.pallas_call(
        head_kernel,
        in_specs=[vmem()] * 3 + [hbm()] * 5,
        out_specs=vmem(),
        out_shape=jax.ShapeDtypeStruct((1, rows), F32),
        scratch_shapes=[pltpu.VMEM((8 * width, vocab), BF16), pltpu.VMEM((RING, 8, rows, width), BF16),
                        pltpu.VMEM((rows, 8 * width), BF16), pltpu.VMEM((rows, vocab), F32),
                        pltpu.VMEM((RING, 1, rows), jnp.int32), pltpu.VMEM((RING,) + stats, F32),
                        pltpu.VMEM((RING,) + stats, F32), pltpu.VMEM((8,) + stats, F32),
                        dma((16,)), dma((4, 7)), dma((4, 8)), dma((3,)), dma((3,)), dma((3,)), dma((3,)),
                        dma((3,)), dma((4,)), dma((7,)), dma((8,))],
        compiler_params=pltpu.CompilerParams(collective_id=3, has_side_effects=True,
                                             vmem_limit_bytes=48 << 20),
        cost_estimate=pl.CostEstimate(flops=30 << 30, bytes_accessed=9 << 20, transcendentals=0),
        name="head",
    )(share, final_gain, targets, *slabs)


def spread_head(w_head):
    y = lax.axis_index("y")
    part = w_head.shape[1] // RING
    got = []
    for shift in range(RING):
        give = lax.dynamic_slice_in_dim(w_head, lax.rem(y + shift, RING) * part, part, 1)
        if shift:
            give = lax.ppermute(give, "y", [(i, (i + shift) % RING) for i in range(RING)])
        got.append(give)
    slab = jnp.concatenate(got, axis=0)
    up = [(i, (i + 1) % RING) for i in range(RING)]
    down = [(i, (i + 3) % RING) for i in range(RING)]
    back = lax.ppermute(slab, "z", up)
    ahead = lax.ppermute(slab, "z", down)
    middle = slab.shape[0] // 2
    far_a = lax.ppermute(back[:middle], "z", up)
    far_b = lax.ppermute(ahead[middle:], "z", down)
    return (slab, ahead, back, far_a, far_b)


def body(tokens, attn_gain, mlp_gain, final_gain, q_gain, k_gain, w_query, w_keyval, w_out, w_gate,
         w_up, w_down, w_head, targets, req_lengths, req_tenant, prefix_piece, prefix_kv):
    slabs = spread_head(w_head)
    queries, own, pieces = entry(req_lengths, tokens, attn_gain[None], q_gain[None], k_gain[None],
                                 w_query, w_keyval, prefix_kv)
    attended = attention(req_lengths, req_tenant, prefix_piece, queries, own, pieces)
    share = layer(attended, tokens, mlp_gain[None], w_out, w_gate, w_up, w_down)
    logprob = head(share, final_gain[None], targets[None], slabs)
    return (share, logprob[0])


def solution(mesh):
    req = ("z", "y")
    mlp = ("x", "c")
    in_specs = (
        P(req, mlp), P(), P(), P(), P(), P(), P(None, mlp), P(None, mlp), P(mlp, None),
        P(None, mlp), P(None, mlp), P(mlp, None), P(req, mlp), P(req), P(req, None), P(req, None),
        P(), P(req, None, mlp),
    )
    out_specs = (P(req, mlp), P(req))
    split = Mesh(mesh.devices.reshape(RING, RING, RING, 2), ("z", "y", "x", "c"))
    return jax.shard_map(body, mesh=split, in_specs=in_specs, out_specs=out_specs, check_vma=False)
```

```python
import functools
import math

import jax
import jax.numpy as jnp
from jax import lax
from jax.experimental import pallas as pl
from jax.experimental.pallas import tpu as pltpu
from jax.sharding import Mesh
from jax.sharding import PartitionSpec as P

TENANTS = 4
PLEN = 4096
BLOCK = 64
EPS = 1e-05
LOG_THETA = math.log(1000000.0)
NEG = -1e30
RING = 4
MESH = pl.DeviceIdType.MESH
F32 = jnp.float32
BF16 = jnp.bfloat16


def dot(a, b):
    return jnp.dot(a, b, preferred_element_type=F32)


def dot_nt(a, b):
    return lax.dot_general(a, b, (((1,), (1,)), ((), ())), preferred_element_type=F32)


def remote(src, dst, send_sem, recv_sem, **device):
    return pltpu.make_async_remote_copy(
        src_ref=src, dst_ref=dst, send_sem=send_sem, recv_sem=recv_sem,
        device_id=device, device_id_type=MESH,
    )


def arrived(ref, sem):
    pltpu.make_async_copy(ref, ref, sem).wait()


def greet(peers):
    barrier = pltpu.get_barrier_semaphore()
    for peer in peers:
        pl.semaphore_signal(barrier, inc=1, device_id=peer, device_id_type=MESH)
    pl.semaphore_wait(barrier, len(peers))


def ring_of(axis, core):
    me = lax.axis_index(axis)
    ahead = lax.rem(me + 1 + 2 * core, RING)
    back = lax.rem(me + 3 + 2 * core, RING)
    far = lax.rem(me + 2, RING)
    return (me, ahead, back, far)


class Gather:
    def __init__(self, slots, send, recv):
        self.slots, self.send, self.recv, self.sent = slots, send, recv, []
        self.core = lax.axis_index("c")
        self.x, self.ahead, self.back, self.far = ring_of("x", self.core)

    def push(self, at, core, src=None, **device):
        slot = 2 * at + core
        copy = remote(self.slots.at[slot] if src is None else src, self.slots.at[slot],
                      self.send.at[len(self.sent)], self.recv.at[slot], **device)
        copy.start()
        self.sent.append(copy)

    def wait(self, at, core):
        slot = 2 * at + core
        arrived(self.slots.at[slot], self.recv.at[slot])

    def open(self, src=None):
        self.push(self.x, self.core, src, x=self.ahead)
        self.push(self.x, self.core, src, x=self.back)
        self.push(self.x, self.core, src, c=1 - self.core)

    def relay(self):
        self.wait(self.back, self.core)
        self.push(self.back, self.core, x=self.ahead)
        self.push(self.back, self.core, c=1 - self.core)
        self.wait(self.ahead, self.core)
        self.push(self.ahead, self.core, c=1 - self.core)

    def close(self):
        self.wait(self.far, self.core)
        self.push(self.far, self.core, c=1 - self.core)
        for x in (self.x, self.back, self.ahead, self.far):
            self.wait(x, 1 - self.core)

    def finish(self):
        for copy in self.sent:
            copy.wait_send()


def scatter_sum(partial, stage, paired, inbox, send, pair_sem, in_sem):
    core = lax.axis_index("c")
    x, ahead, back, far = ring_of("x", core)
    sent = []

    def push(value, dst, recv, **device):
        index = len(sent)
        stage[index] = value.astype(BF16)
        copy = remote(stage.at[index], dst, send.at[index], recv, **device)
        copy.start()
        sent.append(copy)

    def chip(to):
        mine = partial(2 * to + core)
        arrived(paired.at[to], pair_sem.at[to])
        return mine + paired[to].astype(F32)

    for to in (far, back, ahead, x):
        push(partial(2 * to + 1 - core), paired.at[to], pair_sem.at[to], c=1 - core)
    push(chip(far), inbox.at[2], in_sem.at[2], x=ahead)
    push(chip(back), inbox.at[1], in_sem.at[1], x=back)
    value = chip(ahead)
    arrived(inbox.at[2], in_sem.at[2])
    push(value + inbox[2].astype(F32), inbox.at[0], in_sem.at[0], x=ahead)
    value = chip(x)
    for slot in (1, 0):
        arrived(inbox.at[slot], in_sem.at[slot])
        value += inbox[slot].astype(F32)
    for copy in sent:
        copy.wait_send()
    return value


def normalise(blocks, gain_ref, normed):
    count, rows, width = blocks.shape
    square = jnp.zeros((rows, 1), F32)
    for m in range(count):
        value = blocks[m].astype(F32)
        square += jnp.sum(value * value, axis=1, keepdims=True)
    factor = lax.rsqrt(square / (count * width) + EPS)
    for m in range(count):
        columns = slice(m * width, (m + 1) * width)
        normed[:, columns] = (blocks[m].astype(F32) * factor * gain_ref[:, columns]).astype(BF16)


def x_peers():
    core = lax.axis_index("c")
    _, ahead, back, _ = ring_of("x", core)
    return [dict(x=ahead), dict(x=back), dict(c=1 - core)]


def entry_kernel(requests, scale, length_ref, tok_ref, gain_ref, qgain_ref, kgain_ref, wq_ref,
                 wkv_ref, prefix_ref, head_ref, q_out, own_out, pieces, head_out, passing, stream,
                 normed, send, recv, psend, precv, wsend, wrecv, local_sem):
    core = lax.axis_index("c")
    rows = tok_ref.shape[0]
    size = qgain_ref.shape[1]
    half = prefix_ref.shape[1] // 2
    y, y_ahead, y_back, y_far = ring_of("y", core)
    z, z_ahead, z_back, z_far = ring_of("z", core)
    greet(x_peers() + [dict(y=y_ahead), dict(y=y_back), dict(z=z_ahead), dict(z=z_back)])

    sent = []

    def view(part, pz, py):
        return pieces.at[pz * RING + py, pl.ds(part * half, half)]

    def push(part, pz, py, src=None, **device):
        slot = pz * RING + py
        copy = remote(view(part, pz, py) if src is None else src, view(part, pz, py),
                      psend.at[len(sent)], precv.at[part, slot], **device)
        copy.start()
        sent.append(copy)

    def wait(part, pz, py):
        arrived(view(part, pz, py), precv.at[part, pz * RING + py])

    first = [prefix_ref.at[0, pl.ds(part * half, half)] for part in range(2)]
    gather = Gather(stream, send, recv)
    gather.open(tok_ref)
    push(0, z, y, first[0], y=y_ahead)
    push(0, z, y, first[0], y=y_back)
    push(1, z, y, first[1], z=z_ahead)
    push(1, z, y, first[1], z=z_back)
    push(0, z, y, first[0], z=z_ahead)
    push(0, z, y, first[0], z=z_back)
    push(1, z, y, first[1], y=y_ahead)
    push(1, z, y, first[1], y=y_back)

    given = []
    part_words = head_out.shape[2]

    def words(index):
        return head_ref.at[:, pl.ds(pl.multiple_of(index * part_words, part_words), part_words)]

    def piece(pz, py):
        return head_out.at[pz * RING + py]

    def give(index, src, dst, **device):
        copy = remote(src, dst, wsend.at[index], wrecv.at[index], **device)
        copy.start()
        given.append(copy)

    give(2, words(y_far), passing, y=y_ahead)
    give(4, words(y), piece(z, y), z=z_ahead)
    give(5, words(y), piece(z, y), z=z_back)
    give(0, words(y_ahead), piece(z, y), y=y_ahead)
    give(1, words(y_back), piece(z, y), y=y_back)
    keep = [pltpu.make_async_copy(prefix_ref.at[0], pieces.at[z * RING + y], local_sem.at[0]),
            pltpu.make_async_copy(tok_ref, stream.at[2 * gather.x + core], local_sem.at[1])]
    for copy in keep:
        copy.start()

    wait(0, z, y_back)
    push(0, z, y_back, y=y_ahead)
    push(0, z, y_back, z=z_ahead)
    push(0, z, y_back, z=z_back)
    wait(1, z_back, y)
    push(1, z_back, y, z=z_ahead)
    push(1, z_back, y, y=y_ahead)
    push(1, z_back, y, y=y_back)
    wait(0, z, y_ahead)
    push(0, z, y_ahead, z=z_ahead)
    push(0, z, y_ahead, z=z_back)
    wait(1, z_ahead, y)
    push(1, z_ahead, y, y=y_ahead)
    push(1, z_ahead, y, y=y_back)
    gather.relay()
    wait(0, z, y_far)
    push(0, z, y_far, z=z_ahead)
    push(0, z, y_far, z=z_back)
    wait(1, z_far, y)
    push(1, z_far, y, y=y_ahead)
    push(1, z_far, y, y=y_back)

    row = lax.broadcasted_iota(jnp.int32, (rows, 1), 0)
    offset = row
    end = 0
    for r in range(requests):
        end = end + length_ref[0, r]
        offset = offset - jnp.where(row >= end, length_ref[0, r], 0)
    lane = lax.broadcasted_iota(jnp.int32, (1, size), 1)
    freq = jnp.exp((lane & (size // 2 - 1)).astype(F32) * (-2.0 * LOG_THETA / size))
    angle = (PLEN + offset).astype(F32) * freq
    cosine, sine = jnp.cos(angle), jnp.sin(angle)

    def turned(value, gain):
        value = value * lax.rsqrt(jnp.mean(value * value, axis=1, keepdims=True) + EPS) * gain
        other = jnp.concatenate([-value[:, size // 2:], value[:, : size // 2]], axis=1)
        return (value * cosine + other * sine).astype(BF16)

    keep[1].wait()
    gather.close()
    normalise(stream, gain_ref, normed)

    far_z = [(py, z_back, z_ahead) for py in (y, y_far)] + [(py, z_ahead, z_back) for py in (y_back, y_ahead)]
    far_y = [(pz, y_back, y_ahead) for pz in (z, z_far)] + [(pz, y_ahead, y_back) for pz in (z_back, z_ahead)]
    order = (0, 2, 3, 1)
    for i in order:
        py, come, go = far_z[i]
        wait(0, come, py)
        push(0, come, py, z=go)
        pz, come, go = far_y[i]
        wait(1, pz, come)
        push(1, pz, come, y=go)

    arrived(passing, wrecv.at[2])
    give(3, passing, piece(z, y_back), y=y_ahead)
    arrived(piece(z_back, y), wrecv.at[4])
    give(6, piece(z_back, y), piece(z_back, y), z=z_ahead)

    query = dot(normed[...], wq_ref[...])
    keyval = dot(normed[...], wkv_ref[...])
    heads = query.shape[1] // size
    zero = jnp.zeros((rows, size), BF16)
    for h in range(heads):
        value = turned(query[:, h * size:(h + 1) * size], qgain_ref[...])
        value = jnp.concatenate([value * jnp.asarray(scale, BF16), zero], axis=1)
        for i in range(rows // BLOCK):
            q_out[i, h * BLOCK:(h + 1) * BLOCK, :] = value[i * BLOCK:(i + 1) * BLOCK]
    own_out[...] = jnp.concatenate(
        [turned(keyval[:, :size], kgain_ref[...]), keyval[:, size:].astype(BF16)], axis=1
    )

    for py, come, go in far_z:
        wait(0, go, py)
    for pz, come, go in far_y:
        wait(1, pz, go)
    for py, come, go in far_z:
        wait(0, z_far, py)
    for pz, come, go in far_y:
        wait(1, pz, y_far)
    arrived(piece(z, y_back), wrecv.at[0])
    arrived(piece(z, y_ahead), wrecv.at[1])
    arrived(piece(z, y_far), wrecv.at[3])
    arrived(piece(z_ahead, y), wrecv.at[5])
    arrived(piece(z_far, y), wrecv.at[6])
    keep[0].wait()
    gather.finish()
    for copy in sent + given:
        copy.wait_send()


def vmem():
    return pl.BlockSpec(memory_space=pltpu.VMEM)


def hbm():
    return pl.BlockSpec(memory_space=pl.ANY)


def smem():
    return pl.BlockSpec(memory_space=pltpu.SMEM)


def entry(lengths, tokens, attn_gain, q_gain, k_gain, w_query, w_keyval, prefix_kv, w_head):
    rows, width = tokens.shape
    size = q_gain.shape[1]
    heads = w_query.shape[1] // size
    count = RING * RING
    quarter = (w_head.shape[0], w_head.shape[1] // RING)
    return pl.pallas_call(
        functools.partial(entry_kernel, lengths.shape[1], size ** (-0.5)),
        in_specs=[smem()] + [vmem()] * 7 + [hbm()],
        out_specs=[vmem(), vmem(), hbm(), hbm(), hbm()],
        out_shape=[jax.ShapeDtypeStruct((rows // BLOCK, heads * BLOCK, 2 * size), BF16),
                   jax.ShapeDtypeStruct((rows, 2 * size), BF16),
                   jax.ShapeDtypeStruct((count,) + prefix_kv.shape[1:], BF16),
                   jax.ShapeDtypeStruct((count,) + quarter, BF16),
                   jax.ShapeDtypeStruct(quarter, BF16)],
        scratch_shapes=[pltpu.VMEM((8, rows, width), BF16), pltpu.VMEM((rows, 8 * width), BF16),
                        pltpu.SemaphoreType.DMA((7,)), pltpu.SemaphoreType.DMA((8,)),
                        pltpu.SemaphoreType.DMA((30,)), pltpu.SemaphoreType.DMA((2, count)),
                        pltpu.SemaphoreType.DMA((7,)), pltpu.SemaphoreType.DMA((7,)),
                        pltpu.SemaphoreType.DMA((2,))],
        compiler_params=pltpu.CompilerParams(collective_id=1, has_side_effects=True),
        cost_estimate=pl.CostEstimate(flops=30 << 30, bytes_accessed=8 << 20, transcendentals=0),
        name="entry",
    )(lengths, tokens, attn_gain, q_gain, k_gain, w_query, w_keyval, prefix_kv, w_head)


def attention_kernel(requests, split, length_ref, tenant_ref, piece_ref,
                     q_ref, own_ref, kv_ref, out_ref, best_ref, total_ref, accum_ref, slot_ref):
    block = pl.program_id(0)
    queries = q_ref[0]
    count = queries.shape[0]
    rows = own_ref.shape[0]
    size = own_ref.shape[1] // 2
    for j in range(kv_ref.shape[0]):
        slot_ref[piece_ref[j]] = j
    row = (lax.broadcasted_iota(jnp.int32, (count, 1), 0) & (BLOCK - 1)) + block * BLOCK
    col = lax.broadcasted_iota(jnp.int32, (1, rows), 1)
    row_request = jnp.zeros((count, 1), jnp.int32)
    col_request = jnp.zeros((1, rows), jnp.int32)
    ends = []
    for r in range(requests):
        ends.append(length_ref[0, r] + (ends[-1] if ends else 0))
        row_request += (row >= ends[r]).astype(jnp.int32)
        col_request += (col >= ends[r]).astype(jnp.int32)
    seen = (row_request == col_request) & (col <= row)
    own = own_ref[...]
    scores = jnp.where(seen, dot_nt(queries, own), NEG)
    best = jnp.max(scores, axis=1, keepdims=True)
    weights = jnp.where(seen, jnp.exp(scores - best), 0.0)
    best_ref[...] = best
    total_ref[...] = jnp.sum(weights, axis=1, keepdims=True)
    accum_ref[...] = dot(weights.astype(BF16), own)
    for r in range(requests):
        begin = ends[r] - length_ref[0, r]

        @pl.when((ends[r] > block * BLOCK) & (begin < block * BLOCK + BLOCK))
        def _():
            inside = row_request == r
            tenant = tenant_ref[0, r]

            def piece(index, carry):
                keyval = kv_ref[slot_ref[tenant * split + index]]
                part = dot_nt(queries, keyval)
                old = best_ref[...]
                new = jnp.where(inside, jnp.maximum(old, jnp.max(part, axis=1, keepdims=True)), old)
                keep = jnp.exp(old - new)
                piece_weights = jnp.exp(part - jnp.where(inside, new, -NEG))
                best_ref[...] = new
                total_ref[...] = total_ref[...] * keep + jnp.sum(piece_weights, axis=1, keepdims=True)
                accum_ref[...] = accum_ref[...] * keep + dot(piece_weights.astype(BF16), keyval)
                return carry

            lax.fori_loop(0, split, piece, 0)

    out = accum_ref[...] / total_ref[...]
    heads = [out[h * BLOCK:(h + 1) * BLOCK, size:] for h in range(count // BLOCK)]
    out_ref[...] = jnp.concatenate(heads, axis=1).astype(BF16)


def attention(lengths, tenants, prefix_piece, queries, own, pieces):
    blocks, count, width = queries.shape
    rows = own.shape[0]
    columns = count // BLOCK * width // 2
    return pl.pallas_call(
        functools.partial(attention_kernel, lengths.shape[1], pieces.shape[0] // TENANTS),
        grid=(blocks,),
        in_specs=[smem(), smem(), smem(),
                  pl.BlockSpec((1, count, width), lambda i: (i, 0, 0)),
                  pl.BlockSpec(own.shape, lambda i: (0, 0)),
                  pl.BlockSpec(pieces.shape, lambda i: (0, 0, 0), pipeline_mode=pl.Buffered(1))],
        out_specs=pl.BlockSpec((BLOCK, columns), lambda i: (i, 0)),
        out_shape=jax.ShapeDtypeStruct((rows, columns), BF16),
        scratch_shapes=[pltpu.VMEM((count, 1), F32), pltpu.VMEM((count, 1), F32),
                        pltpu.VMEM((count, width), F32), pltpu.SMEM((pieces.shape[0],), jnp.int32)],
        cost_estimate=pl.CostEstimate(flops=24 << 30, bytes_accessed=5 << 20, transcendentals=0),
        name="attention",
    )(lengths, tenants, prefix_piece, queries, own, pieces)


def finish_kernel(att_ref, tok_ref, gain_ref, wo_ref, last_gain_ref, target_ref, wg_hbm, wu_hbm, wd_hbm,
                  head_hbm, pieces_hbm, out_ref, log_ref,
                  wg, wu, wd, stage, paired, inbox, stage2, paired2, inbox2, mid, normed, inner,
                  weight, hidden, logits, wanted, stat, stat_y, stat_m,
                  load, send, pair_sem, in_sem, send2, pair_sem2, in_sem2, msend, mrecv,
                  gsend, grecv, ysend, yrecv, tsend, trecv, ssend, srecv, ksend, krecv,
                  zsend, zrecv):
    core = lax.axis_index("c")
    rows, width = tok_ref.shape
    depth, vocab = pieces_hbm.shape[1:]
    x, x_ahead, x_back, x_far = ring_of("x", core)
    y, y_ahead, y_back, y_far = ring_of("y", core)
    z, z_ahead, z_back, z_far = ring_of("z", core)
    mine = 2 * x + core
    sent = []

    def push(src, dst, send_sem, recv_sem, **device):
        copy = remote(src, dst, send_sem, recv_sem, **device)
        copy.start()
        sent.append(copy)

    def columns(index, count):
        return pl.ds(pl.multiple_of(index * count, count), count)

    def place(pz, py):
        return weight.at[columns(pz * RING + py, depth)]

    loads = []

    def fetch(src, dst):
        copy = pltpu.make_async_copy(src, dst, load.at[len(loads)])
        copy.start()
        loads.append(copy)

    fetch(wg_hbm, wg)
    fetch(wu_hbm, wu)
    fetch(wd_hbm, wd)
    fetch(head_hbm.at[:, columns(y, vocab)], place(z, y))
    for pz in (z_ahead, z_back, z_far):
        fetch(pieces_hbm.at[pz * RING + y], place(pz, y))
    rest = (y_back, y_ahead, y_far)
    for py in rest:
        fetch(pieces_hbm.at[z * RING + py], place(z, py))
    others = [dict(x=lax.rem(x + i // 2, RING), c=lax.rem(core + i % 2, 2)) for i in range(1, 8)]
    greet([dict(y=y_ahead), dict(y=y_back), dict(y=y_far), dict(z=z_ahead), dict(z=z_back)] + others)

    for i, py in enumerate(rest):
        source = pieces_hbm.at[z * RING + py]
        push(source, place(z, py), zsend.at[i, 0], zrecv.at[i, 0], z=z_ahead)
        push(source, place(z, py), zsend.at[i, 1], zrecv.at[i, 1], z=z_back)
    for i, to in enumerate((y_ahead, y_back, y_far)):
        push(target_ref, wanted.at[y], tsend.at[i], trecv.at[i], y=to)
    wanted[y] = target_ref[...]

    def head_relay(i):
        arrived(place(z_back, rest[i]), zrecv.at[i, 0])
        push(place(z_back, rest[i]), place(z_back, rest[i]), zsend.at[i, 2], zrecv.at[i, 2], z=z_ahead)

    att = att_ref[...]
    value = scatter_sum(lambda d: dot(att, wo_ref[:, columns(d, width)]),
                        stage, paired, inbox, send, pair_sem, in_sem)
    middle = Gather(mid, msend, mrecv)
    mid[mine] = (tok_ref[...].astype(F32) + value).astype(BF16)
    middle.open()
    middle.relay()
    middle.close()
    normalise(mid, gain_ref, normed)
    loads[0].wait()
    loads[1].wait()
    for t in range(inner.shape[1] // width):
        tile = slice(t * width, (t + 1) * width)
        gate = dot(normed[...], wg[:, tile])
        upper = dot(normed[...], wu[:, tile])
        inner[:, tile] = (gate / (1.0 + jnp.exp(-gate)) * upper).astype(BF16)
    loads[2].wait()
    head_relay(0)
    value = scatter_sum(lambda d: dot(inner[...], wd[:, columns(d, width)]),
                        stage2, paired2, inbox2, send2, pair_sem2, in_sem2)
    share = (mid[mine].astype(F32) + value).astype(BF16)
    out_ref[...] = share
    hidden[y, mine] = share

    gathers = {}

    def gather_of(index, group):
        gathers[index] = Gather(hidden.at[group], gsend.at[index], grecv.at[group])
        return gathers[index]

    own = hidden.at[y, mine]
    first = gather_of(0, y)
    push(own, own, ysend.at[0], yrecv.at[0], y=y_ahead)
    push(own, own, ysend.at[1], yrecv.at[1], y=y_back)
    first.open()
    head_relay(1)

    arrived(hidden.at[y_back, mine], yrecv.at[0])
    push(hidden.at[y_back, mine], hidden.at[y_back, mine], ysend.at[2], yrecv.at[2], y=y_ahead)
    arrived(hidden.at[y_ahead, mine], yrecv.at[1])
    y_down, y_up = lax.rem(y + 3, RING), lax.rem(y + 1, RING)
    gather_of(1, y_down).open()
    gather_of(2, y_up).open()
    first.relay()
    arrived(hidden.at[y_far, mine], yrecv.at[2])
    gather_of(3, y_far).open()
    head_relay(2)
    first.close()
    for i, group in enumerate((y_back, y_ahead, y_far)):
        arrived(wanted.at[group], trecv.at[i])
    for copy in loads[3:]:
        copy.wait()
    for i, py in enumerate(rest):
        arrived(place(z_ahead, py), zrecv.at[i, 1])
        arrived(place(z_far, py), zrecv.at[i, 2])

    tile = 512
    eye = (lax.broadcasted_iota(jnp.int32, (rows, rows), 0)
           == lax.broadcasted_iota(jnp.int32, (rows, rows), 1))
    start = (mine * RING + y) * vocab
    column = lax.broadcasted_iota(jnp.int32, (1, vocab), 1)

    def to_row(value):
        return jnp.sum(jnp.where(eye, value, 0.0), axis=0, keepdims=True)

    for index, group in enumerate((y, y_down, y_up, y_far)):
        if index:
            gathers[index].close()
        normalise(hidden.at[group], last_gain_ref, normed)
        if index < 3:
            gathers[index + 1].relay()
        for t in range(vocab // tile):
            logits[:, t * tile:(t + 1) * tile] = dot(normed[...], weight[:, t * tile:(t + 1) * tile])
        value = logits[...]
        top = jnp.max(value, axis=1, keepdims=True)
        total = jnp.sum(jnp.exp(value - top), axis=1, keepdims=True)
        target = jnp.sum(jnp.where(eye, wanted[group], 0), axis=1, keepdims=True)
        picked = jnp.sum(jnp.where(target - start == column, value, 0.0), axis=1, keepdims=True)
        stat[group, 0:1, :] = to_row(top)
        stat[group, 1:2, :] = to_row(total)
        stat[group, 2:3, :] = to_row(picked)
        if index:
            push(stat.at[group], stat_y.at[y], ssend.at[index - 1], srecv.at[y], y=group)

    stat_y[y] = stat[y]
    for group in (y_back, y_ahead, y_far):
        arrived(stat_y.at[group], srecv.at[group])

    def merge(parts, count):
        top = parts[0, 0:1, :]
        for i in range(1, count):
            top = jnp.maximum(top, parts[i, 0:1, :])
        total = jnp.zeros_like(top)
        picked = jnp.zeros_like(top)
        for i in range(count):
            total += parts[i, 1:2, :] * jnp.exp(parts[i, 0:1, :] - top)
            picked += parts[i, 2:3, :]
        return (top, total, picked)

    for i, value in enumerate(merge(stat_y, RING)):
        stat_m[mine, i:i + 1, :] = value
    for i, peer in enumerate(others):
        push(stat_m.at[mine], stat_m.at[mine], ksend.at[i], krecv.at[mine], **peer)
    for peer in others:
        slot = 2 * peer["x"] + peer["c"]
        arrived(stat_m.at[slot], krecv.at[slot])
    top, total, picked = merge(stat_m, 8)
    log_ref[...] = picked - top - jnp.log(total)
    middle.finish()
    for gather in gathers.values():
        gather.finish()
    for copy in sent:
        copy.wait_send()


def finish(attended, tokens, mlp_gain, w_out, final_gain, targets, w_gate, w_up, w_down, w_head, pieces):
    rows, width = tokens.shape
    units = w_gate.shape[1]
    block = (rows, width)
    vocab = pieces.shape[2]
    dma = pltpu.SemaphoreType.DMA
    stats = (8, rows)

    def blocks(n):
        return pltpu.VMEM((n,) + block, BF16)

    return pl.pallas_call(
        finish_kernel,
        in_specs=[vmem()] * 6 + [hbm()] * 5,
        out_specs=[vmem(), vmem()],
        out_shape=[jax.ShapeDtypeStruct(block, BF16), jax.ShapeDtypeStruct((1, rows), F32)],
        scratch_shapes=[pltpu.VMEM(w_gate.shape, BF16), pltpu.VMEM(w_up.shape, BF16),
                        pltpu.VMEM(w_down.shape, BF16),
                        blocks(7), blocks(4), blocks(3), blocks(7), blocks(4), blocks(3), blocks(8),
                        pltpu.VMEM((rows, 8 * width), BF16), pltpu.VMEM((rows, units), BF16),
                        pltpu.VMEM((8 * width, vocab), BF16), pltpu.VMEM((RING, 8) + block, BF16),
                        pltpu.VMEM((rows, vocab), F32),
                        pltpu.VMEM((RING, 1, rows), jnp.int32), pltpu.VMEM((RING,) + stats, F32),
                        pltpu.VMEM((RING,) + stats, F32), pltpu.VMEM((8,) + stats, F32),
                        dma((10,)), dma((7,)), dma((4,)), dma((3,)), dma((7,)), dma((4,)), dma((3,)),
                        dma((7,)), dma((8,)),
                        dma((4, 7)), dma((4, 8)), dma((3,)), dma((3,)), dma((3,)), dma((3,)),
                        dma((3,)), dma((4,)), dma((7,)), dma((8,)), dma((3, 3)), dma((3, 3))],
        compiler_params=pltpu.CompilerParams(collective_id=2, has_side_effects=True,
                                             vmem_limit_bytes=56 << 20),
        cost_estimate=pl.CostEstimate(flops=60 << 30, bytes_accessed=24 << 20, transcendentals=0),
        name="finish",
    )(attended, tokens, mlp_gain, w_out, final_gain, targets, w_gate, w_up, w_down, w_head, pieces)


def body(tokens, attn_gain, mlp_gain, final_gain, q_gain, k_gain, w_query, w_keyval, w_out, w_gate,
         w_up, w_down, w_head, targets, req_lengths, req_tenant, prefix_piece, prefix_kv):
    queries, own, pieces, slabs, _ = entry(
        req_lengths, tokens, attn_gain[None], q_gain[None], k_gain[None], w_query, w_keyval,
        prefix_kv, w_head)
    attended = attention(req_lengths, req_tenant, prefix_piece, queries, own, pieces)
    share, logprob = finish(attended, tokens, mlp_gain[None], w_out, final_gain[None], targets[None],
                            w_gate, w_up, w_down, w_head, slabs)
    return (share, logprob[0])


def solution(mesh):
    req = ("z", "y")
    mlp = ("x", "c")
    in_specs = (
        P(req, mlp), P(), P(), P(), P(), P(), P(None, mlp), P(None, mlp), P(mlp, None),
        P(None, mlp), P(None, mlp), P(mlp, None), P(req, mlp), P(req), P(req, None), P(req, None),
        P(), P(req, None, mlp),
    )
    out_specs = (P(req, mlp), P(req))
    split = Mesh(mesh.devices.reshape(RING, RING, RING, 2), ("z", "y", "x", "c"))
    return jax.shard_map(body, mesh=split, in_specs=in_specs, out_specs=out_specs, check_vma=False)
```

```python
import functools
import math

import jax
import jax.numpy as jnp
from jax import lax
from jax.experimental import pallas as pl
from jax.experimental.pallas import tpu as pltpu
from jax.sharding import Mesh
from jax.sharding import PartitionSpec as P

TENANTS = 4
PLEN = 4096
BLOCK = 64
EPS = 1e-05
LOG_THETA = math.log(1000000.0)
NEG = -1e30
RING = 4
MESH = pl.DeviceIdType.MESH
F32 = jnp.float32
BF16 = jnp.bfloat16


def dot(a, b):
    return jnp.dot(a, b, preferred_element_type=F32)


def dot_nt(a, b):
    return lax.dot_general(a, b, (((1,), (1,)), ((), ())), preferred_element_type=F32)


def remote(src, dst, send_sem, recv_sem, **device):
    return pltpu.make_async_remote_copy(
        src_ref=src, dst_ref=dst, send_sem=send_sem, recv_sem=recv_sem,
        device_id=device, device_id_type=MESH,
    )


def arrived(ref, sem):
    pltpu.make_async_copy(ref, ref, sem).wait()


def greet(peers):
    barrier = pltpu.get_barrier_semaphore()
    for peer in peers:
        pl.semaphore_signal(barrier, inc=1, device_id=peer, device_id_type=MESH)
    pl.semaphore_wait(barrier, len(peers))


def ring_of(axis, core):
    me = lax.axis_index(axis)
    ahead = lax.rem(me + 1 + 2 * core, RING)
    back = lax.rem(me + 3 + 2 * core, RING)
    far = lax.rem(me + 2, RING)
    return (me, ahead, back, far)


class Gather:
    def __init__(self, slots, send, recv):
        self.slots, self.send, self.recv, self.sent = slots, send, recv, []
        self.core = lax.axis_index("c")
        self.x, self.ahead, self.back, self.far = ring_of("x", self.core)

    def push(self, at, core, src=None, **device):
        slot = 2 * at + core
        copy = remote(self.slots.at[slot] if src is None else src, self.slots.at[slot],
                      self.send.at[len(self.sent)], self.recv.at[slot], **device)
        copy.start()
        self.sent.append(copy)

    def wait(self, at, core):
        slot = 2 * at + core
        arrived(self.slots.at[slot], self.recv.at[slot])

    def open(self, src=None):
        self.push(self.x, self.core, src, x=self.ahead)
        self.push(self.x, self.core, src, x=self.back)
        self.push(self.x, self.core, src, c=1 - self.core)

    def relay(self):
        self.wait(self.back, self.core)
        self.push(self.back, self.core, x=self.ahead)
        self.push(self.back, self.core, c=1 - self.core)
        self.wait(self.ahead, self.core)
        self.push(self.ahead, self.core, c=1 - self.core)

    def close(self):
        self.wait(self.far, self.core)
        self.push(self.far, self.core, c=1 - self.core)
        for x in (self.x, self.back, self.ahead, self.far):
            self.wait(x, 1 - self.core)

    def finish(self):
        for copy in self.sent:
            copy.wait_send()


def scatter_sum(partial, stage, paired, inbox, send, pair_sem, in_sem):
    core = lax.axis_index("c")
    x, ahead, back, far = ring_of("x", core)
    sent = []

    def push(value, dst, recv, **device):
        index = len(sent)
        stage[index] = value.astype(BF16)
        copy = remote(stage.at[index], dst, send.at[index], recv, **device)
        copy.start()
        sent.append(copy)

    def chip(to):
        mine = partial(2 * to + core)
        arrived(paired.at[to], pair_sem.at[to])
        return mine + paired[to].astype(F32)

    for to in (far, back, ahead, x):
        push(partial(2 * to + 1 - core), paired.at[to], pair_sem.at[to], c=1 - core)
    push(chip(far), inbox.at[2], in_sem.at[2], x=ahead)
    push(chip(back), inbox.at[1], in_sem.at[1], x=back)
    value = chip(ahead)
    arrived(inbox.at[2], in_sem.at[2])
    push(value + inbox[2].astype(F32), inbox.at[0], in_sem.at[0], x=ahead)
    value = chip(x)
    for slot in (1, 0):
        arrived(inbox.at[slot], in_sem.at[slot])
        value += inbox[slot].astype(F32)
    for copy in sent:
        copy.wait_send()
    return value


def normalise(blocks, gain_ref, normed):
    count, rows, width = blocks.shape
    square = jnp.zeros((rows, 1), F32)
    for m in range(count):
        value = blocks[m].astype(F32)
        square += jnp.sum(value * value, axis=1, keepdims=True)
    factor = lax.rsqrt(square / (count * width) + EPS)
    for m in range(count):
        columns = slice(m * width, (m + 1) * width)
        normed[:, columns] = (blocks[m].astype(F32) * factor * gain_ref[:, columns]).astype(BF16)


def x_peers():
    core = lax.axis_index("c")
    _, ahead, back, _ = ring_of("x", core)
    return [dict(x=ahead), dict(x=back), dict(c=1 - core)]


def entry_kernel(requests, scale, length_ref, tok_ref, gain_ref, qgain_ref, kgain_ref, wq_ref,
                 wkv_ref, prefix_ref, head_ref, q_out, own_out, pieces, head_out, passing, stream,
                 normed, send, recv, psend, precv, wsend, wrecv, local_sem):
    core = lax.axis_index("c")
    rows = tok_ref.shape[0]
    size = qgain_ref.shape[1]
    half = prefix_ref.shape[1] // 2
    y, y_ahead, y_back, y_far = ring_of("y", core)
    z, z_ahead, z_back, z_far = ring_of("z", core)
    greet(x_peers() + [dict(y=y_ahead), dict(y=y_back), dict(z=z_ahead), dict(z=z_back)])

    sent = []

    def view(part, pz, py):
        return pieces.at[pz * RING + py, pl.ds(part * half, half)]

    def push(part, pz, py, src=None, **device):
        slot = pz * RING + py
        copy = remote(view(part, pz, py) if src is None else src, view(part, pz, py),
                      psend.at[len(sent)], precv.at[part, slot], **device)
        copy.start()
        sent.append(copy)

    def wait(part, pz, py):
        arrived(view(part, pz, py), precv.at[part, pz * RING + py])

    first = [prefix_ref.at[0, pl.ds(part * half, half)] for part in range(2)]
    gather = Gather(stream, send, recv)
    gather.open(tok_ref)
    push(0, z, y, first[0], y=y_ahead)
    push(0, z, y, first[0], y=y_back)
    push(1, z, y, first[1], z=z_ahead)
    push(1, z, y, first[1], z=z_back)
    push(0, z, y, first[0], z=z_ahead)
    push(0, z, y, first[0], z=z_back)
    push(1, z, y, first[1], y=y_ahead)
    push(1, z, y, first[1], y=y_back)

    given = []
    part_words = head_out.shape[2]

    def words(index):
        return head_ref.at[:, pl.ds(pl.multiple_of(index * part_words, part_words), part_words)]

    def piece(pz, py):
        return head_out.at[pz * RING + py]

    def give(index, src, dst, **device):
        copy = remote(src, dst, wsend.at[index], wrecv.at[index], **device)
        copy.start()
        given.append(copy)

    give(2, words(y_far), passing, y=y_ahead)
    give(4, words(y), piece(z, y), z=z_ahead)
    give(5, words(y), piece(z, y), z=z_back)
    give(0, words(y_ahead), piece(z, y), y=y_ahead)
    give(1, words(y_back), piece(z, y), y=y_back)
    keep = [pltpu.make_async_copy(prefix_ref.at[0], pieces.at[z * RING + y], local_sem.at[0]),
            pltpu.make_async_copy(tok_ref, stream.at[2 * gather.x + core], local_sem.at[1])]
    for copy in keep:
        copy.start()

    wait(0, z, y_back)
    push(0, z, y_back, y=y_ahead)
    push(0, z, y_back, z=z_ahead)
    push(0, z, y_back, z=z_back)
    wait(1, z_back, y)
    push(1, z_back, y, z=z_ahead)
    push(1, z_back, y, y=y_ahead)
    push(1, z_back, y, y=y_back)
    wait(0, z, y_ahead)
    push(0, z, y_ahead, z=z_ahead)
    push(0, z, y_ahead, z=z_back)
    wait(1, z_ahead, y)
    push(1, z_ahead, y, y=y_ahead)
    push(1, z_ahead, y, y=y_back)
    gather.relay()
    wait(0, z, y_far)
    push(0, z, y_far, z=z_ahead)
    push(0, z, y_far, z=z_back)
    wait(1, z_far, y)
    push(1, z_far, y, y=y_ahead)
    push(1, z_far, y, y=y_back)

    row = lax.broadcasted_iota(jnp.int32, (rows, 1), 0)
    offset = row
    end = 0
    for r in range(requests):
        end = end + length_ref[0, r]
        offset = offset - jnp.where(row >= end, length_ref[0, r], 0)
    lane = lax.broadcasted_iota(jnp.int32, (1, size), 1)
    freq = jnp.exp((lane & (size // 2 - 1)).astype(F32) * (-2.0 * LOG_THETA / size))
    angle = (PLEN + offset).astype(F32) * freq
    cosine, sine = jnp.cos(angle), jnp.sin(angle)

    def turned(value, gain):
        value = value * lax.rsqrt(jnp.mean(value * value, axis=1, keepdims=True) + EPS) * gain
        other = jnp.concatenate([-value[:, size // 2:], value[:, : size // 2]], axis=1)
        return (value * cosine + other * sine).astype(BF16)

    keep[1].wait()
    gather.close()
    normalise(stream, gain_ref, normed)

    far_z = [(py, z_back, z_ahead) for py in (y, y_far)] + [(py, z_ahead, z_back) for py in (y_back, y_ahead)]
    far_y = [(pz, y_back, y_ahead) for pz in (z, z_far)] + [(pz, y_ahead, y_back) for pz in (z_back, z_ahead)]
    order = (0, 2, 3, 1)
    for i in order:
        py, come, go = far_z[i]
        wait(0, come, py)
        push(0, come, py, z=go)
        pz, come, go = far_y[i]
        wait(1, pz, come)
        push(1, pz, come, y=go)

    arrived(passing, wrecv.at[2])
    give(3, passing, piece(z, y_back), y=y_ahead)
    arrived(piece(z_back, y), wrecv.at[4])
    give(6, piece(z_back, y), piece(z_back, y), z=z_ahead)

    query = dot(normed[...], wq_ref[...])
    keyval = dot(normed[...], wkv_ref[...])
    heads = query.shape[1] // size
    zero = jnp.zeros((rows, size), BF16)
    for h in range(heads):
        value = turned(query[:, h * size:(h + 1) * size], qgain_ref[...])
        value = jnp.concatenate([value * jnp.asarray(scale, BF16), zero], axis=1)
        for i in range(rows // BLOCK):
            q_out[i, h * BLOCK:(h + 1) * BLOCK, :] = value[i * BLOCK:(i + 1) * BLOCK]
    own_out[...] = jnp.concatenate(
        [turned(keyval[:, :size], kgain_ref[...]), keyval[:, size:].astype(BF16)], axis=1
    )

    for py, come, go in far_z:
        wait(0, go, py)
    for pz, come, go in far_y:
        wait(1, pz, go)
    for py, come, go in far_z:
        wait(0, z_far, py)
    for pz, come, go in far_y:
        wait(1, pz, y_far)
    arrived(piece(z, y_back), wrecv.at[0])
    arrived(piece(z, y_ahead), wrecv.at[1])
    arrived(piece(z, y_far), wrecv.at[3])
    arrived(piece(z_ahead, y), wrecv.at[5])
    arrived(piece(z_far, y), wrecv.at[6])
    keep[0].wait()
    gather.finish()
    for copy in sent + given:
        copy.wait_send()


def vmem():
    return pl.BlockSpec(memory_space=pltpu.VMEM)


def hbm():
    return pl.BlockSpec(memory_space=pl.ANY)


def smem():
    return pl.BlockSpec(memory_space=pltpu.SMEM)


def entry(lengths, tokens, attn_gain, q_gain, k_gain, w_query, w_keyval, prefix_kv, w_head):
    rows, width = tokens.shape
    size = q_gain.shape[1]
    heads = w_query.shape[1] // size
    count = RING * RING
    quarter = (w_head.shape[0], w_head.shape[1] // RING)
    return pl.pallas_call(
        functools.partial(entry_kernel, lengths.shape[1], size ** (-0.5)),
        in_specs=[smem()] + [vmem()] * 7 + [hbm()],
        out_specs=[vmem(), vmem(), hbm(), hbm(), hbm()],
        out_shape=[jax.ShapeDtypeStruct((rows // BLOCK, heads * BLOCK, 2 * size), BF16),
                   jax.ShapeDtypeStruct((rows, 2 * size), BF16),
                   jax.ShapeDtypeStruct((count,) + prefix_kv.shape[1:], BF16),
                   jax.ShapeDtypeStruct((count,) + quarter, BF16),
                   jax.ShapeDtypeStruct(quarter, BF16)],
        scratch_shapes=[pltpu.VMEM((8, rows, width), BF16), pltpu.VMEM((rows, 8 * width), BF16),
                        pltpu.SemaphoreType.DMA((7,)), pltpu.SemaphoreType.DMA((8,)),
                        pltpu.SemaphoreType.DMA((30,)), pltpu.SemaphoreType.DMA((2, count)),
                        pltpu.SemaphoreType.DMA((7,)), pltpu.SemaphoreType.DMA((7,)),
                        pltpu.SemaphoreType.DMA((2,))],
        compiler_params=pltpu.CompilerParams(collective_id=1, has_side_effects=True),
        cost_estimate=pl.CostEstimate(flops=30 << 30, bytes_accessed=8 << 20, transcendentals=0),
        name="entry",
    )(lengths, tokens, attn_gain, q_gain, k_gain, w_query, w_keyval, prefix_kv, w_head)


def attention_kernel(requests, split, length_ref, tenant_ref, piece_ref,
                     q_ref, own_ref, kv_ref, out_ref, best_ref, total_ref, accum_ref, slot_ref):
    block = pl.program_id(0)
    queries = q_ref[0]
    count = queries.shape[0]
    rows = own_ref.shape[0]
    size = own_ref.shape[1] // 2
    for j in range(kv_ref.shape[0]):
        slot_ref[piece_ref[j]] = j
    row = (lax.broadcasted_iota(jnp.int32, (count, 1), 0) & (BLOCK - 1)) + block * BLOCK
    col = lax.broadcasted_iota(jnp.int32, (1, rows), 1)
    row_request = jnp.zeros((count, 1), jnp.int32)
    col_request = jnp.zeros((1, rows), jnp.int32)
    ends = []
    for r in range(requests):
        ends.append(length_ref[0, r] + (ends[-1] if ends else 0))
        row_request += (row >= ends[r]).astype(jnp.int32)
        col_request += (col >= ends[r]).astype(jnp.int32)
    seen = (row_request == col_request) & (col <= row)
    own = own_ref[...]
    scores = jnp.where(seen, dot_nt(queries, own), NEG)
    best = jnp.max(scores, axis=1, keepdims=True)
    weights = jnp.where(seen, jnp.exp(scores - best), 0.0)
    best_ref[...] = best
    total_ref[...] = jnp.sum(weights, axis=1, keepdims=True)
    accum_ref[...] = dot(weights.astype(BF16), own)
    for r in range(requests):
        begin = ends[r] - length_ref[0, r]

        @pl.when((ends[r] > block * BLOCK) & (begin < block * BLOCK + BLOCK))
        def _():
            inside = row_request == r
            tenant = tenant_ref[0, r]

            def piece(index, carry):
                keyval = kv_ref[slot_ref[tenant * split + index]]
                part = dot_nt(queries, keyval)
                old = best_ref[...]
                new = jnp.where(inside, jnp.maximum(old, jnp.max(part, axis=1, keepdims=True)), old)
                keep = jnp.exp(old - new)
                piece_weights = jnp.exp(part - jnp.where(inside, new, -NEG))
                best_ref[...] = new
                total_ref[...] = total_ref[...] * keep + jnp.sum(piece_weights, axis=1, keepdims=True)
                accum_ref[...] = accum_ref[...] * keep + dot(piece_weights.astype(BF16), keyval)
                return carry

            lax.fori_loop(0, split, piece, 0)

    out = accum_ref[...] / total_ref[...]
    heads = [out[h * BLOCK:(h + 1) * BLOCK, size:] for h in range(count // BLOCK)]
    out_ref[...] = jnp.concatenate(heads, axis=1).astype(BF16)


def attention(lengths, tenants, prefix_piece, queries, own, pieces):
    blocks, count, width = queries.shape
    rows = own.shape[0]
    columns = count // BLOCK * width // 2
    return pl.pallas_call(
        functools.partial(attention_kernel, lengths.shape[1], pieces.shape[0] // TENANTS),
        grid=(blocks,),
        in_specs=[smem(), smem(), smem(),
                  pl.BlockSpec((1, count, width), lambda i: (i, 0, 0)),
                  pl.BlockSpec(own.shape, lambda i: (0, 0)),
                  pl.BlockSpec(pieces.shape, lambda i: (0, 0, 0), pipeline_mode=pl.Buffered(1))],
        out_specs=pl.BlockSpec((BLOCK, columns), lambda i: (i, 0)),
        out_shape=jax.ShapeDtypeStruct((rows, columns), BF16),
        scratch_shapes=[pltpu.VMEM((count, 1), F32), pltpu.VMEM((count, 1), F32),
                        pltpu.VMEM((count, width), F32), pltpu.SMEM((pieces.shape[0],), jnp.int32)],
        cost_estimate=pl.CostEstimate(flops=24 << 30, bytes_accessed=5 << 20, transcendentals=0),
        name="attention",
    )(lengths, tenants, prefix_piece, queries, own, pieces)


def finish_kernel(att_ref, tok_ref, gain_ref, wo_ref, last_gain_ref, target_ref, wg_hbm, wu_hbm, wd_hbm,
                  head_hbm, pieces_hbm, out_ref, log_ref,
                  wg, wu, wd, stage, paired, inbox, stage2, paired2, inbox2, mid, normed, inner,
                  weight, hidden, logits, wanted, stat, stat_y, stat_m,
                  load, send, pair_sem, in_sem, send2, pair_sem2, in_sem2, msend, mrecv,
                  gsend, grecv, ysend, yrecv, tsend, trecv, ssend, srecv, ksend, krecv,
                  zsend, zrecv):
    core = lax.axis_index("c")
    rows, width = tok_ref.shape
    depth, vocab = pieces_hbm.shape[1:]
    x, x_ahead, x_back, x_far = ring_of("x", core)
    y, y_ahead, y_back, y_far = ring_of("y", core)
    z, z_ahead, z_back, z_far = ring_of("z", core)
    mine = 2 * x + core
    sent = []

    def push(src, dst, send_sem, recv_sem, **device):
        copy = remote(src, dst, send_sem, recv_sem, **device)
        copy.start()
        sent.append(copy)

    def columns(index, count):
        return pl.ds(pl.multiple_of(index * count, count), count)

    def place(pz, py):
        return weight.at[columns(pz * RING + py, depth)]

    loads = []

    def fetch(src, dst):
        copy = pltpu.make_async_copy(src, dst, load.at[len(loads)])
        copy.start()
        loads.append(copy)

    fetch(wg_hbm, wg)
    fetch(wu_hbm, wu)
    fetch(wd_hbm, wd)
    fetch(head_hbm.at[:, columns(y, vocab)], place(z, y))
    for pz in (z_ahead, z_back, z_far):
        fetch(pieces_hbm.at[pz * RING + y], place(pz, y))
    rest = (y_back, y_ahead, y_far)
    for py in rest:
        fetch(pieces_hbm.at[z * RING + py], place(z, py))
    others = [dict(x=lax.rem(x + i // 2, RING), c=lax.rem(core + i % 2, 2)) for i in range(1, 8)]
    greet([dict(y=y_ahead), dict(y=y_back), dict(y=y_far), dict(z=z_ahead), dict(z=z_back)] + others)

    for i, py in enumerate(rest):
        source = pieces_hbm.at[z * RING + py]
        push(source, place(z, py), zsend.at[i, 0], zrecv.at[i, 0], z=z_ahead)
        push(source, place(z, py), zsend.at[i, 1], zrecv.at[i, 1], z=z_back)
    for i, to in enumerate((y_ahead, y_back, y_far)):
        push(target_ref, wanted.at[y], tsend.at[i], trecv.at[i], y=to)
    wanted[y] = target_ref[...]

    def head_relay(i):
        arrived(place(z_back, rest[i]), zrecv.at[i, 0])
        push(place(z_back, rest[i]), place(z_back, rest[i]), zsend.at[i, 2], zrecv.at[i, 2], z=z_ahead)

    att = att_ref[...]
    value = scatter_sum(lambda d: dot(att, wo_ref[:, columns(d, width)]),
                        stage, paired, inbox, send, pair_sem, in_sem)
    middle = Gather(mid, msend, mrecv)
    mid[mine] = (tok_ref[...].astype(F32) + value).astype(BF16)
    middle.open()
    middle.relay()
    middle.close()
    normalise(mid, gain_ref, normed)
    head_relay(0)
    loads[0].wait()
    loads[1].wait()
    for t in range(inner.shape[1] // width):
        tile = slice(t * width, (t + 1) * width)
        gate = dot(normed[...], wg[:, tile])
        upper = dot(normed[...], wu[:, tile])
        inner[:, tile] = (gate / (1.0 + jnp.exp(-gate)) * upper).astype(BF16)
    loads[2].wait()
    head_relay(1)
    value = scatter_sum(lambda d: dot(inner[...], wd[:, columns(d, width)]),
                        stage2, paired2, inbox2, send2, pair_sem2, in_sem2)
    share = (mid[mine].astype(F32) + value).astype(BF16)
    out_ref[...] = share
    hidden[y, mine] = share

    gathers = {}

    def gather_of(index, group):
        gathers[index] = Gather(hidden.at[group], gsend.at[index], grecv.at[group])
        return gathers[index]

    own = hidden.at[y, mine]
    first = gather_of(0, y)
    push(own, own, ysend.at[0], yrecv.at[0], y=y_ahead)
    push(own, own, ysend.at[1], yrecv.at[1], y=y_back)
    first.open()
    head_relay(2)

    arrived(hidden.at[y_back, mine], yrecv.at[0])
    push(hidden.at[y_back, mine], hidden.at[y_back, mine], ysend.at[2], yrecv.at[2], y=y_ahead)
    arrived(hidden.at[y_ahead, mine], yrecv.at[1])
    y_down, y_up = lax.rem(y + 3, RING), lax.rem(y + 1, RING)
    gather_of(1, y_down).open()
    gather_of(2, y_up).open()
    first.relay()
    arrived(hidden.at[y_far, mine], yrecv.at[2])
    gather_of(3, y_far).open()
    gathers[1].relay()
    first.close()
    for i, group in enumerate((y_back, y_ahead, y_far)):
        arrived(wanted.at[group], trecv.at[i])
    for copy in loads[3:]:
        copy.wait()
    for i, py in enumerate(rest):
        arrived(place(z_ahead, py), zrecv.at[i, 1])
        arrived(place(z_far, py), zrecv.at[i, 2])

    tile = 512
    eye = (lax.broadcasted_iota(jnp.int32, (rows, rows), 0)
           == lax.broadcasted_iota(jnp.int32, (rows, rows), 1))
    start = (mine * RING + y) * vocab
    column = lax.broadcasted_iota(jnp.int32, (1, vocab), 1)

    def to_row(value):
        return jnp.sum(jnp.where(eye, value, 0.0), axis=0, keepdims=True)

    for index, group in enumerate((y, y_down, y_up, y_far)):
        if index:
            gathers[index].close()
        normalise(hidden.at[group], last_gain_ref, normed)
        if index == 0:
            gathers[2].relay()
        for t in range(vocab // tile):
            logits[:, t * tile:(t + 1) * tile] = dot(normed[...], weight[:, t * tile:(t + 1) * tile])
        if index == 0:
            gathers[3].relay()
        value = logits[...]
        top = jnp.max(value, axis=1, keepdims=True)
        total = jnp.sum(jnp.exp(value - top), axis=1, keepdims=True)
        target = jnp.sum(jnp.where(eye, wanted[group], 0), axis=1, keepdims=True)
        picked = jnp.sum(jnp.where(target - start == column, value, 0.0), axis=1, keepdims=True)
        stat[group, 0:1, :] = to_row(top)
        stat[group, 1:2, :] = to_row(total)
        stat[group, 2:3, :] = to_row(picked)
        if index:
            push(stat.at[group], stat_y.at[y], ssend.at[index - 1], srecv.at[y], y=group)

    stat_y[y] = stat[y]
    for group in (y_back, y_ahead, y_far):
        arrived(stat_y.at[group], srecv.at[group])

    def merge(parts, count):
        top = parts[0, 0:1, :]
        for i in range(1, count):
            top = jnp.maximum(top, parts[i, 0:1, :])
        total = jnp.zeros_like(top)
        picked = jnp.zeros_like(top)
        for i in range(count):
            total += parts[i, 1:2, :] * jnp.exp(parts[i, 0:1, :] - top)
            picked += parts[i, 2:3, :]
        return (top, total, picked)

    for i, value in enumerate(merge(stat_y, RING)):
        stat_m[mine, i:i + 1, :] = value
    for i, peer in enumerate(others):
        push(stat_m.at[mine], stat_m.at[mine], ksend.at[i], krecv.at[mine], **peer)
    for peer in others:
        slot = 2 * peer["x"] + peer["c"]
        arrived(stat_m.at[slot], krecv.at[slot])
    top, total, picked = merge(stat_m, 8)
    log_ref[...] = picked - top - jnp.log(total)
    middle.finish()
    for gather in gathers.values():
        gather.finish()
    for copy in sent:
        copy.wait_send()


def finish(attended, tokens, mlp_gain, w_out, final_gain, targets, w_gate, w_up, w_down, w_head, pieces):
    rows, width = tokens.shape
    units = w_gate.shape[1]
    block = (rows, width)
    vocab = pieces.shape[2]
    dma = pltpu.SemaphoreType.DMA
    stats = (8, rows)

    def blocks(n):
        return pltpu.VMEM((n,) + block, BF16)

    return pl.pallas_call(
        finish_kernel,
        in_specs=[vmem()] * 6 + [hbm()] * 5,
        out_specs=[vmem(), vmem()],
        out_shape=[jax.ShapeDtypeStruct(block, BF16), jax.ShapeDtypeStruct((1, rows), F32)],
        scratch_shapes=[pltpu.VMEM(w_gate.shape, BF16), pltpu.VMEM(w_up.shape, BF16),
                        pltpu.VMEM(w_down.shape, BF16),
                        blocks(7), blocks(4), blocks(3), blocks(7), blocks(4), blocks(3), blocks(8),
                        pltpu.VMEM((rows, 8 * width), BF16), pltpu.VMEM((rows, units), BF16),
                        pltpu.VMEM((8 * width, vocab), BF16), pltpu.VMEM((RING, 8) + block, BF16),
                        pltpu.VMEM((rows, vocab), F32),
                        pltpu.VMEM((RING, 1, rows), jnp.int32), pltpu.VMEM((RING,) + stats, F32),
                        pltpu.VMEM((RING,) + stats, F32), pltpu.VMEM((8,) + stats, F32),
                        dma((10,)), dma((7,)), dma((4,)), dma((3,)), dma((7,)), dma((4,)), dma((3,)),
                        dma((7,)), dma((8,)),
                        dma((4, 7)), dma((4, 8)), dma((3,)), dma((3,)), dma((3,)), dma((3,)),
                        dma((3,)), dma((4,)), dma((7,)), dma((8,)), dma((3, 3)), dma((3, 3))],
        compiler_params=pltpu.CompilerParams(collective_id=2, has_side_effects=True,
                                             vmem_limit_bytes=56 << 20),
        cost_estimate=pl.CostEstimate(flops=60 << 30, bytes_accessed=24 << 20, transcendentals=0),
        name="finish",
    )(attended, tokens, mlp_gain, w_out, final_gain, targets, w_gate, w_up, w_down, w_head, pieces)


def body(tokens, attn_gain, mlp_gain, final_gain, q_gain, k_gain, w_query, w_keyval, w_out, w_gate,
         w_up, w_down, w_head, targets, req_lengths, req_tenant, prefix_piece, prefix_kv):
    queries, own, pieces, slabs, _ = entry(
        req_lengths, tokens, attn_gain[None], q_gain[None], k_gain[None], w_query, w_keyval,
        prefix_kv, w_head)
    attended = attention(req_lengths, req_tenant, prefix_piece, queries, own, pieces)
    share, logprob = finish(attended, tokens, mlp_gain[None], w_out, final_gain[None], targets[None],
                            w_gate, w_up, w_down, w_head, slabs)
    return (share, logprob[0])


def solution(mesh):
    req = ("z", "y")
    mlp = ("x", "c")
    in_specs = (
        P(req, mlp), P(), P(), P(), P(), P(), P(None, mlp), P(None, mlp), P(mlp, None),
        P(None, mlp), P(None, mlp), P(mlp, None), P(req, mlp), P(req), P(req, None), P(req, None),
        P(), P(req, None, mlp),
    )
    out_specs = (P(req, mlp), P(req))
    split = Mesh(mesh.devices.reshape(RING, RING, RING, 2), ("z", "y", "x", "c"))
    return jax.shard_map(body, mesh=split, in_specs=in_specs, out_specs=out_specs, check_vma=False)
```

```python
import functools
import math

import jax
import jax.numpy as jnp
from jax import lax
from jax.experimental import pallas as pl
from jax.experimental.pallas import tpu as pltpu
from jax.sharding import Mesh
from jax.sharding import PartitionSpec as P

TENANTS = 4
PLEN = 4096
BLOCK = 64
EPS = 1e-05
LOG_THETA = math.log(1000000.0)
NEG = -1e30
RING = 4
MESH = pl.DeviceIdType.MESH
F32 = jnp.float32
BF16 = jnp.bfloat16


def dot(a, b):
    return jnp.dot(a, b, preferred_element_type=F32)


def dot_nt(a, b):
    return lax.dot_general(a, b, (((1,), (1,)), ((), ())), preferred_element_type=F32)


def remote(src, dst, send_sem, recv_sem, **device):
    return pltpu.make_async_remote_copy(
        src_ref=src, dst_ref=dst, send_sem=send_sem, recv_sem=recv_sem,
        device_id=device, device_id_type=MESH,
    )


def arrived(ref, sem):
    pltpu.make_async_copy(ref, ref, sem).wait()


def greet(peers):
    barrier = pltpu.get_barrier_semaphore()
    for peer in peers:
        pl.semaphore_signal(barrier, inc=1, device_id=peer, device_id_type=MESH)
    pl.semaphore_wait(barrier, len(peers))


def ring_of(axis, core):
    me = lax.axis_index(axis)
    ahead = lax.rem(me + 1 + 2 * core, RING)
    back = lax.rem(me + 3 + 2 * core, RING)
    far = lax.rem(me + 2, RING)
    return (me, ahead, back, far)


class Gather:
    def __init__(self, slots, send, recv):
        self.slots, self.send, self.recv, self.sent = slots, send, recv, []
        self.core = lax.axis_index("c")
        self.x, self.ahead, self.back, self.far = ring_of("x", self.core)

    def push(self, at, core, src=None, **device):
        slot = 2 * at + core
        copy = remote(self.slots.at[slot] if src is None else src, self.slots.at[slot],
                      self.send.at[len(self.sent)], self.recv.at[slot], **device)
        copy.start()
        self.sent.append(copy)

    def wait(self, at, core):
        slot = 2 * at + core
        arrived(self.slots.at[slot], self.recv.at[slot])

    def open(self, src=None):
        self.push(self.x, self.core, src, x=self.ahead)
        self.push(self.x, self.core, src, x=self.back)
        self.push(self.x, self.core, src, c=1 - self.core)

    def relay(self):
        self.wait(self.back, self.core)
        self.push(self.back, self.core, x=self.ahead)
        self.push(self.back, self.core, c=1 - self.core)
        self.wait(self.ahead, self.core)
        self.push(self.ahead, self.core, c=1 - self.core)

    def last(self):
        self.wait(self.far, self.core)
        self.push(self.far, self.core, c=1 - self.core)

    def close(self):
        self.last()
        self.rest()

    def rest(self):
        for x in (self.x, self.back, self.ahead, self.far):
            self.wait(x, 1 - self.core)

    def finish(self):
        for copy in self.sent:
            copy.wait_send()


def scatter_sum(partial, stage, paired, inbox, send, pair_sem, in_sem):
    core = lax.axis_index("c")
    x, ahead, back, far = ring_of("x", core)
    sent = []

    def push(value, dst, recv, **device):
        index = len(sent)
        stage[index] = value.astype(BF16)
        copy = remote(stage.at[index], dst, send.at[index], recv, **device)
        copy.start()
        sent.append(copy)

    def chip(to):
        mine = partial(2 * to + core)
        arrived(paired.at[to], pair_sem.at[to])
        return mine + paired[to].astype(F32)

    for to in (far, back, ahead, x):
        push(partial(2 * to + 1 - core), paired.at[to], pair_sem.at[to], c=1 - core)
    push(chip(far), inbox.at[2], in_sem.at[2], x=ahead)
    push(chip(back), inbox.at[1], in_sem.at[1], x=back)
    value = chip(ahead)
    arrived(inbox.at[2], in_sem.at[2])
    push(value + inbox[2].astype(F32), inbox.at[0], in_sem.at[0], x=ahead)
    value = chip(x)
    for slot in (1, 0):
        arrived(inbox.at[slot], in_sem.at[slot])
        value += inbox[slot].astype(F32)
    for copy in sent:
        copy.wait_send()
    return value


def normalise(blocks, gain_ref, normed):
    count, rows, width = blocks.shape
    square = jnp.zeros((rows, 1), F32)
    for m in range(count):
        value = blocks[m].astype(F32)
        square += jnp.sum(value * value, axis=1, keepdims=True)
    factor = lax.rsqrt(square / (count * width) + EPS)
    for m in range(count):
        columns = slice(m * width, (m + 1) * width)
        normed[:, columns] = (blocks[m].astype(F32) * factor * gain_ref[:, columns]).astype(BF16)


def x_peers():
    core = lax.axis_index("c")
    _, ahead, back, _ = ring_of("x", core)
    return [dict(x=ahead), dict(x=back), dict(c=1 - core)]


def entry_kernel(requests, scale, length_ref, tok_ref, gain_ref, qgain_ref, kgain_ref, wq_ref,
                 wkv_ref, prefix_ref, head_ref, q_out, own_out, pieces, head_out, stream,
                 normed, send, recv, psend, precv, wsend, wrecv, local_sem):
    core = lax.axis_index("c")
    rows = tok_ref.shape[0]
    size = qgain_ref.shape[1]
    half = prefix_ref.shape[1] // 2
    y, y_ahead, y_back, y_far = ring_of("y", core)
    z, z_ahead, z_back, z_far = ring_of("z", core)
    greet(x_peers() + [dict(y=y_ahead), dict(y=y_back), dict(z=z_ahead), dict(z=z_back)])

    sent = []

    def view(part, pz, py):
        return pieces.at[pz * RING + py, pl.ds(part * half, half)]

    def push(part, pz, py, src=None, **device):
        slot = pz * RING + py
        copy = remote(view(part, pz, py) if src is None else src, view(part, pz, py),
                      psend.at[len(sent)], precv.at[part, slot], **device)
        copy.start()
        sent.append(copy)

    def wait(part, pz, py):
        arrived(view(part, pz, py), precv.at[part, pz * RING + py])

    first = [prefix_ref.at[0, pl.ds(part * half, half)] for part in range(2)]
    gather = Gather(stream, send, recv)
    gather.open(tok_ref)
    push(0, z, y, first[0], y=y_ahead)
    push(0, z, y, first[0], y=y_back)
    push(1, z, y, first[1], z=z_ahead)
    push(1, z, y, first[1], z=z_back)
    push(0, z, y, first[0], z=z_ahead)
    push(0, z, y, first[0], z=z_back)
    push(1, z, y, first[1], y=y_ahead)
    push(1, z, y, first[1], y=y_back)

    given = []
    part_words = head_out.shape[2]

    def words(index):
        return head_ref.at[:, pl.ds(pl.multiple_of(index * part_words, part_words), part_words)]

    def piece(pz, py):
        return head_out.at[pz * RING + py]

    def give(index, src, dst, **device):
        copy = remote(src, dst, wsend.at[index], wrecv.at[index], **device)
        copy.start()
        given.append(copy)

    give(2, words(y), piece(z, y), z=z_ahead)
    give(3, words(y), piece(z, y), z=z_back)
    give(0, words(y_ahead), piece(z, y), y=y_ahead)
    give(1, words(y_back), piece(z, y), y=y_back)
    keep = [pltpu.make_async_copy(prefix_ref.at[0], pieces.at[z * RING + y], local_sem.at[0]),
            pltpu.make_async_copy(tok_ref, stream.at[2 * gather.x + core], local_sem.at[1])]
    for copy in keep:
        copy.start()

    wait(0, z, y_back)
    push(0, z, y_back, y=y_ahead)
    push(0, z, y_back, z=z_ahead)
    push(0, z, y_back, z=z_back)
    wait(1, z_back, y)
    push(1, z_back, y, z=z_ahead)
    push(1, z_back, y, y=y_ahead)
    push(1, z_back, y, y=y_back)
    wait(0, z, y_ahead)
    push(0, z, y_ahead, z=z_ahead)
    push(0, z, y_ahead, z=z_back)
    wait(1, z_ahead, y)
    push(1, z_ahead, y, y=y_ahead)
    push(1, z_ahead, y, y=y_back)
    gather.relay()
    wait(0, z, y_far)
    push(0, z, y_far, z=z_ahead)
    push(0, z, y_far, z=z_back)
    wait(1, z_far, y)
    push(1, z_far, y, y=y_ahead)
    push(1, z_far, y, y=y_back)

    row = lax.broadcasted_iota(jnp.int32, (rows, 1), 0)
    offset = row
    end = 0
    for r in range(requests):
        end = end + length_ref[0, r]
        offset = offset - jnp.where(row >= end, length_ref[0, r], 0)
    lane = lax.broadcasted_iota(jnp.int32, (1, size), 1)
    freq = jnp.exp((lane & (size // 2 - 1)).astype(F32) * (-2.0 * LOG_THETA / size))
    angle = (PLEN + offset).astype(F32) * freq
    cosine, sine = jnp.cos(angle), jnp.sin(angle)

    def turned(value, gain):
        value = value * lax.rsqrt(jnp.mean(value * value, axis=1, keepdims=True) + EPS) * gain
        other = jnp.concatenate([-value[:, size // 2:], value[:, : size // 2]], axis=1)
        return (value * cosine + other * sine).astype(BF16)

    keep[1].wait()
    gather.close()
    normalise(stream, gain_ref, normed)

    far_z = [(py, z_back, z_ahead) for py in (y, y_far)] + [(py, z_ahead, z_back) for py in (y_back, y_ahead)]
    far_y = [(pz, y_back, y_ahead) for pz in (z, z_far)] + [(pz, y_ahead, y_back) for pz in (z_back, z_ahead)]
    order = (0, 2, 3, 1)
    arrived(piece(z_back, y), wrecv.at[2])
    give(4, piece(z_back, y), piece(z_back, y), z=z_ahead)
    for i in order:
        py, come, go = far_z[i]
        wait(0, come, py)
        push(0, come, py, z=go)
        pz, come, go = far_y[i]
        wait(1, pz, come)
        push(1, pz, come, y=go)

    query = dot(normed[...], wq_ref[...])
    keyval = dot(normed[...], wkv_ref[...])
    heads = query.shape[1] // size
    zero = jnp.zeros((rows, size), BF16)
    for h in range(heads):
        value = turned(query[:, h * size:(h + 1) * size], qgain_ref[...])
        value = jnp.concatenate([value * jnp.asarray(scale, BF16), zero], axis=1)
        for i in range(rows // BLOCK):
            q_out[i, h * BLOCK:(h + 1) * BLOCK, :] = value[i * BLOCK:(i + 1) * BLOCK]
    own_out[...] = jnp.concatenate(
        [turned(keyval[:, :size], kgain_ref[...]), keyval[:, size:].astype(BF16)], axis=1
    )

    for py, come, go in far_z:
        wait(0, go, py)
    for pz, come, go in far_y:
        wait(1, pz, go)
    for py, come, go in far_z:
        wait(0, z_far, py)
    for pz, come, go in far_y:
        wait(1, pz, y_far)
    arrived(piece(z, y_back), wrecv.at[0])
    arrived(piece(z, y_ahead), wrecv.at[1])
    arrived(piece(z_ahead, y), wrecv.at[3])
    arrived(piece(z_far, y), wrecv.at[4])
    keep[0].wait()
    gather.finish()
    for copy in sent + given:
        copy.wait_send()


def vmem():
    return pl.BlockSpec(memory_space=pltpu.VMEM)


def hbm():
    return pl.BlockSpec(memory_space=pl.ANY)


def smem():
    return pl.BlockSpec(memory_space=pltpu.SMEM)


def entry(lengths, tokens, attn_gain, q_gain, k_gain, w_query, w_keyval, prefix_kv, w_head):
    rows, width = tokens.shape
    size = q_gain.shape[1]
    heads = w_query.shape[1] // size
    count = RING * RING
    quarter = (w_head.shape[0], w_head.shape[1] // RING)
    return pl.pallas_call(
        functools.partial(entry_kernel, lengths.shape[1], size ** (-0.5)),
        in_specs=[smem()] + [vmem()] * 7 + [hbm()],
        out_specs=[vmem(), vmem(), hbm(), hbm()],
        out_shape=[jax.ShapeDtypeStruct((rows // BLOCK, heads * BLOCK, 2 * size), BF16),
                   jax.ShapeDtypeStruct((rows, 2 * size), BF16),
                   jax.ShapeDtypeStruct((count,) + prefix_kv.shape[1:], BF16),
                   jax.ShapeDtypeStruct((count,) + quarter, BF16)],
        scratch_shapes=[pltpu.VMEM((8, rows, width), BF16), pltpu.VMEM((rows, 8 * width), BF16),
                        pltpu.SemaphoreType.DMA((7,)), pltpu.SemaphoreType.DMA((8,)),
                        pltpu.SemaphoreType.DMA((30,)), pltpu.SemaphoreType.DMA((2, count)),
                        pltpu.SemaphoreType.DMA((5,)), pltpu.SemaphoreType.DMA((5,)),
                        pltpu.SemaphoreType.DMA((2,))],
        compiler_params=pltpu.CompilerParams(collective_id=1, has_side_effects=True),
        cost_estimate=pl.CostEstimate(flops=30 << 30, bytes_accessed=8 << 20, transcendentals=0),
        name="entry",
    )(lengths, tokens, attn_gain, q_gain, k_gain, w_query, w_keyval, prefix_kv, w_head)


def attention_kernel(requests, split, length_ref, tenant_ref, piece_ref,
                     q_ref, own_ref, kv_ref, out_ref, best_ref, total_ref, accum_ref, slot_ref):
    block = pl.program_id(0)
    queries = q_ref[0]
    count = queries.shape[0]
    rows = own_ref.shape[0]
    size = own_ref.shape[1] // 2
    for j in range(kv_ref.shape[0]):
        slot_ref[piece_ref[j]] = j
    row = (lax.broadcasted_iota(jnp.int32, (count, 1), 0) & (BLOCK - 1)) + block * BLOCK
    col = lax.broadcasted_iota(jnp.int32, (1, rows), 1)
    row_request = jnp.zeros((count, 1), jnp.int32)
    col_request = jnp.zeros((1, rows), jnp.int32)
    ends = []
    for r in range(requests):
        ends.append(length_ref[0, r] + (ends[-1] if ends else 0))
        row_request += (row >= ends[r]).astype(jnp.int32)
        col_request += (col >= ends[r]).astype(jnp.int32)
    seen = (row_request == col_request) & (col <= row)
    own = own_ref[...]
    scores = jnp.where(seen, dot_nt(queries, own), NEG)
    best = jnp.max(scores, axis=1, keepdims=True)
    weights = jnp.where(seen, jnp.exp(scores - best), 0.0)
    best_ref[...] = best
    total_ref[...] = jnp.sum(weights, axis=1, keepdims=True)
    accum_ref[...] = dot(weights.astype(BF16), own)
    for r in range(requests):
        begin = ends[r] - length_ref[0, r]

        @pl.when((ends[r] > block * BLOCK) & (begin < block * BLOCK + BLOCK))
        def _():
            inside = row_request == r
            tenant = tenant_ref[0, r]

            def piece(index, carry):
                keyval = kv_ref[slot_ref[tenant * split + index]]
                part = dot_nt(queries, keyval)
                old = best_ref[...]
                new = jnp.where(inside, jnp.maximum(old, jnp.max(part, axis=1, keepdims=True)), old)
                keep = jnp.exp(old - new)
                piece_weights = jnp.exp(part - jnp.where(inside, new, -NEG))
                best_ref[...] = new
                total_ref[...] = total_ref[...] * keep + jnp.sum(piece_weights, axis=1, keepdims=True)
                accum_ref[...] = accum_ref[...] * keep + dot(piece_weights.astype(BF16), keyval)
                return carry

            lax.fori_loop(0, split, piece, 0)

    out = accum_ref[...] / total_ref[...]
    heads = [out[h * BLOCK:(h + 1) * BLOCK, size:] for h in range(count // BLOCK)]
    out_ref[...] = jnp.concatenate(heads, axis=1).astype(BF16)


def attention(lengths, tenants, prefix_piece, queries, own, pieces):
    blocks, count, width = queries.shape
    rows = own.shape[0]
    columns = count // BLOCK * width // 2
    return pl.pallas_call(
        functools.partial(attention_kernel, lengths.shape[1], pieces.shape[0] // TENANTS),
        grid=(blocks,),
        in_specs=[smem(), smem(), smem(),
                  pl.BlockSpec((1, count, width), lambda i: (i, 0, 0)),
                  pl.BlockSpec(own.shape, lambda i: (0, 0)),
                  pl.BlockSpec(pieces.shape, lambda i: (0, 0, 0), pipeline_mode=pl.Buffered(1))],
        out_specs=pl.BlockSpec((BLOCK, columns), lambda i: (i, 0)),
        out_shape=jax.ShapeDtypeStruct((rows, columns), BF16),
        scratch_shapes=[pltpu.VMEM((count, 1), F32), pltpu.VMEM((count, 1), F32),
                        pltpu.VMEM((count, width), F32), pltpu.SMEM((pieces.shape[0],), jnp.int32)],
        cost_estimate=pl.CostEstimate(flops=24 << 30, bytes_accessed=5 << 20, transcendentals=0),
        name="attention",
    )(lengths, tenants, prefix_piece, queries, own, pieces)


def finish_kernel(att_ref, tok_ref, gain_ref, wo_ref, last_gain_ref, target_ref, wg_hbm, wu_hbm, wd_hbm,
                  head_hbm, pieces_hbm, out_ref, log_ref,
                  wg, wu, wd, stage, paired, inbox, stage2, paired2, inbox2, mid, normed, inner,
                  weight, hidden, logits, wanted, stat, stat_y, stat_m,
                  load, send, pair_sem, in_sem, send2, pair_sem2, in_sem2, msend, mrecv,
                  gsend, grecv, ysend, tsend, trecv, ssend, srecv, ksend, krecv,
                  zsend, zrecv, passing, wsend, wrecv):
    core = lax.axis_index("c")
    rows, width = tok_ref.shape
    depth, vocab = pieces_hbm.shape[1:]
    x, x_ahead, x_back, x_far = ring_of("x", core)
    y, y_ahead, y_back, y_far = ring_of("y", core)
    z, z_ahead, z_back, z_far = ring_of("z", core)
    mine = 2 * x + core
    sent = []

    def push(src, dst, send_sem, recv_sem, **device):
        copy = remote(src, dst, send_sem, recv_sem, **device)
        copy.start()
        sent.append(copy)

    def columns(index, count):
        return pl.ds(pl.multiple_of(index * count, count), count)

    def place(pz, py):
        return weight.at[columns(pz * RING + py, depth)]

    loads = []

    def fetch(src, dst):
        copy = pltpu.make_async_copy(src, dst, load.at[len(loads)])
        copy.start()
        loads.append(copy)

    fetch(wg_hbm, wg)
    fetch(wu_hbm, wu)
    fetch(wd_hbm, wd)
    fetch(head_hbm.at[:, columns(y, vocab)], place(z, y))
    for pz in (z_ahead, z_back, z_far):
        fetch(pieces_hbm.at[pz * RING + y], place(pz, y))
    rest = (y_back, y_ahead, y_far)
    for py in rest[:2]:
        fetch(pieces_hbm.at[z * RING + py], place(z, py))
    others = [dict(x=lax.rem(x + i // 2, RING), c=lax.rem(core + i % 2, 2)) for i in range(1, 8)]
    greet([dict(y=y_ahead), dict(y=y_back), dict(y=y_far), dict(z=z_ahead), dict(z=z_back)] + others)

    def head_open(i, source):
        to = place(z, rest[i])
        push(source, to, zsend.at[i, 0], zrecv.at[i, 0], z=z_ahead)
        push(source, to, zsend.at[i, 1], zrecv.at[i, 1], z=z_back)

    push(head_hbm.at[:, columns(y_far, vocab)], passing, wsend.at[0], wrecv.at[0], y=y_ahead)
    for i in range(2):
        head_open(i, pieces_hbm.at[z * RING + rest[i]])
    for i, to in enumerate((y_ahead, y_back, y_far)):
        push(target_ref, wanted.at[y], tsend.at[i], trecv.at[i], y=to)
    wanted[y] = target_ref[...]

    def head_relay(i):
        arrived(place(z_back, rest[i]), zrecv.at[i, 0])
        push(place(z_back, rest[i]), place(z_back, rest[i]), zsend.at[i, 2], zrecv.at[i, 2], z=z_ahead)

    att = att_ref[...]
    value = scatter_sum(lambda d: dot(att, wo_ref[:, columns(d, width)]),
                        stage, paired, inbox, send, pair_sem, in_sem)
    middle = Gather(mid, msend, mrecv)
    mid[mine] = (tok_ref[...].astype(F32) + value).astype(BF16)
    middle.open()
    arrived(passing, wrecv.at[0])
    push(passing, place(z, y_back), wsend.at[1], wrecv.at[1], y=y_ahead)
    middle.relay()
    middle.close()
    normalise(mid, gain_ref, normed)
    arrived(place(z, y_far), wrecv.at[1])
    head_open(2, place(z, y_far))
    head_relay(0)
    loads[0].wait()
    loads[1].wait()
    for t in range(inner.shape[1] // width):
        tile = slice(t * width, (t + 1) * width)
        gate = dot(normed[...], wg[:, tile])
        upper = dot(normed[...], wu[:, tile])
        inner[:, tile] = (gate / (1.0 + jnp.exp(-gate)) * upper).astype(BF16)
    loads[2].wait()
    head_relay(1)
    value = scatter_sum(lambda d: dot(inner[...], wd[:, columns(d, width)]),
                        stage2, paired2, inbox2, send2, pair_sem2, in_sem2)
    share = (mid[mine].astype(F32) + value).astype(BF16)
    out_ref[...] = share
    hidden[y, mine] = share

    first = Gather(hidden.at[y], gsend.at[0], grecv.at[y])
    distant = Gather(hidden.at[y_far], gsend.at[1], grecv.at[y_far])
    y_down, y_up = lax.rem(y + 3, RING), lax.rem(y + 1, RING)
    moved = []

    def hand(group, slot, **device):
        push(hidden.at[group, slot], hidden.at[group, slot], ysend.at[len(moved)], grecv.at[group, slot],
             **device)
        moved.append(slot)

    def spread(to):
        hand(y, 2 * to + core, y=y_ahead)
        hand(y, 2 * to + core, y=y_back)

    def collect(group, to):
        arrived(hidden.at[group, 2 * to + core], grecv.at[group, 2 * to + core])
        hand(group, 2 * to + core, c=1 - core)

    first.open()
    spread(x)
    head_relay(2)
    first.relay()
    spread(x_back)
    spread(x_ahead)
    collect(y_back, x)
    hand(y_back, mine, y=y_ahead)
    collect(y_ahead, x)
    first.last()
    spread(x_far)
    arrived(hidden.at[y_far, mine], grecv.at[y_far, mine])
    distant.open()
    first.rest()
    for i, group in enumerate((y_back, y_ahead, y_far)):
        arrived(wanted.at[group], trecv.at[i])
    for copy in loads[3:]:
        copy.wait()
    for i, py in enumerate(rest):
        arrived(place(z_ahead, py), zrecv.at[i, 1])
        arrived(place(z_far, py), zrecv.at[i, 2])

    tile = 512
    eye = (lax.broadcasted_iota(jnp.int32, (rows, rows), 0)
           == lax.broadcasted_iota(jnp.int32, (rows, rows), 1))
    start = (mine * RING + y) * vocab
    column = lax.broadcasted_iota(jnp.int32, (1, vocab), 1)

    def to_row(value):
        return jnp.sum(jnp.where(eye, value, 0.0), axis=0, keepdims=True)

    for index, group in enumerate((y, y_down, y_up, y_far)):
        if index in (1, 2):
            for to in range(RING):
                slot = 2 * to + 1 - core
                arrived(hidden.at[group, slot], grecv.at[group, slot])
        if index == 3:
            distant.rest()
        normalise(hidden.at[group], last_gain_ref, normed)
        if index == 0:
            for to in (x_back, x_ahead):
                collect(y_back, to)
                collect(y_ahead, to)
            distant.relay()
        for t in range(vocab // tile):
            logits[:, t * tile:(t + 1) * tile] = dot(normed[...], weight[:, t * tile:(t + 1) * tile])
        if index == 0:
            collect(y_back, x_far)
            collect(y_ahead, x_far)
            distant.last()
        value = logits[...]
        top = jnp.max(value, axis=1, keepdims=True)
        total = jnp.sum(jnp.exp(value - top), axis=1, keepdims=True)
        target = jnp.sum(jnp.where(eye, wanted[group], 0), axis=1, keepdims=True)
        picked = jnp.sum(jnp.where(target - start == column, value, 0.0), axis=1, keepdims=True)
        stat[group, 0:1, :] = to_row(top)
        stat[group, 1:2, :] = to_row(total)
        stat[group, 2:3, :] = to_row(picked)
        if index:
            push(stat.at[group], stat_y.at[y], ssend.at[index - 1], srecv.at[y], y=group)

    stat_y[y] = stat[y]
    for group in (y_back, y_ahead, y_far):
        arrived(stat_y.at[group], srecv.at[group])

    def merge(parts, count):
        top = parts[0, 0:1, :]
        for i in range(1, count):
            top = jnp.maximum(top, parts[i, 0:1, :])
        total = jnp.zeros_like(top)
        picked = jnp.zeros_like(top)
        for i in range(count):
            total += parts[i, 1:2, :] * jnp.exp(parts[i, 0:1, :] - top)
            picked += parts[i, 2:3, :]
        return (top, total, picked)

    for i, value in enumerate(merge(stat_y, RING)):
        stat_m[mine, i:i + 1, :] = value
    for i, peer in enumerate(others):
        push(stat_m.at[mine], stat_m.at[mine], ksend.at[i], krecv.at[mine], **peer)
    for peer in others:
        slot = 2 * peer["x"] + peer["c"]
        arrived(stat_m.at[slot], krecv.at[slot])
    top, total, picked = merge(stat_m, 8)
    log_ref[...] = picked - top - jnp.log(total)
    middle.finish()
    first.finish()
    distant.finish()
    for copy in sent:
        copy.wait_send()


def finish(attended, tokens, mlp_gain, w_out, final_gain, targets, w_gate, w_up, w_down, w_head, pieces):
    rows, width = tokens.shape
    units = w_gate.shape[1]
    block = (rows, width)
    vocab = pieces.shape[2]
    dma = pltpu.SemaphoreType.DMA
    stats = (8, rows)

    def blocks(n):
        return pltpu.VMEM((n,) + block, BF16)

    return pl.pallas_call(
        finish_kernel,
        in_specs=[vmem()] * 6 + [hbm()] * 5,
        out_specs=[vmem(), vmem()],
        out_shape=[jax.ShapeDtypeStruct(block, BF16), jax.ShapeDtypeStruct((1, rows), F32)],
        scratch_shapes=[pltpu.VMEM(w_gate.shape, BF16), pltpu.VMEM(w_up.shape, BF16),
                        pltpu.VMEM(w_down.shape, BF16),
                        blocks(7), blocks(4), blocks(3), blocks(7), blocks(4), blocks(3), blocks(8),
                        pltpu.VMEM((rows, 8 * width), BF16), pltpu.VMEM((rows, units), BF16),
                        pltpu.VMEM((8 * width, vocab), BF16), pltpu.VMEM((RING, 8) + block, BF16),
                        pltpu.VMEM((rows, vocab), F32),
                        pltpu.VMEM((RING, 1, rows), jnp.int32), pltpu.VMEM((RING,) + stats, F32),
                        pltpu.VMEM((RING,) + stats, F32), pltpu.VMEM((8,) + stats, F32),
                        dma((9,)), dma((7,)), dma((4,)), dma((3,)), dma((7,)), dma((4,)), dma((3,)),
                        dma((7,)), dma((8,)),
                        dma((2, 7)), dma((4, 8)), dma((17,)), dma((3,)), dma((3,)),
                        dma((3,)), dma((4,)), dma((7,)), dma((8,)), dma((3, 3)), dma((3, 3)),
                        pltpu.VMEM((w_head.shape[0], vocab), BF16), dma((2,)), dma((2,))],
        compiler_params=pltpu.CompilerParams(collective_id=2, has_side_effects=True,
                                             vmem_limit_bytes=56 << 20),
        cost_estimate=pl.CostEstimate(flops=60 << 30, bytes_accessed=24 << 20, transcendentals=0),
        name="finish",
    )(attended, tokens, mlp_gain, w_out, final_gain, targets, w_gate, w_up, w_down, w_head, pieces)


def body(tokens, attn_gain, mlp_gain, final_gain, q_gain, k_gain, w_query, w_keyval, w_out, w_gate,
         w_up, w_down, w_head, targets, req_lengths, req_tenant, prefix_piece, prefix_kv):
    queries, own, pieces, slabs = entry(
        req_lengths, tokens, attn_gain[None], q_gain[None], k_gain[None], w_query, w_keyval,
        prefix_kv, w_head)
    attended = attention(req_lengths, req_tenant, prefix_piece, queries, own, pieces)
    share, logprob = finish(attended, tokens, mlp_gain[None], w_out, final_gain[None], targets[None],
                            w_gate, w_up, w_down, w_head, slabs)
    return (share, logprob[0])


def solution(mesh):
    req = ("z", "y")
    mlp = ("x", "c")
    in_specs = (
        P(req, mlp), P(), P(), P(), P(), P(), P(None, mlp), P(None, mlp), P(mlp, None),
        P(None, mlp), P(None, mlp), P(mlp, None), P(req, mlp), P(req), P(req, None), P(req, None),
        P(), P(req, None, mlp),
    )
    out_specs = (P(req, mlp), P(req))
    split = Mesh(mesh.devices.reshape(RING, RING, RING, 2), ("z", "y", "x", "c"))
    return jax.shard_map(body, mesh=split, in_specs=in_specs, out_specs=out_specs, check_vma=False)
```

```python
import functools
import math

import jax
import jax.numpy as jnp
from jax import lax
from jax.experimental import pallas as pl
from jax.experimental.pallas import tpu as pltpu
from jax.sharding import Mesh
from jax.sharding import PartitionSpec as P

TENANTS = 4
PLEN = 4096
BLOCK = 64
EPS = 1e-05
LOG_THETA = math.log(1000000.0)
NEG = -1e30
RING = 4
MESH = pl.DeviceIdType.MESH
F32 = jnp.float32
BF16 = jnp.bfloat16


def dot(a, b):
    return jnp.dot(a, b, preferred_element_type=F32)


def dot_nt(a, b):
    return lax.dot_general(a, b, (((1,), (1,)), ((), ())), preferred_element_type=F32)


def remote(src, dst, send_sem, recv_sem, **device):
    return pltpu.make_async_remote_copy(
        src_ref=src, dst_ref=dst, send_sem=send_sem, recv_sem=recv_sem,
        device_id=device, device_id_type=MESH,
    )


def arrived(ref, sem):
    pltpu.make_async_copy(ref, ref, sem).wait()


def greet(peers):
    barrier = pltpu.get_barrier_semaphore()
    for peer in peers:
        pl.semaphore_signal(barrier, inc=1, device_id=peer, device_id_type=MESH)
    pl.semaphore_wait(barrier, len(peers))


def ring_of(axis, core):
    me = lax.axis_index(axis)
    ahead = lax.rem(me + 1 + 2 * core, RING)
    back = lax.rem(me + 3 + 2 * core, RING)
    far = lax.rem(me + 2, RING)
    return (me, ahead, back, far)


class Gather:
    def __init__(self, slots, send, recv):
        self.slots, self.send, self.recv, self.sent = slots, send, recv, []
        self.core = lax.axis_index("c")
        self.x, self.ahead, self.back, self.far = ring_of("x", self.core)

    def push(self, at, core, src=None, **device):
        slot = 2 * at + core
        copy = remote(self.slots.at[slot] if src is None else src, self.slots.at[slot],
                      self.send.at[len(self.sent)], self.recv.at[slot], **device)
        copy.start()
        self.sent.append(copy)

    def wait(self, at, core):
        slot = 2 * at + core
        arrived(self.slots.at[slot], self.recv.at[slot])

    def open(self, src=None):
        self.push(self.x, self.core, src, x=self.ahead)
        self.push(self.x, self.core, src, x=self.back)
        self.push(self.x, self.core, src, c=1 - self.core)

    def relay(self):
        self.wait(self.back, self.core)
        self.push(self.back, self.core, x=self.ahead)
        self.push(self.back, self.core, c=1 - self.core)
        self.wait(self.ahead, self.core)
        self.push(self.ahead, self.core, c=1 - self.core)

    def last(self):
        self.wait(self.far, self.core)
        self.push(self.far, self.core, c=1 - self.core)

    def close(self):
        self.last()
        self.rest()

    def rest(self):
        for x in (self.x, self.back, self.ahead, self.far):
            self.wait(x, 1 - self.core)

    def finish(self):
        for copy in self.sent:
            copy.wait_send()


def scatter_sum(partial, stage, paired, inbox, send, pair_sem, in_sem):
    core = lax.axis_index("c")
    x, ahead, back, far = ring_of("x", core)
    sent = []

    def push(value, dst, recv, **device):
        index = len(sent)
        stage[index] = value.astype(BF16)
        copy = remote(stage.at[index], dst, send.at[index], recv, **device)
        copy.start()
        sent.append(copy)

    def chip(to):
        mine = partial(2 * to + core)
        arrived(paired.at[to], pair_sem.at[to])
        return mine + paired[to].astype(F32)

    for to in (far, back, ahead, x):
        push(partial(2 * to + 1 - core), paired.at[to], pair_sem.at[to], c=1 - core)
    push(chip(far), inbox.at[2], in_sem.at[2], x=ahead)
    push(chip(back), inbox.at[1], in_sem.at[1], x=back)
    value = chip(ahead)
    arrived(inbox.at[2], in_sem.at[2])
    push(value + inbox[2].astype(F32), inbox.at[0], in_sem.at[0], x=ahead)
    value = chip(x)
    for slot in (1, 0):
        arrived(inbox.at[slot], in_sem.at[slot])
        value += inbox[slot].astype(F32)
    for copy in sent:
        copy.wait_send()
    return value


def normalise(blocks, gain_ref, normed):
    count, rows, width = blocks.shape
    square = jnp.zeros((rows, 1), F32)
    for m in range(count):
        value = blocks[m].astype(F32)
        square += jnp.sum(value * value, axis=1, keepdims=True)
    factor = lax.rsqrt(square / (count * width) + EPS)
    for m in range(count):
        columns = slice(m * width, (m + 1) * width)
        normed[:, columns] = (blocks[m].astype(F32) * factor * gain_ref[:, columns]).astype(BF16)


def x_peers():
    core = lax.axis_index("c")
    _, ahead, back, _ = ring_of("x", core)
    return [dict(x=ahead), dict(x=back), dict(c=1 - core)]


def entry_kernel(requests, scale, length_ref, tok_ref, gain_ref, qgain_ref, kgain_ref, wq_ref,
                 wkv_ref, prefix_ref, head_ref, q_out, own_out, pieces, head_out, stream,
                 normed, send, recv, psend, precv, wsend, wrecv, local_sem):
    core = lax.axis_index("c")
    rows = tok_ref.shape[0]
    size = qgain_ref.shape[1]
    half = prefix_ref.shape[1] // 2
    y, y_ahead, y_back, y_far = ring_of("y", core)
    z, z_ahead, z_back, z_far = ring_of("z", core)
    greet(x_peers() + [dict(y=y_ahead), dict(y=y_back), dict(z=z_ahead), dict(z=z_back)])

    sent = []

    def view(part, pz, py):
        return pieces.at[pz * RING + py, pl.ds(part * half, half)]

    def push(part, pz, py, src=None, **device):
        slot = pz * RING + py
        copy = remote(view(part, pz, py) if src is None else src, view(part, pz, py),
                      psend.at[len(sent)], precv.at[part, slot], **device)
        copy.start()
        sent.append(copy)

    def wait(part, pz, py):
        arrived(view(part, pz, py), precv.at[part, pz * RING + py])

    first = [prefix_ref.at[0, pl.ds(part * half, half)] for part in range(2)]
    gather = Gather(stream, send, recv)
    gather.open(tok_ref)
    push(0, z, y, first[0], y=y_ahead)
    push(0, z, y, first[0], y=y_back)
    push(1, z, y, first[1], z=z_ahead)
    push(1, z, y, first[1], z=z_back)
    push(0, z, y, first[0], z=z_ahead)
    push(0, z, y, first[0], z=z_back)
    push(1, z, y, first[1], y=y_ahead)
    push(1, z, y, first[1], y=y_back)

    given = []
    part_words = head_out.shape[2]

    def words(index):
        return head_ref.at[:, pl.ds(pl.multiple_of(index * part_words, part_words), part_words)]

    def piece(pz, py):
        return head_out.at[pz * RING + py]

    def give(index, src, dst, **device):
        copy = remote(src, dst, wsend.at[index], wrecv.at[index], **device)
        copy.start()
        given.append(copy)

    keep = [pltpu.make_async_copy(prefix_ref.at[0], pieces.at[z * RING + y], local_sem.at[0]),
            pltpu.make_async_copy(tok_ref, stream.at[2 * gather.x + core], local_sem.at[1])]
    for copy in keep:
        copy.start()

    wait(0, z, y_back)
    push(0, z, y_back, y=y_ahead)
    push(0, z, y_back, z=z_ahead)
    push(0, z, y_back, z=z_back)
    wait(1, z_back, y)
    push(1, z_back, y, z=z_ahead)
    push(1, z_back, y, y=y_ahead)
    push(1, z_back, y, y=y_back)
    wait(0, z, y_ahead)
    push(0, z, y_ahead, z=z_ahead)
    push(0, z, y_ahead, z=z_back)
    wait(1, z_ahead, y)
    push(1, z_ahead, y, y=y_ahead)
    push(1, z_ahead, y, y=y_back)
    gather.relay()
    wait(0, z, y_far)
    push(0, z, y_far, z=z_ahead)
    push(0, z, y_far, z=z_back)
    wait(1, z_far, y)
    push(1, z_far, y, y=y_ahead)
    push(1, z_far, y, y=y_back)
    give(2, words(y), piece(z, y), z=z_ahead)
    give(3, words(y), piece(z, y), z=z_back)
    give(0, words(y_ahead), piece(z, y), y=y_ahead)
    give(1, words(y_back), piece(z, y), y=y_back)

    row = lax.broadcasted_iota(jnp.int32, (rows, 1), 0)
    offset = row
    end = 0
    for r in range(requests):
        end = end + length_ref[0, r]
        offset = offset - jnp.where(row >= end, length_ref[0, r], 0)
    lane = lax.broadcasted_iota(jnp.int32, (1, size), 1)
    freq = jnp.exp((lane & (size // 2 - 1)).astype(F32) * (-2.0 * LOG_THETA / size))
    angle = (PLEN + offset).astype(F32) * freq
    cosine, sine = jnp.cos(angle), jnp.sin(angle)

    def turned(value, gain):
        value = value * lax.rsqrt(jnp.mean(value * value, axis=1, keepdims=True) + EPS) * gain
        other = jnp.concatenate([-value[:, size // 2:], value[:, : size // 2]], axis=1)
        return (value * cosine + other * sine).astype(BF16)

    keep[1].wait()
    gather.close()
    normalise(stream, gain_ref, normed)

    far_z = [(py, z_back, z_ahead) for py in (y, y_far)] + [(py, z_ahead, z_back) for py in (y_back, y_ahead)]
    far_y = [(pz, y_back, y_ahead) for pz in (z, z_far)] + [(pz, y_ahead, y_back) for pz in (z_back, z_ahead)]
    order = (0, 2, 3, 1)
    arrived(piece(z_back, y), wrecv.at[2])
    give(4, piece(z_back, y), piece(z_back, y), z=z_ahead)
    for i in order:
        py, come, go = far_z[i]
        wait(0, come, py)
        push(0, come, py, z=go)
        pz, come, go = far_y[i]
        wait(1, pz, come)
        push(1, pz, come, y=go)

    query = dot(normed[...], wq_ref[...])
    keyval = dot(normed[...], wkv_ref[...])
    heads = query.shape[1] // size
    zero = jnp.zeros((rows, size), BF16)
    for h in range(heads):
        value = turned(query[:, h * size:(h + 1) * size], qgain_ref[...])
        value = jnp.concatenate([value * jnp.asarray(scale, BF16), zero], axis=1)
        for i in range(rows // BLOCK):
            q_out[i, h * BLOCK:(h + 1) * BLOCK, :] = value[i * BLOCK:(i + 1) * BLOCK]
    own_out[...] = jnp.concatenate(
        [turned(keyval[:, :size], kgain_ref[...]), keyval[:, size:].astype(BF16)], axis=1
    )

    for py, come, go in far_z:
        wait(0, go, py)
    for pz, come, go in far_y:
        wait(1, pz, go)
    for py, come, go in far_z:
        wait(0, z_far, py)
    for pz, come, go in far_y:
        wait(1, pz, y_far)
    arrived(piece(z, y_back), wrecv.at[0])
    arrived(piece(z, y_ahead), wrecv.at[1])
    arrived(piece(z_ahead, y), wrecv.at[3])
    arrived(piece(z_far, y), wrecv.at[4])
    keep[0].wait()
    gather.finish()
    for copy in sent + given:
        copy.wait_send()


def vmem():
    return pl.BlockSpec(memory_space=pltpu.VMEM)


def hbm():
    return pl.BlockSpec(memory_space=pl.ANY)


def smem():
    return pl.BlockSpec(memory_space=pltpu.SMEM)


def entry(lengths, tokens, attn_gain, q_gain, k_gain, w_query, w_keyval, prefix_kv, w_head):
    rows, width = tokens.shape
    size = q_gain.shape[1]
    heads = w_query.shape[1] // size
    count = RING * RING
    quarter = (w_head.shape[0], w_head.shape[1] // RING)
    return pl.pallas_call(
        functools.partial(entry_kernel, lengths.shape[1], size ** (-0.5)),
        in_specs=[smem()] + [vmem()] * 7 + [hbm()],
        out_specs=[vmem(), vmem(), hbm(), hbm()],
        out_shape=[jax.ShapeDtypeStruct((rows // BLOCK, heads * BLOCK, 2 * size), BF16),
                   jax.ShapeDtypeStruct((rows, 2 * size), BF16),
                   jax.ShapeDtypeStruct((count,) + prefix_kv.shape[1:], BF16),
                   jax.ShapeDtypeStruct((count,) + quarter, BF16)],
        scratch_shapes=[pltpu.VMEM((8, rows, width), BF16), pltpu.VMEM((rows, 8 * width), BF16),
                        pltpu.SemaphoreType.DMA((7,)), pltpu.SemaphoreType.DMA((8,)),
                        pltpu.SemaphoreType.DMA((30,)), pltpu.SemaphoreType.DMA((2, count)),
                        pltpu.SemaphoreType.DMA((5,)), pltpu.SemaphoreType.DMA((5,)),
                        pltpu.SemaphoreType.DMA((2,))],
        compiler_params=pltpu.CompilerParams(collective_id=1, has_side_effects=True),
        cost_estimate=pl.CostEstimate(flops=30 << 30, bytes_accessed=8 << 20, transcendentals=0),
        name="entry",
    )(lengths, tokens, attn_gain, q_gain, k_gain, w_query, w_keyval, prefix_kv, w_head)


def attention_kernel(requests, split, length_ref, tenant_ref, piece_ref,
                     q_ref, own_ref, kv_ref, out_ref, best_ref, total_ref, accum_ref, slot_ref):
    block = pl.program_id(0)
    queries = q_ref[0]
    count = queries.shape[0]
    rows = own_ref.shape[0]
    size = own_ref.shape[1] // 2
    for j in range(kv_ref.shape[0]):
        slot_ref[piece_ref[j]] = j
    row = (lax.broadcasted_iota(jnp.int32, (count, 1), 0) & (BLOCK - 1)) + block * BLOCK
    col = lax.broadcasted_iota(jnp.int32, (1, rows), 1)
    row_request = jnp.zeros((count, 1), jnp.int32)
    col_request = jnp.zeros((1, rows), jnp.int32)
    ends = []
    for r in range(requests):
        ends.append(length_ref[0, r] + (ends[-1] if ends else 0))
        row_request += (row >= ends[r]).astype(jnp.int32)
        col_request += (col >= ends[r]).astype(jnp.int32)
    seen = (row_request == col_request) & (col <= row)
    own = own_ref[...]
    scores = jnp.where(seen, dot_nt(queries, own), NEG)
    best = jnp.max(scores, axis=1, keepdims=True)
    weights = jnp.where(seen, jnp.exp(scores - best), 0.0)
    best_ref[...] = best
    total_ref[...] = jnp.sum(weights, axis=1, keepdims=True)
    accum_ref[...] = dot(weights.astype(BF16), own)
    for r in range(requests):
        begin = ends[r] - length_ref[0, r]

        @pl.when((ends[r] > block * BLOCK) & (begin < block * BLOCK + BLOCK))
        def _():
            inside = row_request == r
            tenant = tenant_ref[0, r]

            old = best_ref[...]
            keyvals = [kv_ref[slot_ref[tenant * split + index]] for index in range(split)]
            parts = [dot_nt(queries, keyval) for keyval in keyvals]
            new = old
            for part in parts:
                new = jnp.maximum(new, jnp.max(part, axis=1, keepdims=True))
            new = jnp.where(inside, new, old)
            keep = jnp.exp(old - new)
            shift = jnp.where(inside, new, -NEG)
            total = total_ref[...] * keep
            accum = accum_ref[...] * keep
            for part, keyval in zip(parts, keyvals):
                piece_weights = jnp.exp(part - shift)
                total += jnp.sum(piece_weights, axis=1, keepdims=True)
                accum += dot(piece_weights.astype(BF16), keyval)
            best_ref[...], total_ref[...], accum_ref[...] = new, total, accum

    out = accum_ref[...] / total_ref[...]
    heads = [out[h * BLOCK:(h + 1) * BLOCK, size:] for h in range(count // BLOCK)]
    out_ref[...] = jnp.concatenate(heads, axis=1).astype(BF16)


def attention(lengths, tenants, prefix_piece, queries, own, pieces):
    blocks, count, width = queries.shape
    rows = own.shape[0]
    columns = count // BLOCK * width // 2
    return pl.pallas_call(
        functools.partial(attention_kernel, lengths.shape[1], pieces.shape[0] // TENANTS),
        grid=(blocks,),
        in_specs=[smem(), smem(), smem(),
                  pl.BlockSpec((1, count, width), lambda i: (i, 0, 0)),
                  pl.BlockSpec(own.shape, lambda i: (0, 0)),
                  pl.BlockSpec(pieces.shape, lambda i: (0, 0, 0), pipeline_mode=pl.Buffered(1))],
        out_specs=pl.BlockSpec((BLOCK, columns), lambda i: (i, 0)),
        out_shape=jax.ShapeDtypeStruct((rows, columns), BF16),
        scratch_shapes=[pltpu.VMEM((count, 1), F32), pltpu.VMEM((count, 1), F32),
                        pltpu.VMEM((count, width), F32), pltpu.SMEM((pieces.shape[0],), jnp.int32)],
        cost_estimate=pl.CostEstimate(flops=24 << 30, bytes_accessed=5 << 20, transcendentals=0),
        name="attention",
    )(lengths, tenants, prefix_piece, queries, own, pieces)


def finish_kernel(att_ref, tok_ref, gain_ref, wo_ref, last_gain_ref, target_ref, wg_hbm, wu_hbm, wd_hbm,
                  head_hbm, pieces_hbm, out_ref, log_ref,
                  wg, wu, wd, stage, paired, inbox, stage2, paired2, inbox2, mid, normed, inner,
                  weight, hidden, logits, wanted, stat, stat_y, stat_m,
                  load, send, pair_sem, in_sem, send2, pair_sem2, in_sem2, msend, mrecv,
                  gsend, grecv, ysend, tsend, trecv, ssend, srecv, ksend, krecv,
                  zsend, zrecv, passing, wsend, wrecv):
    core = lax.axis_index("c")
    rows, width = tok_ref.shape
    depth, vocab = pieces_hbm.shape[1:]
    x, x_ahead, x_back, x_far = ring_of("x", core)
    y, y_ahead, y_back, y_far = ring_of("y", core)
    z, z_ahead, z_back, z_far = ring_of("z", core)
    mine = 2 * x + core
    sent = []

    def push(src, dst, send_sem, recv_sem, **device):
        copy = remote(src, dst, send_sem, recv_sem, **device)
        copy.start()
        sent.append(copy)

    def columns(index, count):
        return pl.ds(pl.multiple_of(index * count, count), count)

    def place(pz, py):
        return weight.at[columns(pz * RING + py, depth)]

    loads = []

    def fetch(src, dst):
        copy = pltpu.make_async_copy(src, dst, load.at[len(loads)])
        copy.start()
        loads.append(copy)

    fetch(wg_hbm, wg)
    fetch(wu_hbm, wu)
    fetch(wd_hbm, wd)
    fetch(head_hbm.at[:, columns(y, vocab)], place(z, y))
    for pz in (z_ahead, z_back, z_far):
        fetch(pieces_hbm.at[pz * RING + y], place(pz, y))
    rest = (y_back, y_ahead, y_far)
    for py in rest[:2]:
        fetch(pieces_hbm.at[z * RING + py], place(z, py))
    others = [dict(x=lax.rem(x + i // 2, RING), c=lax.rem(core + i % 2, 2)) for i in range(1, 8)]
    greet([dict(y=y_ahead), dict(y=y_back), dict(y=y_far), dict(z=z_ahead), dict(z=z_back)] + others)

    def head_open(i, source):
        to = place(z, rest[i])
        push(source, to, zsend.at[i, 0], zrecv.at[i, 0], z=z_ahead)
        push(source, to, zsend.at[i, 1], zrecv.at[i, 1], z=z_back)

    push(head_hbm.at[:, columns(y_far, vocab)], passing, wsend.at[0], wrecv.at[0], y=y_ahead)
    for i in range(2):
        head_open(i, pieces_hbm.at[z * RING + rest[i]])
    for i, to in enumerate((y_ahead, y_back, y_far)):
        push(target_ref, wanted.at[y], tsend.at[i], trecv.at[i], y=to)
    wanted[y] = target_ref[...]

    def head_relay(i):
        arrived(place(z_back, rest[i]), zrecv.at[i, 0])
        push(place(z_back, rest[i]), place(z_back, rest[i]), zsend.at[i, 2], zrecv.at[i, 2], z=z_ahead)

    att = att_ref[...]
    value = scatter_sum(lambda d: dot(att, wo_ref[:, columns(d, width)]),
                        stage, paired, inbox, send, pair_sem, in_sem)
    middle = Gather(mid, msend, mrecv)
    mid[mine] = (tok_ref[...].astype(F32) + value).astype(BF16)
    middle.open()
    arrived(passing, wrecv.at[0])
    push(passing, place(z, y_back), wsend.at[1], wrecv.at[1], y=y_ahead)
    middle.relay()
    middle.close()
    normalise(mid, gain_ref, normed)
    arrived(place(z, y_far), wrecv.at[1])
    head_open(2, place(z, y_far))
    head_relay(0)
    loads[0].wait()
    loads[1].wait()
    for t in range(inner.shape[1] // width):
        tile = slice(t * width, (t + 1) * width)
        gate = dot(normed[...], wg[:, tile])
        upper = dot(normed[...], wu[:, tile])
        inner[:, tile] = (gate / (1.0 + jnp.exp(-gate)) * upper).astype(BF16)
    loads[2].wait()
    head_relay(1)
    value = scatter_sum(lambda d: dot(inner[...], wd[:, columns(d, width)]),
                        stage2, paired2, inbox2, send2, pair_sem2, in_sem2)
    share = (mid[mine].astype(F32) + value).astype(BF16)
    out_ref[...] = share
    hidden[y, mine] = share

    first = Gather(hidden.at[y], gsend.at[0], grecv.at[y])
    distant = Gather(hidden.at[y_far], gsend.at[1], grecv.at[y_far])
    y_down, y_up = lax.rem(y + 3, RING), lax.rem(y + 1, RING)
    moved = []

    def hand(group, slot, **device):
        push(hidden.at[group, slot], hidden.at[group, slot], ysend.at[len(moved)], grecv.at[group, slot],
             **device)
        moved.append(slot)

    def spread(to):
        hand(y, 2 * to + core, y=y_ahead)
        hand(y, 2 * to + core, y=y_back)

    def collect(group, to):
        arrived(hidden.at[group, 2 * to + core], grecv.at[group, 2 * to + core])
        hand(group, 2 * to + core, c=1 - core)

    first.open()
    spread(x)
    head_relay(2)
    first.relay()
    spread(x_back)
    spread(x_ahead)
    collect(y_back, x)
    hand(y_back, mine, y=y_ahead)
    collect(y_ahead, x)
    first.last()
    spread(x_far)
    arrived(hidden.at[y_far, mine], grecv.at[y_far, mine])
    distant.open()
    first.rest()
    for i, group in enumerate((y_back, y_ahead, y_far)):
        arrived(wanted.at[group], trecv.at[i])
    for copy in loads[3:]:
        copy.wait()
    for i, py in enumerate(rest):
        arrived(place(z_ahead, py), zrecv.at[i, 1])
        arrived(place(z_far, py), zrecv.at[i, 2])

    tile = 512
    eye = (lax.broadcasted_iota(jnp.int32, (rows, rows), 0)
           == lax.broadcasted_iota(jnp.int32, (rows, rows), 1))
    start = (mine * RING + y) * vocab
    column = lax.broadcasted_iota(jnp.int32, (1, vocab), 1)

    def to_row(value):
        return jnp.sum(jnp.where(eye, value, 0.0), axis=0, keepdims=True)

    for index, group in enumerate((y, y_down, y_up, y_far)):
        if index in (1, 2):
            for to in range(RING):
                slot = 2 * to + 1 - core
                arrived(hidden.at[group, slot], grecv.at[group, slot])
        if index == 3:
            distant.rest()
        normalise(hidden.at[group], last_gain_ref, normed)
        if index == 0:
            for to in (x_back, x_ahead):
                collect(y_back, to)
                collect(y_ahead, to)
            distant.relay()
        for t in range(vocab // tile):
            logits[:, t * tile:(t + 1) * tile] = dot(normed[...], weight[:, t * tile:(t + 1) * tile])
        if index == 0:
            collect(y_back, x_far)
            collect(y_ahead, x_far)
            distant.last()
        value = logits[...]
        top = jnp.max(value, axis=1, keepdims=True)
        total = jnp.sum(jnp.exp(value - top), axis=1, keepdims=True)
        target = jnp.sum(jnp.where(eye, wanted[group], 0), axis=1, keepdims=True)
        picked = jnp.sum(jnp.where(target - start == column, value, 0.0), axis=1, keepdims=True)
        stat[group, 0:1, :] = to_row(top)
        stat[group, 1:2, :] = to_row(total)
        stat[group, 2:3, :] = to_row(picked)
        if index:
            push(stat.at[group], stat_y.at[y], ssend.at[index - 1], srecv.at[y], y=group)

    stat_y[y] = stat[y]
    for group in (y_back, y_ahead, y_far):
        arrived(stat_y.at[group], srecv.at[group])

    def merge(parts, count):
        top = parts[0, 0:1, :]
        for i in range(1, count):
            top = jnp.maximum(top, parts[i, 0:1, :])
        total = jnp.zeros_like(top)
        picked = jnp.zeros_like(top)
        for i in range(count):
            total += parts[i, 1:2, :] * jnp.exp(parts[i, 0:1, :] - top)
            picked += parts[i, 2:3, :]
        return (top, total, picked)

    for i, value in enumerate(merge(stat_y, RING)):
        stat_m[mine, i:i + 1, :] = value
    for i, peer in enumerate(others):
        push(stat_m.at[mine], stat_m.at[mine], ksend.at[i], krecv.at[mine], **peer)
    for peer in others:
        slot = 2 * peer["x"] + peer["c"]
        arrived(stat_m.at[slot], krecv.at[slot])
    top, total, picked = merge(stat_m, 8)
    log_ref[...] = picked - top - jnp.log(total)
    middle.finish()
    first.finish()
    distant.finish()
    for copy in sent:
        copy.wait_send()


def finish(attended, tokens, mlp_gain, w_out, final_gain, targets, w_gate, w_up, w_down, w_head, pieces):
    rows, width = tokens.shape
    units = w_gate.shape[1]
    block = (rows, width)
    vocab = pieces.shape[2]
    dma = pltpu.SemaphoreType.DMA
    stats = (8, rows)

    def blocks(n):
        return pltpu.VMEM((n,) + block, BF16)

    return pl.pallas_call(
        finish_kernel,
        in_specs=[vmem()] * 6 + [hbm()] * 5,
        out_specs=[vmem(), vmem()],
        out_shape=[jax.ShapeDtypeStruct(block, BF16), jax.ShapeDtypeStruct((1, rows), F32)],
        scratch_shapes=[pltpu.VMEM(w_gate.shape, BF16), pltpu.VMEM(w_up.shape, BF16),
                        pltpu.VMEM(w_down.shape, BF16),
                        blocks(7), blocks(4), blocks(3), blocks(7), blocks(4), blocks(3), blocks(8),
                        pltpu.VMEM((rows, 8 * width), BF16), pltpu.VMEM((rows, units), BF16),
                        pltpu.VMEM((8 * width, vocab), BF16), pltpu.VMEM((RING, 8) + block, BF16),
                        pltpu.VMEM((rows, vocab), F32),
                        pltpu.VMEM((RING, 1, rows), jnp.int32), pltpu.VMEM((RING,) + stats, F32),
                        pltpu.VMEM((RING,) + stats, F32), pltpu.VMEM((8,) + stats, F32),
                        dma((9,)), dma((7,)), dma((4,)), dma((3,)), dma((7,)), dma((4,)), dma((3,)),
                        dma((7,)), dma((8,)),
                        dma((2, 7)), dma((4, 8)), dma((17,)), dma((3,)), dma((3,)),
                        dma((3,)), dma((4,)), dma((7,)), dma((8,)), dma((3, 3)), dma((3, 3)),
                        pltpu.VMEM((w_head.shape[0], vocab), BF16), dma((2,)), dma((2,))],
        compiler_params=pltpu.CompilerParams(collective_id=2, has_side_effects=True,
                                             vmem_limit_bytes=56 << 20),
        cost_estimate=pl.CostEstimate(flops=60 << 30, bytes_accessed=24 << 20, transcendentals=0),
        name="finish",
    )(attended, tokens, mlp_gain, w_out, final_gain, targets, w_gate, w_up, w_down, w_head, pieces)


def results_kernel(share_ref, log_ref, share_out, log_out):
    share_out[...] = share_ref[...]
    log_out[...] = log_ref[0]


def results(share, logprob):
    return pl.pallas_call(
        results_kernel,
        in_specs=[vmem()] * 2,
        out_specs=[vmem()] * 2,
        out_shape=[jax.ShapeDtypeStruct(share.shape, BF16), jax.ShapeDtypeStruct(logprob.shape[1:], F32)],
        name="results",
    )(share, logprob)


def body(tokens, attn_gain, mlp_gain, final_gain, q_gain, k_gain, w_query, w_keyval, w_out, w_gate,
         w_up, w_down, w_head, targets, req_lengths, req_tenant, prefix_piece, prefix_kv):
    queries, own, pieces, slabs = entry(
        req_lengths, tokens, attn_gain[None], q_gain[None], k_gain[None], w_query, w_keyval,
        prefix_kv, w_head)
    attended = attention(req_lengths, req_tenant, prefix_piece, queries, own, pieces)
    share, logprob = finish(attended, tokens, mlp_gain[None], w_out, final_gain[None], targets[None],
                            w_gate, w_up, w_down, w_head, slabs)
    return tuple(results(share, logprob))


def solution(mesh):
    req = ("z", "y")
    mlp = ("x", "c")
    in_specs = (
        P(req, mlp), P(), P(), P(), P(), P(), P(None, mlp), P(None, mlp), P(mlp, None),
        P(None, mlp), P(None, mlp), P(mlp, None), P(req, mlp), P(req), P(req, None), P(req, None),
        P(), P(req, None, mlp),
    )
    out_specs = (P(req, mlp), P(req))
    split = Mesh(mesh.devices.reshape(RING, RING, RING, 2), ("z", "y", "x", "c"))
    return jax.shard_map(body, mesh=split, in_specs=in_specs, out_specs=out_specs, check_vma=False)
```

```python
import functools
import math

import jax
import jax.numpy as jnp
from jax import lax
from jax.experimental import pallas as pl
from jax.experimental.pallas import tpu as pltpu
from jax.sharding import Mesh
from jax.sharding import PartitionSpec as P

TENANTS = 4
PLEN = 4096
BLOCK = 64
EPS = 1e-05
LOG_THETA = math.log(1000000.0)
NEG = -1e30
RING = 4
MESH = pl.DeviceIdType.MESH
F32 = jnp.float32
BF16 = jnp.bfloat16


def dot(a, b):
    return jnp.dot(a, b, preferred_element_type=F32)


def dot_nt(a, b):
    return lax.dot_general(a, b, (((1,), (1,)), ((), ())), preferred_element_type=F32)


def remote(src, dst, send_sem, recv_sem, **device):
    return pltpu.make_async_remote_copy(
        src_ref=src, dst_ref=dst, send_sem=send_sem, recv_sem=recv_sem,
        device_id=device, device_id_type=MESH,
    )


def arrived(ref, sem):
    pltpu.make_async_copy(ref, ref, sem).wait()


def greet(peers):
    barrier = pltpu.get_barrier_semaphore()
    for peer in peers:
        pl.semaphore_signal(barrier, inc=1, device_id=peer, device_id_type=MESH)
    pl.semaphore_wait(barrier, len(peers))


def ring_of(axis, core):
    me = lax.axis_index(axis)
    ahead = lax.rem(me + 1 + 2 * core, RING)
    back = lax.rem(me + 3 + 2 * core, RING)
    far = lax.rem(me + 2, RING)
    return (me, ahead, back, far)


class Gather:
    def __init__(self, slots, send, recv):
        self.slots, self.send, self.recv, self.sent = slots, send, recv, []
        self.core = lax.axis_index("c")
        self.x, self.ahead, self.back, self.far = ring_of("x", self.core)

    def push(self, at, core, src=None, **device):
        slot = 2 * at + core
        copy = remote(self.slots.at[slot] if src is None else src, self.slots.at[slot],
                      self.send.at[len(self.sent)], self.recv.at[slot], **device)
        copy.start()
        self.sent.append(copy)

    def wait(self, at, core):
        slot = 2 * at + core
        arrived(self.slots.at[slot], self.recv.at[slot])

    def open(self, src=None):
        self.push(self.x, self.core, src, x=self.ahead)
        self.push(self.x, self.core, src, x=self.back)
        self.push(self.x, self.core, src, c=1 - self.core)

    def relay(self):
        self.wait(self.back, self.core)
        self.push(self.back, self.core, x=self.ahead)
        self.push(self.back, self.core, c=1 - self.core)
        self.wait(self.ahead, self.core)
        self.push(self.ahead, self.core, c=1 - self.core)

    def last(self):
        self.wait(self.far, self.core)
        self.push(self.far, self.core, c=1 - self.core)

    def close(self):
        self.last()
        self.rest()

    def rest(self):
        for x in (self.x, self.back, self.ahead, self.far):
            self.wait(x, 1 - self.core)

    def finish(self):
        for copy in self.sent:
            copy.wait_send()


def scatter_sum(partial, stage, paired, inbox, send, pair_sem, in_sem):
    core = lax.axis_index("c")
    x, ahead, back, far = ring_of("x", core)
    sent = []

    def push(value, dst, recv, **device):
        index = len(sent)
        stage[index] = value.astype(BF16)
        copy = remote(stage.at[index], dst, send.at[index], recv, **device)
        copy.start()
        sent.append(copy)

    def chip(to):
        mine = partial(2 * to + core)
        arrived(paired.at[to], pair_sem.at[to])
        return mine + paired[to].astype(F32)

    for to in (far, back, ahead, x):
        push(partial(2 * to + 1 - core), paired.at[to], pair_sem.at[to], c=1 - core)
    push(chip(far), inbox.at[2], in_sem.at[2], x=ahead)
    push(chip(back), inbox.at[1], in_sem.at[1], x=back)
    value = chip(ahead)
    arrived(inbox.at[2], in_sem.at[2])
    push(value + inbox[2].astype(F32), inbox.at[0], in_sem.at[0], x=ahead)
    value = chip(x)
    for slot in (1, 0):
        arrived(inbox.at[slot], in_sem.at[slot])
        value += inbox[slot].astype(F32)
    for copy in sent:
        copy.wait_send()
    return value


def normalise(blocks, gain_ref, normed):
    count, rows, width = blocks.shape
    square = jnp.zeros((rows, 1), F32)
    for m in range(count):
        value = blocks[m].astype(F32)
        square += jnp.sum(value * value, axis=1, keepdims=True)
    factor = lax.rsqrt(square / (count * width) + EPS)
    for m in range(count):
        columns = slice(m * width, (m + 1) * width)
        normed[:, columns] = (blocks[m].astype(F32) * factor * gain_ref[:, columns]).astype(BF16)


def x_peers():
    core = lax.axis_index("c")
    _, ahead, back, _ = ring_of("x", core)
    return [dict(x=ahead), dict(x=back), dict(c=1 - core)]


def entry_kernel(requests, scale, length_ref, tok_ref, gain_ref, qgain_ref, kgain_ref, wq_ref,
                 wkv_ref, prefix_ref, head_ref, q_out, own_out, pieces, head_out, stream,
                 normed, send, recv, psend, precv, wsend, wrecv, local_sem):
    core = lax.axis_index("c")
    rows = tok_ref.shape[0]
    size = qgain_ref.shape[1]
    cut = prefix_ref.shape[1] * 3 // 8
    spans = (pl.ds(0, cut), pl.ds(cut, prefix_ref.shape[1] - cut))
    y, y_ahead, y_back, y_far = ring_of("y", core)
    z, z_ahead, z_back, z_far = ring_of("z", core)
    greet(x_peers() + [dict(y=y_ahead), dict(y=y_back), dict(z=z_ahead), dict(z=z_back)])

    sent = []

    def view(part, pz, py):
        return pieces.at[pz * RING + py, spans[part]]

    def push(part, pz, py, src=None, **device):
        slot = pz * RING + py
        copy = remote(view(part, pz, py) if src is None else src, view(part, pz, py),
                      psend.at[len(sent)], precv.at[part, slot], **device)
        copy.start()
        sent.append(copy)

    def wait(part, pz, py):
        arrived(view(part, pz, py), precv.at[part, pz * RING + py])

    first = [prefix_ref.at[0, spans[part]] for part in range(2)]
    gather = Gather(stream, send, recv)
    gather.open(tok_ref)
    push(0, z, y, first[0], y=y_ahead)
    push(0, z, y, first[0], y=y_back)
    push(1, z, y, first[1], z=z_ahead)
    push(1, z, y, first[1], z=z_back)
    push(0, z, y, first[0], z=z_ahead)
    push(0, z, y, first[0], z=z_back)
    push(1, z, y, first[1], y=y_ahead)
    push(1, z, y, first[1], y=y_back)

    given = []
    part_words = head_out.shape[2]

    def words(index):
        return head_ref.at[:, pl.ds(pl.multiple_of(index * part_words, part_words), part_words)]

    def piece(pz, py):
        return head_out.at[pz * RING + py]

    def give(index, src, dst, **device):
        copy = remote(src, dst, wsend.at[index], wrecv.at[index], **device)
        copy.start()
        given.append(copy)

    keep = [pltpu.make_async_copy(prefix_ref.at[0], pieces.at[z * RING + y], local_sem.at[0]),
            pltpu.make_async_copy(tok_ref, stream.at[2 * gather.x + core], local_sem.at[1])]
    for copy in keep:
        copy.start()

    wait(0, z, y_back)
    push(0, z, y_back, y=y_ahead)
    push(0, z, y_back, z=z_ahead)
    push(0, z, y_back, z=z_back)
    wait(1, z_back, y)
    push(1, z_back, y, z=z_ahead)
    push(1, z_back, y, y=y_ahead)
    push(1, z_back, y, y=y_back)
    wait(0, z, y_ahead)
    push(0, z, y_ahead, z=z_ahead)
    push(0, z, y_ahead, z=z_back)
    wait(1, z_ahead, y)
    push(1, z_ahead, y, y=y_ahead)
    push(1, z_ahead, y, y=y_back)
    gather.relay()
    wait(0, z, y_far)
    push(0, z, y_far, z=z_ahead)
    push(0, z, y_far, z=z_back)
    wait(1, z_far, y)
    push(1, z_far, y, y=y_ahead)
    push(1, z_far, y, y=y_back)
    give(2, words(y), piece(z, y), z=z_ahead)
    give(3, words(y), piece(z, y), z=z_back)
    give(0, words(y_ahead), piece(z, y), y=y_ahead)
    give(1, words(y_back), piece(z, y), y=y_back)

    row = lax.broadcasted_iota(jnp.int32, (rows, 1), 0)
    offset = row
    end = 0
    for r in range(requests):
        end = end + length_ref[0, r]
        offset = offset - jnp.where(row >= end, length_ref[0, r], 0)
    lane = lax.broadcasted_iota(jnp.int32, (1, size), 1)
    freq = jnp.exp((lane & (size // 2 - 1)).astype(F32) * (-2.0 * LOG_THETA / size))
    angle = (PLEN + offset).astype(F32) * freq
    cosine, sine = jnp.cos(angle), jnp.sin(angle)

    def turned(value, gain):
        value = value * lax.rsqrt(jnp.mean(value * value, axis=1, keepdims=True) + EPS) * gain
        other = jnp.concatenate([-value[:, size // 2:], value[:, : size // 2]], axis=1)
        return (value * cosine + other * sine).astype(BF16)

    keep[1].wait()
    gather.close()
    normalise(stream, gain_ref, normed)

    far_z = [(py, z_back, z_ahead) for py in (y, y_far)] + [(py, z_ahead, z_back) for py in (y_back, y_ahead)]
    far_y = [(pz, y_back, y_ahead) for pz in (z, z_far)] + [(pz, y_ahead, y_back) for pz in (z_back, z_ahead)]
    order = (0, 2, 3, 1)
    arrived(piece(z_back, y), wrecv.at[2])
    give(4, piece(z_back, y), piece(z_back, y), z=z_ahead)
    for i in order:
        py, come, go = far_z[i]
        wait(0, come, py)
        push(0, come, py, z=go)
        pz, come, go = far_y[i]
        wait(1, pz, come)
        push(1, pz, come, y=go)

    query = dot(normed[...], wq_ref[...])
    keyval = dot(normed[...], wkv_ref[...])
    heads = query.shape[1] // size
    zero = jnp.zeros((rows, size), BF16)
    for h in range(heads):
        value = turned(query[:, h * size:(h + 1) * size], qgain_ref[...])
        value = jnp.concatenate([value * jnp.asarray(scale, BF16), zero], axis=1)
        for i in range(rows // BLOCK):
            q_out[i, h * BLOCK:(h + 1) * BLOCK, :] = value[i * BLOCK:(i + 1) * BLOCK]
    own_out[...] = jnp.concatenate(
        [turned(keyval[:, :size], kgain_ref[...]), keyval[:, size:].astype(BF16)], axis=1
    )

    for py, come, go in far_z:
        wait(0, go, py)
    for pz, come, go in far_y:
        wait(1, pz, go)
    for py, come, go in far_z:
        wait(0, z_far, py)
    for pz, come, go in far_y:
        wait(1, pz, y_far)
    arrived(piece(z, y_back), wrecv.at[0])
    arrived(piece(z, y_ahead), wrecv.at[1])
    arrived(piece(z_ahead, y), wrecv.at[3])
    arrived(piece(z_far, y), wrecv.at[4])
    keep[0].wait()
    gather.finish()
    for copy in sent + given:
        copy.wait_send()


def vmem():
    return pl.BlockSpec(memory_space=pltpu.VMEM)


def hbm():
    return pl.BlockSpec(memory_space=pl.ANY)


def smem():
    return pl.BlockSpec(memory_space=pltpu.SMEM)


def entry(lengths, tokens, attn_gain, q_gain, k_gain, w_query, w_keyval, prefix_kv, w_head):
    rows, width = tokens.shape
    size = q_gain.shape[1]
    heads = w_query.shape[1] // size
    count = RING * RING
    quarter = (w_head.shape[0], w_head.shape[1] // RING)
    return pl.pallas_call(
        functools.partial(entry_kernel, lengths.shape[1], size ** (-0.5)),
        in_specs=[smem()] + [vmem()] * 7 + [hbm()],
        out_specs=[vmem(), vmem(), hbm(), hbm()],
        out_shape=[jax.ShapeDtypeStruct((rows // BLOCK, heads * BLOCK, 2 * size), BF16),
                   jax.ShapeDtypeStruct((rows, 2 * size), BF16),
                   jax.ShapeDtypeStruct((count,) + prefix_kv.shape[1:], BF16),
                   jax.ShapeDtypeStruct((count,) + quarter, BF16)],
        scratch_shapes=[pltpu.VMEM((8, rows, width), BF16), pltpu.VMEM((rows, 8 * width), BF16),
                        pltpu.SemaphoreType.DMA((7,)), pltpu.SemaphoreType.DMA((8,)),
                        pltpu.SemaphoreType.DMA((30,)), pltpu.SemaphoreType.DMA((2, count)),
                        pltpu.SemaphoreType.DMA((5,)), pltpu.SemaphoreType.DMA((5,)),
                        pltpu.SemaphoreType.DMA((2,))],
        compiler_params=pltpu.CompilerParams(collective_id=1, has_side_effects=True),
        cost_estimate=pl.CostEstimate(flops=30 << 30, bytes_accessed=8 << 20, transcendentals=0),
        name="entry",
    )(lengths, tokens, attn_gain, q_gain, k_gain, w_query, w_keyval, prefix_kv, w_head)


def attention_kernel(requests, split, length_ref, tenant_ref, piece_ref,
                     q_ref, own_ref, kv_ref, out_ref, best_ref, total_ref, accum_ref, slot_ref):
    block = pl.program_id(0)
    queries = q_ref[0]
    count = queries.shape[0]
    rows = own_ref.shape[0]
    size = own_ref.shape[1] // 2
    for j in range(kv_ref.shape[0]):
        slot_ref[piece_ref[j]] = j
    row = (lax.broadcasted_iota(jnp.int32, (count, 1), 0) & (BLOCK - 1)) + block * BLOCK
    col = lax.broadcasted_iota(jnp.int32, (1, rows), 1)
    row_request = jnp.zeros((count, 1), jnp.int32)
    col_request = jnp.zeros((1, rows), jnp.int32)
    ends = []
    for r in range(requests):
        ends.append(length_ref[0, r] + (ends[-1] if ends else 0))
        row_request += (row >= ends[r]).astype(jnp.int32)
        col_request += (col >= ends[r]).astype(jnp.int32)
    seen = (row_request == col_request) & (col <= row)
    own = own_ref[...]
    scores = jnp.where(seen, dot_nt(queries, own), NEG)
    best = jnp.max(scores, axis=1, keepdims=True)
    weights = jnp.where(seen, jnp.exp(scores - best), 0.0)
    best_ref[...] = best
    total_ref[...] = jnp.sum(weights, axis=1, keepdims=True)
    accum_ref[...] = dot(weights.astype(BF16), own)
    for r in range(requests):
        begin = ends[r] - length_ref[0, r]

        @pl.when((ends[r] > block * BLOCK) & (begin < block * BLOCK + BLOCK))
        def _():
            inside = row_request == r
            tenant = tenant_ref[0, r]

            old = best_ref[...]
            keyvals = [kv_ref[slot_ref[tenant * split + index]] for index in range(split)]
            parts = [dot_nt(queries, keyval) for keyval in keyvals]
            new = old
            for part in parts:
                new = jnp.maximum(new, jnp.max(part, axis=1, keepdims=True))
            new = jnp.where(inside, new, old)
            keep = jnp.exp(old - new)
            shift = jnp.where(inside, new, -NEG)
            total = total_ref[...] * keep
            accum = accum_ref[...] * keep
            for part, keyval in zip(parts, keyvals):
                piece_weights = jnp.exp(part - shift)
                total += jnp.sum(piece_weights, axis=1, keepdims=True)
                accum += dot(piece_weights.astype(BF16), keyval)
            best_ref[...], total_ref[...], accum_ref[...] = new, total, accum

    out = accum_ref[...] / total_ref[...]
    heads = [out[h * BLOCK:(h + 1) * BLOCK, size:] for h in range(count // BLOCK)]
    out_ref[...] = jnp.concatenate(heads, axis=1).astype(BF16)


def attention(lengths, tenants, prefix_piece, queries, own, pieces):
    blocks, count, width = queries.shape
    rows = own.shape[0]
    columns = count // BLOCK * width // 2
    return pl.pallas_call(
        functools.partial(attention_kernel, lengths.shape[1], pieces.shape[0] // TENANTS),
        grid=(blocks,),
        in_specs=[smem(), smem(), smem(),
                  pl.BlockSpec((1, count, width), lambda i: (i, 0, 0)),
                  pl.BlockSpec(own.shape, lambda i: (0, 0)),
                  pl.BlockSpec(pieces.shape, lambda i: (0, 0, 0), pipeline_mode=pl.Buffered(1))],
        out_specs=pl.BlockSpec((BLOCK, columns), lambda i: (i, 0)),
        out_shape=jax.ShapeDtypeStruct((rows, columns), BF16),
        scratch_shapes=[pltpu.VMEM((count, 1), F32), pltpu.VMEM((count, 1), F32),
                        pltpu.VMEM((count, width), F32), pltpu.SMEM((pieces.shape[0],), jnp.int32)],
        cost_estimate=pl.CostEstimate(flops=24 << 30, bytes_accessed=5 << 20, transcendentals=0),
        name="attention",
    )(lengths, tenants, prefix_piece, queries, own, pieces)


def finish_kernel(att_ref, tok_ref, gain_ref, wo_ref, last_gain_ref, target_ref, wg_hbm, wu_hbm, wd_hbm,
                  head_hbm, pieces_hbm, out_ref, log_ref,
                  wg, wu, wd, stage, paired, inbox, stage2, paired2, inbox2, mid, normed, inner,
                  weight, hidden, logits, wanted, stat, stat_y, stat_m,
                  load, send, pair_sem, in_sem, send2, pair_sem2, in_sem2, msend, mrecv,
                  gsend, grecv, ysend, tsend, trecv, ssend, srecv, ksend, krecv,
                  zsend, zrecv, passing, wsend, wrecv):
    core = lax.axis_index("c")
    rows, width = tok_ref.shape
    depth, vocab = pieces_hbm.shape[1:]
    x, x_ahead, x_back, x_far = ring_of("x", core)
    y, y_ahead, y_back, y_far = ring_of("y", core)
    z, z_ahead, z_back, z_far = ring_of("z", core)
    mine = 2 * x + core
    sent = []

    def push(src, dst, send_sem, recv_sem, **device):
        copy = remote(src, dst, send_sem, recv_sem, **device)
        copy.start()
        sent.append(copy)

    def columns(index, count):
        return pl.ds(pl.multiple_of(index * count, count), count)

    def place(pz, py):
        return weight.at[columns(pz * RING + py, depth)]

    loads = []

    def fetch(src, dst):
        copy = pltpu.make_async_copy(src, dst, load.at[len(loads)])
        copy.start()
        loads.append(copy)

    fetch(wg_hbm, wg)
    fetch(wu_hbm, wu)
    fetch(wd_hbm, wd)
    fetch(head_hbm.at[:, columns(y, vocab)], place(z, y))
    for pz in (z_ahead, z_back, z_far):
        fetch(pieces_hbm.at[pz * RING + y], place(pz, y))
    rest = (y_back, y_ahead, y_far)
    for py in rest[:2]:
        fetch(pieces_hbm.at[z * RING + py], place(z, py))
    others = [dict(x=lax.rem(x + i // 2, RING), c=lax.rem(core + i % 2, 2)) for i in range(1, 8)]
    greet([dict(y=y_ahead), dict(y=y_back), dict(y=y_far), dict(z=z_ahead), dict(z=z_back)] + others)

    def head_open(i, source):
        to = place(z, rest[i])
        push(source, to, zsend.at[i, 0], zrecv.at[i, 0], z=z_ahead)
        push(source, to, zsend.at[i, 1], zrecv.at[i, 1], z=z_back)

    push(head_hbm.at[:, columns(y_far, vocab)], passing, wsend.at[0], wrecv.at[0], y=y_ahead)
    for i in range(2):
        head_open(i, pieces_hbm.at[z * RING + rest[i]])
    for i, to in enumerate((y_ahead, y_back, y_far)):
        push(target_ref, wanted.at[y], tsend.at[i], trecv.at[i], y=to)
    wanted[y] = target_ref[...]

    def head_relay(i):
        arrived(place(z_back, rest[i]), zrecv.at[i, 0])
        push(place(z_back, rest[i]), place(z_back, rest[i]), zsend.at[i, 2], zrecv.at[i, 2], z=z_ahead)

    att = att_ref[...]
    value = scatter_sum(lambda d: dot(att, wo_ref[:, columns(d, width)]),
                        stage, paired, inbox, send, pair_sem, in_sem)
    middle = Gather(mid, msend, mrecv)
    mid[mine] = (tok_ref[...].astype(F32) + value).astype(BF16)
    middle.open()
    arrived(passing, wrecv.at[0])
    push(passing, place(z, y_back), wsend.at[1], wrecv.at[1], y=y_ahead)
    middle.relay()
    middle.close()
    normalise(mid, gain_ref, normed)
    arrived(place(z, y_far), wrecv.at[1])
    head_open(2, place(z, y_far))
    head_relay(0)
    loads[0].wait()
    loads[1].wait()
    for t in range(inner.shape[1] // width):
        tile = slice(t * width, (t + 1) * width)
        gate = dot(normed[...], wg[:, tile])
        upper = dot(normed[...], wu[:, tile])
        inner[:, tile] = (gate / (1.0 + jnp.exp(-gate)) * upper).astype(BF16)
    loads[2].wait()
    head_relay(1)
    value = scatter_sum(lambda d: dot(inner[...], wd[:, columns(d, width)]),
                        stage2, paired2, inbox2, send2, pair_sem2, in_sem2)
    share = (mid[mine].astype(F32) + value).astype(BF16)
    out_ref[...] = share
    hidden[y, mine] = share

    first = Gather(hidden.at[y], gsend.at[0], grecv.at[y])
    distant = Gather(hidden.at[y_far], gsend.at[1], grecv.at[y_far])
    y_down, y_up = lax.rem(y + 3, RING), lax.rem(y + 1, RING)
    moved = []

    def hand(group, slot, **device):
        push(hidden.at[group, slot], hidden.at[group, slot], ysend.at[len(moved)], grecv.at[group, slot],
             **device)
        moved.append(slot)

    def spread(to):
        hand(y, 2 * to + core, y=y_ahead)
        hand(y, 2 * to + core, y=y_back)

    def collect(group, to):
        arrived(hidden.at[group, 2 * to + core], grecv.at[group, 2 * to + core])
        hand(group, 2 * to + core, c=1 - core)

    first.open()
    spread(x)
    arrived(hidden.at[y_back, mine], grecv.at[y_back, mine])
    hand(y_back, mine, y=y_ahead)
    first.relay()
    spread(x_back)
    spread(x_ahead)
    hand(y_back, mine, c=1 - core)
    collect(y_ahead, x)
    head_relay(2)
    first.last()
    spread(x_far)
    arrived(hidden.at[y_far, mine], grecv.at[y_far, mine])
    distant.open()
    first.rest()
    for i, group in enumerate((y_back, y_ahead, y_far)):
        arrived(wanted.at[group], trecv.at[i])
    for copy in loads[3:]:
        copy.wait()
    for i, py in enumerate(rest):
        arrived(place(z_ahead, py), zrecv.at[i, 1])
        arrived(place(z_far, py), zrecv.at[i, 2])

    tile = 512
    eye = (lax.broadcasted_iota(jnp.int32, (rows, rows), 0)
           == lax.broadcasted_iota(jnp.int32, (rows, rows), 1))
    start = (mine * RING + y) * vocab
    column = lax.broadcasted_iota(jnp.int32, (1, vocab), 1)

    def to_row(value):
        return jnp.sum(jnp.where(eye, value, 0.0), axis=0, keepdims=True)

    for index, group in enumerate((y, y_down, y_up, y_far)):
        if index in (1, 2):
            for to in range(RING):
                slot = 2 * to + 1 - core
                arrived(hidden.at[group, slot], grecv.at[group, slot])
        if index == 3:
            distant.rest()
        normalise(hidden.at[group], last_gain_ref, normed)
        for t in range(vocab // tile):
            logits[:, t * tile:(t + 1) * tile] = dot(normed[...], weight[:, t * tile:(t + 1) * tile])
        if index == 0:
            for to in (x_back, x_ahead):
                collect(y_back, to)
                collect(y_ahead, to)
            distant.relay()
            collect(y_back, x_far)
            collect(y_ahead, x_far)
            distant.last()
        value = logits[...]
        top = jnp.max(value, axis=1, keepdims=True)
        total = jnp.sum(jnp.exp(value - top), axis=1, keepdims=True)
        target = jnp.sum(jnp.where(eye, wanted[group], 0), axis=1, keepdims=True)
        picked = jnp.sum(jnp.where(target - start == column, value, 0.0), axis=1, keepdims=True)
        stat[group, 0:1, :] = to_row(top)
        stat[group, 1:2, :] = to_row(total)
        stat[group, 2:3, :] = to_row(picked)
        if index:
            push(stat.at[group], stat_y.at[y], ssend.at[index - 1], srecv.at[y], y=group)

    stat_y[y] = stat[y]
    for group in (y_back, y_ahead, y_far):
        arrived(stat_y.at[group], srecv.at[group])

    def merge(parts, count):
        top = parts[0, 0:1, :]
        for i in range(1, count):
            top = jnp.maximum(top, parts[i, 0:1, :])
        total = jnp.zeros_like(top)
        picked = jnp.zeros_like(top)
        for i in range(count):
            total += parts[i, 1:2, :] * jnp.exp(parts[i, 0:1, :] - top)
            picked += parts[i, 2:3, :]
        return (top, total, picked)

    for i, value in enumerate(merge(stat_y, RING)):
        stat_m[mine, i:i + 1, :] = value
    for i, peer in enumerate(others):
        push(stat_m.at[mine], stat_m.at[mine], ksend.at[i], krecv.at[mine], **peer)
    for peer in others:
        slot = 2 * peer["x"] + peer["c"]
        arrived(stat_m.at[slot], krecv.at[slot])
    top, total, picked = merge(stat_m, 8)
    log_ref[...] = picked - top - jnp.log(total)
    middle.finish()
    first.finish()
    distant.finish()
    for copy in sent:
        copy.wait_send()


def finish(attended, tokens, mlp_gain, w_out, final_gain, targets, w_gate, w_up, w_down, w_head, pieces):
    rows, width = tokens.shape
    units = w_gate.shape[1]
    block = (rows, width)
    vocab = pieces.shape[2]
    dma = pltpu.SemaphoreType.DMA
    stats = (8, rows)

    def blocks(n):
        return pltpu.VMEM((n,) + block, BF16)

    return pl.pallas_call(
        finish_kernel,
        in_specs=[vmem()] * 6 + [hbm()] * 5,
        out_specs=[vmem(), vmem()],
        out_shape=[jax.ShapeDtypeStruct(block, BF16), jax.ShapeDtypeStruct((1, rows), F32)],
        scratch_shapes=[pltpu.VMEM(w_gate.shape, BF16), pltpu.VMEM(w_up.shape, BF16),
                        pltpu.VMEM(w_down.shape, BF16),
                        blocks(7), blocks(4), blocks(3), blocks(7), blocks(4), blocks(3), blocks(8),
                        pltpu.VMEM((rows, 8 * width), BF16), pltpu.VMEM((rows, units), BF16),
                        pltpu.VMEM((8 * width, vocab), BF16), pltpu.VMEM((RING, 8) + block, BF16),
                        pltpu.VMEM((rows, vocab), F32),
                        pltpu.VMEM((RING, 1, rows), jnp.int32), pltpu.VMEM((RING,) + stats, F32),
                        pltpu.VMEM((RING,) + stats, F32), pltpu.VMEM((8,) + stats, F32),
                        dma((9,)), dma((7,)), dma((4,)), dma((3,)), dma((7,)), dma((4,)), dma((3,)),
                        dma((7,)), dma((8,)),
                        dma((2, 7)), dma((4, 8)), dma((17,)), dma((3,)), dma((3,)),
                        dma((3,)), dma((4,)), dma((7,)), dma((8,)), dma((3, 3)), dma((3, 3)),
                        pltpu.VMEM((w_head.shape[0], vocab), BF16), dma((2,)), dma((2,))],
        compiler_params=pltpu.CompilerParams(collective_id=2, has_side_effects=True,
                                             vmem_limit_bytes=56 << 20),
        cost_estimate=pl.CostEstimate(flops=60 << 30, bytes_accessed=24 << 20, transcendentals=0),
        name="finish",
    )(attended, tokens, mlp_gain, w_out, final_gain, targets, w_gate, w_up, w_down, w_head, pieces)


def results_kernel(share_ref, log_ref, share_out, log_out):
    share_out[...] = share_ref[...]
    log_out[...] = log_ref[0]


def results(share, logprob):
    return pl.pallas_call(
        results_kernel,
        in_specs=[vmem()] * 2,
        out_specs=[vmem()] * 2,
        out_shape=[jax.ShapeDtypeStruct(share.shape, BF16), jax.ShapeDtypeStruct(logprob.shape[1:], F32)],
        name="results",
    )(share, logprob)


def body(tokens, attn_gain, mlp_gain, final_gain, q_gain, k_gain, w_query, w_keyval, w_out, w_gate,
         w_up, w_down, w_head, targets, req_lengths, req_tenant, prefix_piece, prefix_kv):
    queries, own, pieces, slabs = entry(
        req_lengths, tokens, attn_gain[None], q_gain[None], k_gain[None], w_query, w_keyval,
        prefix_kv, w_head)
    attended = attention(req_lengths, req_tenant, prefix_piece, queries, own, pieces)
    share, logprob = finish(attended, tokens, mlp_gain[None], w_out, final_gain[None], targets[None],
                            w_gate, w_up, w_down, w_head, slabs)
    return tuple(results(share, logprob))


def solution(mesh):
    req = ("z", "y")
    mlp = ("x", "c")
    in_specs = (
        P(req, mlp), P(), P(), P(), P(), P(), P(None, mlp), P(None, mlp), P(mlp, None),
        P(None, mlp), P(None, mlp), P(mlp, None), P(req, mlp), P(req), P(req, None), P(req, None),
        P(), P(req, None, mlp),
    )
    out_specs = (P(req, mlp), P(req))
    split = Mesh(mesh.devices.reshape(RING, RING, RING, 2), ("z", "y", "x", "c"))
    return jax.shard_map(body, mesh=split, in_specs=in_specs, out_specs=out_specs, check_vma=False)
```

```python
import functools
import math

import jax
import jax.numpy as jnp
from jax import lax
from jax.experimental import pallas as pl
from jax.experimental.pallas import tpu as pltpu
from jax.sharding import Mesh
from jax.sharding import PartitionSpec as P

TENANTS = 4
PLEN = 4096
BLOCK = 64
EPS = 1e-05
LOG_THETA = math.log(1000000.0)
NEG = -1e30
RING = 4
MESH = pl.DeviceIdType.MESH
F32 = jnp.float32
BF16 = jnp.bfloat16


def dot(a, b):
    return jnp.dot(a, b, preferred_element_type=F32)


def dot_nt(a, b):
    return lax.dot_general(a, b, (((1,), (1,)), ((), ())), preferred_element_type=F32)


def remote(src, dst, send_sem, recv_sem, **device):
    return pltpu.make_async_remote_copy(
        src_ref=src, dst_ref=dst, send_sem=send_sem, recv_sem=recv_sem,
        device_id=device, device_id_type=MESH,
    )


def arrived(ref, sem):
    pltpu.make_async_copy(ref, ref, sem).wait()


def greet(peers):
    barrier = pltpu.get_barrier_semaphore()
    for peer in peers:
        pl.semaphore_signal(barrier, inc=1, device_id=peer, device_id_type=MESH)
    pl.semaphore_wait(barrier, len(peers))


def ring_of(axis, core):
    me = lax.axis_index(axis)
    ahead = lax.rem(me + 1 + 2 * core, RING)
    back = lax.rem(me + 3 + 2 * core, RING)
    far = lax.rem(me + 2, RING)
    return (me, ahead, back, far)


class Gather:
    def __init__(self, slots, send, recv):
        self.slots, self.send, self.recv, self.sent = slots, send, recv, []
        self.core = lax.axis_index("c")
        self.x, self.ahead, self.back, self.far = ring_of("x", self.core)

    def push(self, at, core, src=None, **device):
        slot = 2 * at + core
        copy = remote(self.slots.at[slot] if src is None else src, self.slots.at[slot],
                      self.send.at[len(self.sent)], self.recv.at[slot], **device)
        copy.start()
        self.sent.append(copy)

    def wait(self, at, core):
        slot = 2 * at + core
        arrived(self.slots.at[slot], self.recv.at[slot])

    def open(self, src=None):
        self.push(self.x, self.core, src, x=self.ahead)
        self.push(self.x, self.core, src, x=self.back)
        self.push(self.x, self.core, src, c=1 - self.core)

    def relay(self):
        self.wait(self.back, self.core)
        self.push(self.back, self.core, x=self.ahead)
        self.push(self.back, self.core, c=1 - self.core)
        self.wait(self.ahead, self.core)
        self.push(self.ahead, self.core, c=1 - self.core)

    def last(self):
        self.wait(self.far, self.core)
        self.push(self.far, self.core, c=1 - self.core)

    def close(self):
        self.last()
        self.rest()

    def rest(self):
        for x in (self.x, self.back, self.ahead, self.far):
            self.wait(x, 1 - self.core)

    def finish(self):
        for copy in self.sent:
            copy.wait_send()


def scatter_sum(partial, stage, paired, inbox, send, pair_sem, in_sem):
    core = lax.axis_index("c")
    x, ahead, back, far = ring_of("x", core)
    sent = []

    def push(value, dst, recv, **device):
        index = len(sent)
        stage[index] = value.astype(BF16)
        copy = remote(stage.at[index], dst, send.at[index], recv, **device)
        copy.start()
        sent.append(copy)

    def chip(to):
        mine = partial(2 * to + core)
        arrived(paired.at[to], pair_sem.at[to])
        return mine + paired[to].astype(F32)

    for to in (far, back, ahead, x):
        push(partial(2 * to + 1 - core), paired.at[to], pair_sem.at[to], c=1 - core)
    push(chip(far), inbox.at[2], in_sem.at[2], x=ahead)
    push(chip(back), inbox.at[1], in_sem.at[1], x=back)
    value = chip(ahead)
    arrived(inbox.at[2], in_sem.at[2])
    push(value + inbox[2].astype(F32), inbox.at[0], in_sem.at[0], x=ahead)
    value = chip(x)
    for slot in (1, 0):
        arrived(inbox.at[slot], in_sem.at[slot])
        value += inbox[slot].astype(F32)
    for copy in sent:
        copy.wait_send()
    return value


def normalise(blocks, gain_ref, normed):
    count, rows, width = blocks.shape
    square = jnp.zeros((rows, 1), F32)
    for m in range(count):
        value = blocks[m].astype(F32)
        square += jnp.sum(value * value, axis=1, keepdims=True)
    factor = lax.rsqrt(square / (count * width) + EPS)
    for m in range(count):
        columns = slice(m * width, (m + 1) * width)
        normed[:, columns] = (blocks[m].astype(F32) * factor * gain_ref[:, columns]).astype(BF16)


def x_peers():
    core = lax.axis_index("c")
    _, ahead, back, _ = ring_of("x", core)
    return [dict(x=ahead), dict(x=back), dict(c=1 - core)]


def entry_kernel(requests, scale, length_ref, tok_ref, gain_ref, qgain_ref, kgain_ref, wq_ref,
                 wkv_ref, prefix_ref, head_ref, q_out, own_out, pieces, head_out, stream,
                 normed, send, recv, psend, precv, wsend, wrecv, local_sem):
    core = lax.axis_index("c")
    rows = tok_ref.shape[0]
    size = qgain_ref.shape[1]
    cut = prefix_ref.shape[1] * 23 // 32
    spans = (pl.ds(0, cut), pl.ds(cut, prefix_ref.shape[1] - cut))
    y, y_ahead, y_back, y_far = ring_of("y", core)
    z, z_ahead, z_back, z_far = ring_of("z", core)
    greet(x_peers() + [dict(y=y_ahead), dict(y=y_back), dict(z=z_ahead), dict(z=z_back)])

    sent = []

    def view(part, pz, py):
        return pieces.at[pz * RING + py, spans[part]]

    def push(part, pz, py, src=None, **device):
        slot = pz * RING + py
        copy = remote(view(part, pz, py) if src is None else src, view(part, pz, py),
                      psend.at[len(sent)], precv.at[part, slot], **device)
        copy.start()
        sent.append(copy)

    def wait(part, pz, py):
        arrived(view(part, pz, py), precv.at[part, pz * RING + py])

    first = [prefix_ref.at[0, spans[part]] for part in range(2)]
    gather = Gather(stream, send, recv)
    gather.open(tok_ref)
    push(0, z, y, first[0], y=y_ahead)
    push(0, z, y, first[0], y=y_back)
    push(1, z, y, first[1], z=z_ahead)
    push(1, z, y, first[1], z=z_back)
    push(0, z, y, first[0], z=z_ahead)
    push(0, z, y, first[0], z=z_back)
    push(1, z, y, first[1], y=y_ahead)
    push(1, z, y, first[1], y=y_back)

    given = []
    part_words = head_out.shape[2]

    def words(index):
        return head_ref.at[:, pl.ds(pl.multiple_of(index * part_words, part_words), part_words)]

    def give(index, src, dst, **device):
        copy = remote(src, dst, wsend.at[index], wrecv.at[index], **device)
        copy.start()
        given.append(copy)

    keep = [pltpu.make_async_copy(prefix_ref.at[0], pieces.at[z * RING + y], local_sem.at[0]),
            pltpu.make_async_copy(tok_ref, stream.at[2 * gather.x + core], local_sem.at[1])]
    for copy in keep:
        copy.start()

    wait(0, z, y_back)
    push(0, z, y_back, y=y_ahead)
    push(0, z, y_back, z=z_ahead)
    push(0, z, y_back, z=z_back)
    wait(1, z_back, y)
    push(1, z_back, y, z=z_ahead)
    push(1, z_back, y, y=y_ahead)
    push(1, z_back, y, y=y_back)
    wait(0, z, y_ahead)
    push(0, z, y_ahead, z=z_ahead)
    push(0, z, y_ahead, z=z_back)
    wait(1, z_ahead, y)
    push(1, z_ahead, y, y=y_ahead)
    push(1, z_ahead, y, y=y_back)
    gather.relay()
    wait(0, z, y_far)
    push(0, z, y_far, z=z_ahead)
    push(0, z, y_far, z=z_back)
    wait(1, z_far, y)
    push(1, z_far, y, y=y_ahead)
    push(1, z_far, y, y=y_back)
    give(0, words(y_ahead), head_out.at[0], y=y_ahead)
    give(1, words(y_back), head_out.at[1], y=y_back)

    row = lax.broadcasted_iota(jnp.int32, (rows, 1), 0)
    offset = row
    end = 0
    for r in range(requests):
        end = end + length_ref[0, r]
        offset = offset - jnp.where(row >= end, length_ref[0, r], 0)
    lane = lax.broadcasted_iota(jnp.int32, (1, size), 1)
    freq = jnp.exp((lane & (size // 2 - 1)).astype(F32) * (-2.0 * LOG_THETA / size))
    angle = (PLEN + offset).astype(F32) * freq
    cosine, sine = jnp.cos(angle), jnp.sin(angle)

    def turned(value, gain):
        value = value * lax.rsqrt(jnp.mean(value * value, axis=1, keepdims=True) + EPS) * gain
        other = jnp.concatenate([-value[:, size // 2:], value[:, : size // 2]], axis=1)
        return (value * cosine + other * sine).astype(BF16)

    keep[1].wait()
    gather.close()
    normalise(stream, gain_ref, normed)

    far_z = [(py, z_back, z_ahead) for py in (y, y_far)] + [(py, z_ahead, z_back) for py in (y_back, y_ahead)]
    far_y = [(pz, y_back, y_ahead) for pz in (z, z_far)] + [(pz, y_ahead, y_back) for pz in (z_back, z_ahead)]
    order = (0, 2, 3, 1)
    for i in order:
        py, come, go = far_z[i]
        wait(0, come, py)
        push(0, come, py, z=go)
        pz, come, go = far_y[i]
        wait(1, pz, come)
        push(1, pz, come, y=go)

    query = dot(normed[...], wq_ref[...])
    keyval = dot(normed[...], wkv_ref[...])
    heads = query.shape[1] // size
    zero = jnp.zeros((rows, size), BF16)
    for h in range(heads):
        value = turned(query[:, h * size:(h + 1) * size], qgain_ref[...])
        value = jnp.concatenate([value * jnp.asarray(scale, BF16), zero], axis=1)
        for i in range(rows // BLOCK):
            q_out[i, h * BLOCK:(h + 1) * BLOCK, :] = value[i * BLOCK:(i + 1) * BLOCK]
    own_out[...] = jnp.concatenate(
        [turned(keyval[:, :size], kgain_ref[...]), keyval[:, size:].astype(BF16)], axis=1
    )

    for py, come, go in far_z:
        wait(0, go, py)
    for pz, come, go in far_y:
        wait(1, pz, go)
    for py, come, go in far_z:
        wait(0, z_far, py)
    for pz, come, go in far_y:
        wait(1, pz, y_far)
    for i in range(2):
        arrived(head_out.at[i], wrecv.at[i])
    keep[0].wait()
    gather.finish()
    for copy in sent + given:
        copy.wait_send()


def vmem():
    return pl.BlockSpec(memory_space=pltpu.VMEM)


def hbm():
    return pl.BlockSpec(memory_space=pl.ANY)


def smem():
    return pl.BlockSpec(memory_space=pltpu.SMEM)


def entry(lengths, tokens, attn_gain, q_gain, k_gain, w_query, w_keyval, prefix_kv, w_head):
    rows, width = tokens.shape
    size = q_gain.shape[1]
    heads = w_query.shape[1] // size
    count = RING * RING
    quarter = (w_head.shape[0], w_head.shape[1] // RING)
    return pl.pallas_call(
        functools.partial(entry_kernel, lengths.shape[1], size ** (-0.5)),
        in_specs=[smem()] + [vmem()] * 7 + [hbm()],
        out_specs=[vmem(), vmem(), hbm(), hbm()],
        out_shape=[jax.ShapeDtypeStruct((rows // BLOCK, heads * BLOCK, 2 * size), BF16),
                   jax.ShapeDtypeStruct((rows, 2 * size), BF16),
                   jax.ShapeDtypeStruct((count,) + prefix_kv.shape[1:], BF16),
                   jax.ShapeDtypeStruct((2,) + quarter, BF16)],
        scratch_shapes=[pltpu.VMEM((8, rows, width), BF16), pltpu.VMEM((rows, 8 * width), BF16),
                        pltpu.SemaphoreType.DMA((7,)), pltpu.SemaphoreType.DMA((8,)),
                        pltpu.SemaphoreType.DMA((30,)), pltpu.SemaphoreType.DMA((2, count)),
                        pltpu.SemaphoreType.DMA((2,)), pltpu.SemaphoreType.DMA((2,)),
                        pltpu.SemaphoreType.DMA((2,))],
        compiler_params=pltpu.CompilerParams(collective_id=1, has_side_effects=True),
        cost_estimate=pl.CostEstimate(flops=30 << 30, bytes_accessed=8 << 20, transcendentals=0),
        name="entry",
    )(lengths, tokens, attn_gain, q_gain, k_gain, w_query, w_keyval, prefix_kv, w_head)


def attention_kernel(requests, split, length_ref, tenant_ref, piece_ref,
                     q_ref, own_ref, kv_ref, out_ref, best_ref, total_ref, accum_ref, slot_ref):
    block = pl.program_id(0)
    queries = q_ref[0]
    count = queries.shape[0]
    rows = own_ref.shape[0]
    size = own_ref.shape[1] // 2
    for j in range(kv_ref.shape[0]):
        slot_ref[piece_ref[j]] = j
    row = (lax.broadcasted_iota(jnp.int32, (count, 1), 0) & (BLOCK - 1)) + block * BLOCK
    col = lax.broadcasted_iota(jnp.int32, (1, rows), 1)
    row_request = jnp.zeros((count, 1), jnp.int32)
    col_request = jnp.zeros((1, rows), jnp.int32)
    ends = []
    for r in range(requests):
        ends.append(length_ref[0, r] + (ends[-1] if ends else 0))
        row_request += (row >= ends[r]).astype(jnp.int32)
        col_request += (col >= ends[r]).astype(jnp.int32)
    seen = (row_request == col_request) & (col <= row)
    own = own_ref[...]
    scores = jnp.where(seen, dot_nt(queries, own), NEG)
    best = jnp.max(scores, axis=1, keepdims=True)
    weights = jnp.where(seen, jnp.exp(scores - best), 0.0)
    best_ref[...] = best
    total_ref[...] = jnp.sum(weights, axis=1, keepdims=True)
    accum_ref[...] = dot(weights.astype(BF16), own)
    for r in range(requests):
        begin = ends[r] - length_ref[0, r]

        @pl.when((ends[r] > block * BLOCK) & (begin < block * BLOCK + BLOCK))
        def _():
            inside = row_request == r
            tenant = tenant_ref[0, r]

            old = best_ref[...]
            keyvals = [kv_ref[slot_ref[tenant * split + index]] for index in range(split)]
            parts = [dot_nt(queries, keyval) for keyval in keyvals]
            new = old
            for part in parts:
                new = jnp.maximum(new, jnp.max(part, axis=1, keepdims=True))
            new = jnp.where(inside, new, old)
            keep = jnp.exp(old - new)
            shift = jnp.where(inside, new, -NEG)
            total = total_ref[...] * keep
            accum = accum_ref[...] * keep
            for part, keyval in zip(parts, keyvals):
                piece_weights = jnp.exp(part - shift)
                total += jnp.sum(piece_weights, axis=1, keepdims=True)
                accum += dot(piece_weights.astype(BF16), keyval)
            best_ref[...], total_ref[...], accum_ref[...] = new, total, accum

    out = accum_ref[...] / total_ref[...]
    heads = [out[h * BLOCK:(h + 1) * BLOCK, size:] for h in range(count // BLOCK)]
    out_ref[...] = jnp.concatenate(heads, axis=1).astype(BF16)


def attention(lengths, tenants, prefix_piece, queries, own, pieces):
    blocks, count, width = queries.shape
    rows = own.shape[0]
    columns = count // BLOCK * width // 2
    return pl.pallas_call(
        functools.partial(attention_kernel, lengths.shape[1], pieces.shape[0] // TENANTS),
        grid=(blocks,),
        in_specs=[smem(), smem(), smem(),
                  pl.BlockSpec((1, count, width), lambda i: (i, 0, 0)),
                  pl.BlockSpec(own.shape, lambda i: (0, 0)),
                  pl.BlockSpec(pieces.shape, lambda i: (0, 0, 0), pipeline_mode=pl.Buffered(1))],
        out_specs=pl.BlockSpec((BLOCK, columns), lambda i: (i, 0)),
        out_shape=jax.ShapeDtypeStruct((rows, columns), BF16),
        scratch_shapes=[pltpu.VMEM((count, 1), F32), pltpu.VMEM((count, 1), F32),
                        pltpu.VMEM((count, width), F32), pltpu.SMEM((pieces.shape[0],), jnp.int32)],
        cost_estimate=pl.CostEstimate(flops=24 << 30, bytes_accessed=5 << 20, transcendentals=0),
        name="attention",
    )(lengths, tenants, prefix_piece, queries, own, pieces)


def finish_kernel(att_ref, tok_ref, gain_ref, wo_ref, last_gain_ref, target_ref, wg_hbm, wu_hbm, wd_hbm,
                  head_hbm, near_hbm, back_hbm, ahead_hbm, out_ref, log_ref,
                  wg, wu, wd, stage, paired, inbox, stage2, paired2, inbox2, mid, normed, inner,
                  weight, hidden, logits, wanted, stat, stat_y, stat_m,
                  load, send, pair_sem, in_sem, send2, pair_sem2, in_sem2, msend, mrecv,
                  gsend, grecv, ysend, tsend, trecv, ssend, srecv, ksend, krecv,
                  zsend, zrecv, passing, wsend, wrecv, fsend, frecv):
    core = lax.axis_index("c")
    rows, width = tok_ref.shape
    depth, vocab = near_hbm.shape[1:]
    x, x_ahead, x_back, x_far = ring_of("x", core)
    y, y_ahead, y_back, y_far = ring_of("y", core)
    z, z_ahead, z_back, z_far = ring_of("z", core)
    mine = 2 * x + core
    sent = []

    def push(src, dst, send_sem, recv_sem, **device):
        copy = remote(src, dst, send_sem, recv_sem, **device)
        copy.start()
        sent.append(copy)

    def columns(index, count):
        return pl.ds(pl.multiple_of(index * count, count), count)

    def place(pz, py):
        return weight.at[columns(pz * RING + py, depth)]

    loads = []

    def fetch(src, dst):
        copy = pltpu.make_async_copy(src, dst, load.at[len(loads)])
        copy.start()
        loads.append(copy)

    fetch(wg_hbm, wg)
    fetch(wu_hbm, wu)
    fetch(wd_hbm, wd)
    fetch(head_hbm.at[:, columns(y, vocab)], place(z, y))
    for i, py in enumerate((y_back, y_ahead)):
        fetch(near_hbm.at[i], place(z, py))
    for i, py in enumerate((y, y_back)):
        fetch(back_hbm.at[pl.ds(i * depth, depth)], place(z_back, py))
        fetch(ahead_hbm.at[pl.ds(i * depth, depth)], place(z_ahead, py))
    rest = (y_ahead, y_far)
    others = [dict(x=lax.rem(x + i // 2, RING), c=lax.rem(core + i % 2, 2)) for i in range(1, 8)]
    greet([dict(y=y_ahead), dict(y=y_back), dict(y=y_far), dict(z=z_ahead), dict(z=z_back)] + others)

    def head_open(i, source):
        to = place(z, rest[i])
        push(source, to, zsend.at[i, 0], zrecv.at[i, 0], z=z_ahead)
        push(source, to, zsend.at[i, 1], zrecv.at[i, 1], z=z_back)

    push(head_hbm.at[:, columns(y_far, vocab)], passing, wsend.at[0], wrecv.at[0], y=y_ahead)
    head_open(0, near_hbm.at[1])
    for i, py in enumerate((y, y_back)):
        push(back_hbm.at[pl.ds(i * depth, depth)], place(z_back, py), fsend.at[i], frecv.at[i], z=z_ahead)
    for i, to in enumerate((y_ahead, y_back, y_far)):
        push(target_ref, wanted.at[y], tsend.at[i], trecv.at[i], y=to)
    wanted[y] = target_ref[...]

    def head_relay(i):
        arrived(place(z_back, rest[i]), zrecv.at[i, 0])
        push(place(z_back, rest[i]), place(z_back, rest[i]), zsend.at[i, 2], zrecv.at[i, 2], z=z_ahead)

    att = att_ref[...]
    value = scatter_sum(lambda d: dot(att, wo_ref[:, columns(d, width)]),
                        stage, paired, inbox, send, pair_sem, in_sem)
    middle = Gather(mid, msend, mrecv)
    mid[mine] = (tok_ref[...].astype(F32) + value).astype(BF16)
    middle.open()
    arrived(passing, wrecv.at[0])
    push(passing, place(z, y_back), wsend.at[1], wrecv.at[1], y=y_ahead)
    middle.relay()
    middle.close()
    normalise(mid, gain_ref, normed)
    arrived(place(z, y_far), wrecv.at[1])
    head_open(1, place(z, y_far))
    head_relay(0)
    loads[0].wait()
    loads[1].wait()
    for t in range(inner.shape[1] // width):
        tile = slice(t * width, (t + 1) * width)
        gate = dot(normed[...], wg[:, tile])
        upper = dot(normed[...], wu[:, tile])
        inner[:, tile] = (gate / (1.0 + jnp.exp(-gate)) * upper).astype(BF16)
    loads[2].wait()
    value = scatter_sum(lambda d: dot(inner[...], wd[:, columns(d, width)]),
                        stage2, paired2, inbox2, send2, pair_sem2, in_sem2)
    share = (mid[mine].astype(F32) + value).astype(BF16)
    out_ref[...] = share
    hidden[y, mine] = share

    first = Gather(hidden.at[y], gsend.at[0], grecv.at[y])
    distant = Gather(hidden.at[y_far], gsend.at[1], grecv.at[y_far])
    y_down, y_up = lax.rem(y + 3, RING), lax.rem(y + 1, RING)
    moved = []

    def hand(group, slot, **device):
        push(hidden.at[group, slot], hidden.at[group, slot], ysend.at[len(moved)], grecv.at[group, slot],
             **device)
        moved.append(slot)

    def spread(to):
        hand(y, 2 * to + core, y=y_ahead)
        hand(y, 2 * to + core, y=y_back)

    def collect(group, to):
        arrived(hidden.at[group, 2 * to + core], grecv.at[group, 2 * to + core])
        hand(group, 2 * to + core, c=1 - core)

    first.open()
    spread(x)
    arrived(hidden.at[y_back, mine], grecv.at[y_back, mine])
    hand(y_back, mine, y=y_ahead)
    first.relay()
    spread(x_back)
    spread(x_ahead)
    hand(y_back, mine, c=1 - core)
    collect(y_ahead, x)
    head_relay(1)
    first.last()
    spread(x_far)
    arrived(hidden.at[y_far, mine], grecv.at[y_far, mine])
    distant.open()
    first.rest()
    for i, group in enumerate((y_back, y_ahead, y_far)):
        arrived(wanted.at[group], trecv.at[i])
    for copy in loads[3:]:
        copy.wait()
    for i, py in enumerate((y, y_back)):
        arrived(place(z_far, py), frecv.at[i])
    for i, py in enumerate(rest):
        arrived(place(z_ahead, py), zrecv.at[i, 1])
        arrived(place(z_far, py), zrecv.at[i, 2])

    tile = 512
    eye = (lax.broadcasted_iota(jnp.int32, (rows, rows), 0)
           == lax.broadcasted_iota(jnp.int32, (rows, rows), 1))
    start = (mine * RING + y) * vocab
    column = lax.broadcasted_iota(jnp.int32, (1, vocab), 1)

    def to_row(value):
        return jnp.sum(jnp.where(eye, value, 0.0), axis=0, keepdims=True)

    for index, group in enumerate((y, y_down, y_up, y_far)):
        if index in (1, 2):
            for to in range(RING):
                slot = 2 * to + 1 - core
                arrived(hidden.at[group, slot], grecv.at[group, slot])
        if index == 3:
            distant.rest()
        normalise(hidden.at[group], last_gain_ref, normed)
        for t in range(vocab // tile):
            logits[:, t * tile:(t + 1) * tile] = dot(normed[...], weight[:, t * tile:(t + 1) * tile])
        if index == 0:
            for to in (x_back, x_ahead):
                collect(y_back, to)
                collect(y_ahead, to)
            distant.relay()
            collect(y_back, x_far)
            collect(y_ahead, x_far)
            distant.last()
        value = logits[...]
        top = jnp.max(value, axis=1, keepdims=True)
        total = jnp.sum(jnp.exp(value - top), axis=1, keepdims=True)
        target = jnp.sum(jnp.where(eye, wanted[group], 0), axis=1, keepdims=True)
        picked = jnp.sum(jnp.where(target - start == column, value, 0.0), axis=1, keepdims=True)
        stat[group, 0:1, :] = to_row(top)
        stat[group, 1:2, :] = to_row(total)
        stat[group, 2:3, :] = to_row(picked)
        if index:
            push(stat.at[group], stat_y.at[y], ssend.at[index - 1], srecv.at[y], y=group)

    stat_y[y] = stat[y]
    for group in (y_back, y_ahead, y_far):
        arrived(stat_y.at[group], srecv.at[group])

    def merge(parts, count):
        top = parts[0, 0:1, :]
        for i in range(1, count):
            top = jnp.maximum(top, parts[i, 0:1, :])
        total = jnp.zeros_like(top)
        picked = jnp.zeros_like(top)
        for i in range(count):
            total += parts[i, 1:2, :] * jnp.exp(parts[i, 0:1, :] - top)
            picked += parts[i, 2:3, :]
        return (top, total, picked)

    for i, value in enumerate(merge(stat_y, RING)):
        stat_m[mine, i:i + 1, :] = value
    for i, peer in enumerate(others):
        push(stat_m.at[mine], stat_m.at[mine], ksend.at[i], krecv.at[mine], **peer)
    for peer in others:
        slot = 2 * peer["x"] + peer["c"]
        arrived(stat_m.at[slot], krecv.at[slot])
    top, total, picked = merge(stat_m, 8)
    log_ref[...] = picked - top - jnp.log(total)
    middle.finish()
    first.finish()
    distant.finish()
    for copy in sent:
        copy.wait_send()


def finish(attended, tokens, mlp_gain, w_out, final_gain, targets, w_gate, w_up, w_down, w_head, near,
           from_back, from_ahead):
    rows, width = tokens.shape
    units = w_gate.shape[1]
    block = (rows, width)
    vocab = near.shape[2]
    dma = pltpu.SemaphoreType.DMA
    stats = (8, rows)

    def blocks(n):
        return pltpu.VMEM((n,) + block, BF16)

    return pl.pallas_call(
        finish_kernel,
        in_specs=[vmem()] * 6 + [hbm()] * 7,
        out_specs=[vmem(), vmem()],
        out_shape=[jax.ShapeDtypeStruct(block, BF16), jax.ShapeDtypeStruct((1, rows), F32)],
        scratch_shapes=[pltpu.VMEM(w_gate.shape, BF16), pltpu.VMEM(w_up.shape, BF16),
                        pltpu.VMEM(w_down.shape, BF16),
                        blocks(7), blocks(4), blocks(3), blocks(7), blocks(4), blocks(3), blocks(8),
                        pltpu.VMEM((rows, 8 * width), BF16), pltpu.VMEM((rows, units), BF16),
                        pltpu.VMEM((8 * width, vocab), BF16), pltpu.VMEM((RING, 8) + block, BF16),
                        pltpu.VMEM((rows, vocab), F32),
                        pltpu.VMEM((RING, 1, rows), jnp.int32), pltpu.VMEM((RING,) + stats, F32),
                        pltpu.VMEM((RING,) + stats, F32), pltpu.VMEM((8,) + stats, F32),
                        dma((10,)), dma((7,)), dma((4,)), dma((3,)), dma((7,)), dma((4,)), dma((3,)),
                        dma((7,)), dma((8,)),
                        dma((2, 7)), dma((4, 8)), dma((17,)), dma((3,)), dma((3,)),
                        dma((3,)), dma((4,)), dma((7,)), dma((8,)), dma((2, 3)), dma((2, 3)),
                        pltpu.VMEM((w_head.shape[0], vocab), BF16), dma((2,)), dma((2,)),
                        dma((2,)), dma((2,))],
        compiler_params=pltpu.CompilerParams(collective_id=2, has_side_effects=True,
                                             vmem_limit_bytes=56 << 20),
        cost_estimate=pl.CostEstimate(flops=60 << 30, bytes_accessed=24 << 20, transcendentals=0),
        name="finish",
    )(attended, tokens, mlp_gain, w_out, final_gain, targets, w_gate, w_up, w_down, w_head, near,
      from_back, from_ahead)


def results_kernel(share_ref, log_ref, share_out, log_out):
    share_out[...] = share_ref[...]
    log_out[...] = log_ref[0]


def results(share, logprob):
    return pl.pallas_call(
        results_kernel,
        in_specs=[vmem()] * 2,
        out_specs=[vmem()] * 2,
        out_shape=[jax.ShapeDtypeStruct(share.shape, BF16), jax.ShapeDtypeStruct(logprob.shape[1:], F32)],
        name="results",
    )(share, logprob)


def body(tokens, attn_gain, mlp_gain, final_gain, q_gain, k_gain, w_query, w_keyval, w_out, w_gate,
         w_up, w_down, w_head, targets, req_lengths, req_tenant, prefix_piece, prefix_kv):
    queries, own, pieces, near = entry(
        req_lengths, tokens, attn_gain[None], q_gain[None], k_gain[None], w_query, w_keyval,
        prefix_kv, w_head)
    words = w_head.shape[1] // RING
    mine = lax.dynamic_slice_in_dim(w_head, lax.axis_index("y") * words, words, 1)
    pair = jnp.concatenate([mine, near[0]], axis=0)
    ahead = [(2 * z + c, 2 * ((z + 1 + 2 * c) % RING) + c) for z in range(RING) for c in range(2)]
    from_back = lax.ppermute(pair, ("z", "c"), ahead)
    from_ahead = lax.ppermute(pair, ("z", "c"), [(b, a) for a, b in ahead])
    attended = attention(req_lengths, req_tenant, prefix_piece, queries, own, pieces)
    share, logprob = finish(attended, tokens, mlp_gain[None], w_out, final_gain[None], targets[None],
                            w_gate, w_up, w_down, w_head, near, from_back, from_ahead)
    return tuple(results(share, logprob))


def solution(mesh):
    req = ("z", "y")
    mlp = ("x", "c")
    in_specs = (
        P(req, mlp), P(), P(), P(), P(), P(), P(None, mlp), P(None, mlp), P(mlp, None),
        P(None, mlp), P(None, mlp), P(mlp, None), P(req, mlp), P(req), P(req, None), P(req, None),
        P(), P(req, None, mlp),
    )
    out_specs = (P(req, mlp), P(req))
    split = Mesh(mesh.devices.reshape(RING, RING, RING, 2), ("z", "y", "x", "c"))
    return jax.shard_map(body, mesh=split, in_specs=in_specs, out_specs=out_specs, check_vma=False)
```

```python
import functools
import math

import jax
import jax.numpy as jnp
from jax import lax
from jax.experimental import pallas as pl
from jax.experimental.pallas import tpu as pltpu
from jax.sharding import Mesh
from jax.sharding import PartitionSpec as P

TENANTS = 4
PLEN = 4096
BLOCK = 64
EPS = 1e-05
LOG_THETA = math.log(1000000.0)
NEG = -1e30
RING = 4
MESH = pl.DeviceIdType.MESH
F32 = jnp.float32
BF16 = jnp.bfloat16


def dot(a, b):
    return jnp.dot(a, b, preferred_element_type=F32)


def dot_nt(a, b):
    return lax.dot_general(a, b, (((1,), (1,)), ((), ())), preferred_element_type=F32)


def remote(src, dst, send_sem, recv_sem, **device):
    return pltpu.make_async_remote_copy(
        src_ref=src, dst_ref=dst, send_sem=send_sem, recv_sem=recv_sem,
        device_id=device, device_id_type=MESH,
    )


def arrived(ref, sem):
    pltpu.make_async_copy(ref, ref, sem).wait()


def greet(peers):
    barrier = pltpu.get_barrier_semaphore()
    for peer in peers:
        pl.semaphore_signal(barrier, inc=1, device_id=peer, device_id_type=MESH)
    pl.semaphore_wait(barrier, len(peers))


def ring_of(axis, core):
    me = lax.axis_index(axis)
    ahead = lax.rem(me + 1 + 2 * core, RING)
    back = lax.rem(me + 3 + 2 * core, RING)
    far = lax.rem(me + 2, RING)
    return (me, ahead, back, far)


class Gather:
    def __init__(self, slots, send, recv):
        self.slots, self.send, self.recv, self.sent = slots, send, recv, []
        self.core = lax.axis_index("c")
        self.x, self.ahead, self.back, self.far = ring_of("x", self.core)

    def push(self, at, core, src=None, **device):
        slot = 2 * at + core
        copy = remote(self.slots.at[slot] if src is None else src, self.slots.at[slot],
                      self.send.at[len(self.sent)], self.recv.at[slot], **device)
        copy.start()
        self.sent.append(copy)

    def wait(self, at, core):
        slot = 2 * at + core
        arrived(self.slots.at[slot], self.recv.at[slot])

    def open(self, src=None):
        self.push(self.x, self.core, src, x=self.ahead)
        self.push(self.x, self.core, src, x=self.back)
        self.push(self.x, self.core, src, c=1 - self.core)

    def relay(self):
        self.wait(self.back, self.core)
        self.push(self.back, self.core, x=self.ahead)
        self.push(self.back, self.core, c=1 - self.core)
        self.wait(self.ahead, self.core)
        self.push(self.ahead, self.core, c=1 - self.core)

    def last(self):
        self.wait(self.far, self.core)
        self.push(self.far, self.core, c=1 - self.core)

    def close(self):
        self.last()
        self.rest()

    def rest(self):
        for x in (self.x, self.back, self.ahead, self.far):
            self.wait(x, 1 - self.core)

    def finish(self):
        for copy in self.sent:
            copy.wait_send()


def scatter_sum(partial, stage, paired, inbox, send, pair_sem, in_sem):
    core = lax.axis_index("c")
    x, ahead, back, far = ring_of("x", core)
    sent = []

    def push(value, dst, recv, **device):
        index = len(sent)
        stage[index] = value.astype(BF16)
        copy = remote(stage.at[index], dst, send.at[index], recv, **device)
        copy.start()
        sent.append(copy)

    def chip(to):
        mine = partial(2 * to + core)
        arrived(paired.at[to], pair_sem.at[to])
        return mine + paired[to].astype(F32)

    for to in (far, back, ahead, x):
        push(partial(2 * to + 1 - core), paired.at[to], pair_sem.at[to], c=1 - core)
    push(chip(far), inbox.at[2], in_sem.at[2], x=ahead)
    push(chip(back), inbox.at[1], in_sem.at[1], x=back)
    value = chip(ahead)
    arrived(inbox.at[2], in_sem.at[2])
    push(value + inbox[2].astype(F32), inbox.at[0], in_sem.at[0], x=ahead)
    value = chip(x)
    for slot in (1, 0):
        arrived(inbox.at[slot], in_sem.at[slot])
        value += inbox[slot].astype(F32)
    for copy in sent:
        copy.wait_send()
    return value


def normalise(blocks, gain_ref, normed):
    count, rows, width = blocks.shape
    square = jnp.zeros((rows, 1), F32)
    for m in range(count):
        value = blocks[m].astype(F32)
        square += jnp.sum(value * value, axis=1, keepdims=True)
    factor = lax.rsqrt(square / (count * width) + EPS)
    for m in range(count):
        columns = slice(m * width, (m + 1) * width)
        normed[:, columns] = (blocks[m].astype(F32) * factor * gain_ref[:, columns]).astype(BF16)


def x_peers():
    core = lax.axis_index("c")
    _, ahead, back, _ = ring_of("x", core)
    return [dict(x=ahead), dict(x=back), dict(c=1 - core)]


def entry_kernel(requests, scale, length_ref, tok_ref, gain_ref, qgain_ref, kgain_ref, wq_ref,
                 wkv_ref, prefix_ref, head_ref, q_out, own_out, pieces, pair_out, other_out, quarter, stream,
                 normed, send, recv, psend, precv, wsend, wrecv, local_sem):
    core = lax.axis_index("c")
    rows = tok_ref.shape[0]
    size = qgain_ref.shape[1]
    cut = prefix_ref.shape[1] * 23 // 32
    spans = (pl.ds(0, cut), pl.ds(cut, prefix_ref.shape[1] - cut))
    y, y_ahead, y_back, y_far = ring_of("y", core)
    z, z_ahead, z_back, z_far = ring_of("z", core)
    greet(x_peers() + [dict(y=y_ahead), dict(y=y_back), dict(z=z_ahead), dict(z=z_back)])

    sent = []

    def view(part, pz, py):
        return pieces.at[pz * RING + py, spans[part]]

    def push(part, pz, py, src=None, **device):
        slot = pz * RING + py
        copy = remote(view(part, pz, py) if src is None else src, view(part, pz, py),
                      psend.at[len(sent)], precv.at[part, slot], **device)
        copy.start()
        sent.append(copy)

    def wait(part, pz, py):
        arrived(view(part, pz, py), precv.at[part, pz * RING + py])

    first = [prefix_ref.at[0, spans[part]] for part in range(2)]
    gather = Gather(stream, send, recv)
    gather.open(tok_ref)
    push(0, z, y, first[0], y=y_ahead)
    push(0, z, y, first[0], y=y_back)
    push(1, z, y, first[1], z=z_ahead)
    push(1, z, y, first[1], z=z_back)
    push(0, z, y, first[0], z=z_ahead)
    push(0, z, y, first[0], z=z_back)
    push(1, z, y, first[1], y=y_ahead)
    push(1, z, y, first[1], y=y_back)

    given = []
    part_words = pair_out.shape[2]

    def words(index):
        return head_ref.at[:, pl.ds(pl.multiple_of(index * part_words, part_words), part_words)]

    def give(index, src, dst, **device):
        copy = remote(src, dst, wsend.at[index], wrecv.at[index], **device)
        copy.start()
        given.append(copy)

    keep = [pltpu.make_async_copy(prefix_ref.at[0], pieces.at[z * RING + y], local_sem.at[0]),
            pltpu.make_async_copy(tok_ref, stream.at[2 * gather.x + core], local_sem.at[1]),
            pltpu.make_async_copy(words(y), quarter, local_sem.at[2])]
    for copy in keep:
        copy.start()

    wait(0, z, y_back)
    push(0, z, y_back, y=y_ahead)
    push(0, z, y_back, z=z_ahead)
    push(0, z, y_back, z=z_back)
    wait(1, z_back, y)
    push(1, z_back, y, z=z_ahead)
    push(1, z_back, y, y=y_ahead)
    push(1, z_back, y, y=y_back)
    wait(0, z, y_ahead)
    push(0, z, y_ahead, z=z_ahead)
    push(0, z, y_ahead, z=z_back)
    wait(1, z_ahead, y)
    push(1, z_ahead, y, y=y_ahead)
    push(1, z_ahead, y, y=y_back)
    gather.relay()
    wait(0, z, y_far)
    push(0, z, y_far, z=z_ahead)
    push(0, z, y_far, z=z_back)
    wait(1, z_far, y)
    push(1, z_far, y, y=y_ahead)
    push(1, z_far, y, y=y_back)
    give(0, words(y_ahead), pair_out.at[1], y=y_ahead)
    give(1, words(y_back), other_out, y=y_back)
    keep[2].wait()
    keep.append(pltpu.make_async_copy(quarter, pair_out.at[0], local_sem.at[3]))
    keep[3].start()

    row = lax.broadcasted_iota(jnp.int32, (rows, 1), 0)
    offset = row
    end = 0
    for r in range(requests):
        end = end + length_ref[0, r]
        offset = offset - jnp.where(row >= end, length_ref[0, r], 0)
    lane = lax.broadcasted_iota(jnp.int32, (1, size), 1)
    freq = jnp.exp((lane & (size // 2 - 1)).astype(F32) * (-2.0 * LOG_THETA / size))
    angle = (PLEN + offset).astype(F32) * freq
    cosine, sine = jnp.cos(angle), jnp.sin(angle)

    def turned(value, gain):
        value = value * lax.rsqrt(jnp.mean(value * value, axis=1, keepdims=True) + EPS) * gain
        other = jnp.concatenate([-value[:, size // 2:], value[:, : size // 2]], axis=1)
        return (value * cosine + other * sine).astype(BF16)

    keep[1].wait()
    gather.close()
    normalise(stream, gain_ref, normed)

    far_z = [(py, z_back, z_ahead) for py in (y, y_far)] + [(py, z_ahead, z_back) for py in (y_back, y_ahead)]
    far_y = [(pz, y_back, y_ahead) for pz in (z, z_far)] + [(pz, y_ahead, y_back) for pz in (z_back, z_ahead)]
    order = (0, 2, 3, 1)
    for i in order:
        py, come, go = far_z[i]
        wait(0, come, py)
        push(0, come, py, z=go)
        pz, come, go = far_y[i]
        wait(1, pz, come)
        push(1, pz, come, y=go)

    query = dot(normed[...], wq_ref[...])
    keyval = dot(normed[...], wkv_ref[...])
    heads = query.shape[1] // size
    zero = jnp.zeros((rows, size), BF16)
    for h in range(heads):
        value = turned(query[:, h * size:(h + 1) * size], qgain_ref[...])
        value = jnp.concatenate([value * jnp.asarray(scale, BF16), zero], axis=1)
        for i in range(rows // BLOCK):
            q_out[i, h * BLOCK:(h + 1) * BLOCK, :] = value[i * BLOCK:(i + 1) * BLOCK]
    own_out[...] = jnp.concatenate(
        [turned(keyval[:, :size], kgain_ref[...]), keyval[:, size:].astype(BF16)], axis=1
    )

    for py, come, go in far_z:
        wait(0, go, py)
    for pz, come, go in far_y:
        wait(1, pz, go)
    for py, come, go in far_z:
        wait(0, z_far, py)
    for pz, come, go in far_y:
        wait(1, pz, y_far)
    arrived(pair_out.at[1], wrecv.at[0])
    arrived(other_out, wrecv.at[1])
    keep[0].wait()
    keep[3].wait()
    gather.finish()
    for copy in sent + given:
        copy.wait_send()


def vmem():
    return pl.BlockSpec(memory_space=pltpu.VMEM)


def hbm():
    return pl.BlockSpec(memory_space=pl.ANY)


def smem():
    return pl.BlockSpec(memory_space=pltpu.SMEM)


def entry(lengths, tokens, attn_gain, q_gain, k_gain, w_query, w_keyval, prefix_kv, w_head):
    rows, width = tokens.shape
    size = q_gain.shape[1]
    heads = w_query.shape[1] // size
    count = RING * RING
    quarter = (w_head.shape[0], w_head.shape[1] // RING)
    return pl.pallas_call(
        functools.partial(entry_kernel, lengths.shape[1], size ** (-0.5)),
        in_specs=[smem()] + [vmem()] * 7 + [hbm()],
        out_specs=[vmem(), vmem(), hbm(), hbm(), hbm()],
        out_shape=[jax.ShapeDtypeStruct((rows // BLOCK, heads * BLOCK, 2 * size), BF16),
                   jax.ShapeDtypeStruct((rows, 2 * size), BF16),
                   jax.ShapeDtypeStruct((count,) + prefix_kv.shape[1:], BF16),
                   jax.ShapeDtypeStruct((2,) + quarter, BF16),
                   jax.ShapeDtypeStruct(quarter, BF16)],
        scratch_shapes=[pltpu.VMEM(quarter, BF16), pltpu.VMEM((8, rows, width), BF16), pltpu.VMEM((rows, 8 * width), BF16),
                        pltpu.SemaphoreType.DMA((7,)), pltpu.SemaphoreType.DMA((8,)),
                        pltpu.SemaphoreType.DMA((30,)), pltpu.SemaphoreType.DMA((2, count)),
                        pltpu.SemaphoreType.DMA((2,)), pltpu.SemaphoreType.DMA((2,)),
                        pltpu.SemaphoreType.DMA((4,))],
        compiler_params=pltpu.CompilerParams(collective_id=1, has_side_effects=True),
        cost_estimate=pl.CostEstimate(flops=30 << 30, bytes_accessed=8 << 20, transcendentals=0),
        name="entry",
    )(lengths, tokens, attn_gain, q_gain, k_gain, w_query, w_keyval, prefix_kv, w_head)


def attention_kernel(requests, split, length_ref, tenant_ref, piece_ref,
                     q_ref, own_ref, kv_ref, out_ref, best_ref, total_ref, accum_ref, slot_ref):
    block = pl.program_id(0)
    queries = q_ref[0]
    count = queries.shape[0]
    rows = own_ref.shape[0]
    size = own_ref.shape[1] // 2
    for j in range(kv_ref.shape[0]):
        slot_ref[piece_ref[j]] = j
    row = (lax.broadcasted_iota(jnp.int32, (count, 1), 0) & (BLOCK - 1)) + block * BLOCK
    col = lax.broadcasted_iota(jnp.int32, (1, rows), 1)
    row_request = jnp.zeros((count, 1), jnp.int32)
    col_request = jnp.zeros((1, rows), jnp.int32)
    ends = []
    for r in range(requests):
        ends.append(length_ref[0, r] + (ends[-1] if ends else 0))
        row_request += (row >= ends[r]).astype(jnp.int32)
        col_request += (col >= ends[r]).astype(jnp.int32)
    seen = (row_request == col_request) & (col <= row)
    own = own_ref[...]
    scores = jnp.where(seen, dot_nt(queries, own), NEG)
    best = jnp.max(scores, axis=1, keepdims=True)
    weights = jnp.where(seen, jnp.exp(scores - best), 0.0)
    best_ref[...] = best
    total_ref[...] = jnp.sum(weights, axis=1, keepdims=True)
    accum_ref[...] = dot(weights.astype(BF16), own)
    for r in range(requests):
        begin = ends[r] - length_ref[0, r]

        @pl.when((ends[r] > block * BLOCK) & (begin < block * BLOCK + BLOCK))
        def _():
            inside = row_request == r
            tenant = tenant_ref[0, r]

            old = best_ref[...]
            keyvals = [kv_ref[slot_ref[tenant * split + index]] for index in range(split)]
            parts = [dot_nt(queries, keyval) for keyval in keyvals]
            new = old
            for part in parts:
                new = jnp.maximum(new, jnp.max(part, axis=1, keepdims=True))
            new = jnp.where(inside, new, old)
            keep = jnp.exp(old - new)
            shift = jnp.where(inside, new, -NEG)
            total = total_ref[...] * keep
            accum = accum_ref[...] * keep
            for part, keyval in zip(parts, keyvals):
                piece_weights = jnp.exp(part - shift)
                total += jnp.sum(piece_weights, axis=1, keepdims=True)
                accum += dot(piece_weights.astype(BF16), keyval)
            best_ref[...], total_ref[...], accum_ref[...] = new, total, accum

    out = accum_ref[...] / total_ref[...]
    heads = [out[h * BLOCK:(h + 1) * BLOCK, size:] for h in range(count // BLOCK)]
    out_ref[...] = jnp.concatenate(heads, axis=1).astype(BF16)


def attention(lengths, tenants, prefix_piece, queries, own, pieces):
    blocks, count, width = queries.shape
    rows = own.shape[0]
    columns = count // BLOCK * width // 2
    return pl.pallas_call(
        functools.partial(attention_kernel, lengths.shape[1], pieces.shape[0] // TENANTS),
        grid=(blocks,),
        in_specs=[smem(), smem(), smem(),
                  pl.BlockSpec((1, count, width), lambda i: (i, 0, 0)),
                  pl.BlockSpec(own.shape, lambda i: (0, 0)),
                  pl.BlockSpec(pieces.shape, lambda i: (0, 0, 0), pipeline_mode=pl.Buffered(1))],
        out_specs=pl.BlockSpec((BLOCK, columns), lambda i: (i, 0)),
        out_shape=jax.ShapeDtypeStruct((rows, columns), BF16),
        scratch_shapes=[pltpu.VMEM((count, 1), F32), pltpu.VMEM((count, 1), F32),
                        pltpu.VMEM((count, width), F32), pltpu.SMEM((pieces.shape[0],), jnp.int32)],
        cost_estimate=pl.CostEstimate(flops=24 << 30, bytes_accessed=5 << 20, transcendentals=0),
        name="attention",
    )(lengths, tenants, prefix_piece, queries, own, pieces)


def finish_kernel(att_ref, tok_ref, gain_ref, wo_ref, last_gain_ref, target_ref, wg_hbm, wu_hbm, wd_hbm,
                  head_hbm, pair_hbm, other_hbm, back_hbm, ahead_hbm, out_ref, log_ref,
                  wg, wu, wd, stage, paired, inbox, stage2, paired2, inbox2, mid, normed, inner,
                  weight, hidden, logits, wanted, stat, stat_y, stat_m,
                  load, send, pair_sem, in_sem, send2, pair_sem2, in_sem2, msend, mrecv,
                  gsend, grecv, ysend, tsend, trecv, ssend, srecv, ksend, krecv,
                  zsend, zrecv, passing, wsend, wrecv, fsend, frecv):
    core = lax.axis_index("c")
    rows, width = tok_ref.shape
    depth, vocab = other_hbm.shape
    x, x_ahead, x_back, x_far = ring_of("x", core)
    y, y_ahead, y_back, y_far = ring_of("y", core)
    z, z_ahead, z_back, z_far = ring_of("z", core)
    mine = 2 * x + core
    sent = []

    def push(src, dst, send_sem, recv_sem, **device):
        copy = remote(src, dst, send_sem, recv_sem, **device)
        copy.start()
        sent.append(copy)

    def columns(index, count):
        return pl.ds(pl.multiple_of(index * count, count), count)

    def place(pz, py):
        return weight.at[columns(pz * RING + py, depth)]

    loads = []

    def fetch(src, dst):
        copy = pltpu.make_async_copy(src, dst, load.at[len(loads)])
        copy.start()
        loads.append(copy)

    fetch(wg_hbm, wg)
    fetch(wu_hbm, wu)
    fetch(wd_hbm, wd)
    fetch(head_hbm.at[:, columns(y, vocab)], place(z, y))
    fetch(pair_hbm.at[1], place(z, y_back))
    fetch(other_hbm, place(z, y_ahead))
    for i, py in enumerate((y, y_back)):
        fetch(back_hbm.at[pl.ds(i * depth, depth)], place(z_back, py))
        fetch(ahead_hbm.at[pl.ds(i * depth, depth)], place(z_ahead, py))
    rest = (y_ahead, y_far)
    others = [dict(x=lax.rem(x + i // 2, RING), c=lax.rem(core + i % 2, 2)) for i in range(1, 8)]
    greet([dict(y=y_ahead), dict(y=y_back), dict(y=y_far), dict(z=z_ahead), dict(z=z_back)] + others)

    def head_open(i, source):
        to = place(z, rest[i])
        push(source, to, zsend.at[i, 0], zrecv.at[i, 0], z=z_ahead)
        push(source, to, zsend.at[i, 1], zrecv.at[i, 1], z=z_back)

    push(head_hbm.at[:, columns(y_far, vocab)], passing, wsend.at[0], wrecv.at[0], y=y_ahead)
    head_open(0, other_hbm)
    for i, py in enumerate((y, y_back)):
        push(back_hbm.at[pl.ds(i * depth, depth)], place(z_back, py), fsend.at[i], frecv.at[i], z=z_ahead)
    for i, to in enumerate((y_ahead, y_back, y_far)):
        push(target_ref, wanted.at[y], tsend.at[i], trecv.at[i], y=to)
    wanted[y] = target_ref[...]

    def head_relay(i):
        arrived(place(z_back, rest[i]), zrecv.at[i, 0])
        push(place(z_back, rest[i]), place(z_back, rest[i]), zsend.at[i, 2], zrecv.at[i, 2], z=z_ahead)

    att = att_ref[...]
    value = scatter_sum(lambda d: dot(att, wo_ref[:, columns(d, width)]),
                        stage, paired, inbox, send, pair_sem, in_sem)
    middle = Gather(mid, msend, mrecv)
    mid[mine] = (tok_ref[...].astype(F32) + value).astype(BF16)
    middle.open()
    arrived(passing, wrecv.at[0])
    push(passing, place(z, y_back), wsend.at[1], wrecv.at[1], y=y_ahead)
    middle.relay()
    middle.close()
    normalise(mid, gain_ref, normed)
    arrived(place(z, y_far), wrecv.at[1])
    head_open(1, place(z, y_far))
    head_relay(0)
    loads[0].wait()
    loads[1].wait()
    for t in range(inner.shape[1] // width):
        tile = slice(t * width, (t + 1) * width)
        gate = dot(normed[...], wg[:, tile])
        upper = dot(normed[...], wu[:, tile])
        inner[:, tile] = (gate / (1.0 + jnp.exp(-gate)) * upper).astype(BF16)
    loads[2].wait()
    value = scatter_sum(lambda d: dot(inner[...], wd[:, columns(d, width)]),
                        stage2, paired2, inbox2, send2, pair_sem2, in_sem2)
    share = (mid[mine].astype(F32) + value).astype(BF16)
    out_ref[...] = share
    hidden[y, mine] = share

    first = Gather(hidden.at[y], gsend.at[0], grecv.at[y])
    distant = Gather(hidden.at[y_far], gsend.at[1], grecv.at[y_far])
    y_down, y_up = lax.rem(y + 3, RING), lax.rem(y + 1, RING)
    moved = []

    def hand(group, slot, **device):
        push(hidden.at[group, slot], hidden.at[group, slot], ysend.at[len(moved)], grecv.at[group, slot],
             **device)
        moved.append(slot)

    def spread(to):
        hand(y, 2 * to + core, y=y_ahead)
        hand(y, 2 * to + core, y=y_back)

    def collect(group, to):
        arrived(hidden.at[group, 2 * to + core], grecv.at[group, 2 * to + core])
        hand(group, 2 * to + core, c=1 - core)

    first.open()
    spread(x)
    arrived(hidden.at[y_back, mine], grecv.at[y_back, mine])
    hand(y_back, mine, y=y_ahead)
    first.relay()
    spread(x_back)
    spread(x_ahead)
    hand(y_back, mine, c=1 - core)
    collect(y_ahead, x)
    head_relay(1)
    first.last()
    spread(x_far)
    arrived(hidden.at[y_far, mine], grecv.at[y_far, mine])
    distant.open()
    first.rest()
    for i, group in enumerate((y_back, y_ahead, y_far)):
        arrived(wanted.at[group], trecv.at[i])
    for copy in loads[3:]:
        copy.wait()
    for i, py in enumerate((y, y_back)):
        arrived(place(z_far, py), frecv.at[i])
    for i, py in enumerate(rest):
        arrived(place(z_ahead, py), zrecv.at[i, 1])
        arrived(place(z_far, py), zrecv.at[i, 2])

    tile = 512
    eye = (lax.broadcasted_iota(jnp.int32, (rows, rows), 0)
           == lax.broadcasted_iota(jnp.int32, (rows, rows), 1))
    start = (mine * RING + y) * vocab
    column = lax.broadcasted_iota(jnp.int32, (1, vocab), 1)

    def to_row(value):
        return jnp.sum(jnp.where(eye, value, 0.0), axis=0, keepdims=True)

    for index, group in enumerate((y, y_down, y_up, y_far)):
        if index in (1, 2):
            for to in range(RING):
                slot = 2 * to + 1 - core
                arrived(hidden.at[group, slot], grecv.at[group, slot])
        if index == 3:
            distant.rest()
        normalise(hidden.at[group], last_gain_ref, normed)
        for t in range(vocab // tile):
            logits[:, t * tile:(t + 1) * tile] = dot(normed[...], weight[:, t * tile:(t + 1) * tile])
        if index == 0:
            for to in (x_back, x_ahead):
                collect(y_back, to)
                collect(y_ahead, to)
            distant.relay()
            collect(y_back, x_far)
            collect(y_ahead, x_far)
            distant.last()
        value = logits[...]
        top = jnp.max(value, axis=1, keepdims=True)
        total = jnp.sum(jnp.exp(value - top), axis=1, keepdims=True)
        target = jnp.sum(jnp.where(eye, wanted[group], 0), axis=1, keepdims=True)
        picked = jnp.sum(jnp.where(target - start == column, value, 0.0), axis=1, keepdims=True)
        stat[group, 0:1, :] = to_row(top)
        stat[group, 1:2, :] = to_row(total)
        stat[group, 2:3, :] = to_row(picked)
        if index:
            push(stat.at[group], stat_y.at[y], ssend.at[index - 1], srecv.at[y], y=group)

    stat_y[y] = stat[y]
    for group in (y_back, y_ahead, y_far):
        arrived(stat_y.at[group], srecv.at[group])

    def merge(parts, count):
        top = parts[0, 0:1, :]
        for i in range(1, count):
            top = jnp.maximum(top, parts[i, 0:1, :])
        total = jnp.zeros_like(top)
        picked = jnp.zeros_like(top)
        for i in range(count):
            total += parts[i, 1:2, :] * jnp.exp(parts[i, 0:1, :] - top)
            picked += parts[i, 2:3, :]
        return (top, total, picked)

    for i, value in enumerate(merge(stat_y, RING)):
        stat_m[mine, i:i + 1, :] = value
    for i, peer in enumerate(others):
        push(stat_m.at[mine], stat_m.at[mine], ksend.at[i], krecv.at[mine], **peer)
    for peer in others:
        slot = 2 * peer["x"] + peer["c"]
        arrived(stat_m.at[slot], krecv.at[slot])
    top, total, picked = merge(stat_m, 8)
    log_ref[...] = picked - top - jnp.log(total)
    middle.finish()
    first.finish()
    distant.finish()
    for copy in sent:
        copy.wait_send()


def finish(attended, tokens, mlp_gain, w_out, final_gain, targets, w_gate, w_up, w_down, w_head, pair, other,
           from_back, from_ahead):
    rows, width = tokens.shape
    units = w_gate.shape[1]
    block = (rows, width)
    vocab = other.shape[1]
    dma = pltpu.SemaphoreType.DMA
    stats = (8, rows)

    def blocks(n):
        return pltpu.VMEM((n,) + block, BF16)

    return pl.pallas_call(
        finish_kernel,
        in_specs=[vmem()] * 6 + [hbm()] * 8,
        out_specs=[vmem(), vmem()],
        out_shape=[jax.ShapeDtypeStruct(block, BF16), jax.ShapeDtypeStruct((1, rows), F32)],
        scratch_shapes=[pltpu.VMEM(w_gate.shape, BF16), pltpu.VMEM(w_up.shape, BF16),
                        pltpu.VMEM(w_down.shape, BF16),
                        blocks(7), blocks(4), blocks(3), blocks(7), blocks(4), blocks(3), blocks(8),
                        pltpu.VMEM((rows, 8 * width), BF16), pltpu.VMEM((rows, units), BF16),
                        pltpu.VMEM((8 * width, vocab), BF16), pltpu.VMEM((RING, 8) + block, BF16),
                        pltpu.VMEM((rows, vocab), F32),
                        pltpu.VMEM((RING, 1, rows), jnp.int32), pltpu.VMEM((RING,) + stats, F32),
                        pltpu.VMEM((RING,) + stats, F32), pltpu.VMEM((8,) + stats, F32),
                        dma((10,)), dma((7,)), dma((4,)), dma((3,)), dma((7,)), dma((4,)), dma((3,)),
                        dma((7,)), dma((8,)),
                        dma((2, 7)), dma((4, 8)), dma((17,)), dma((3,)), dma((3,)),
                        dma((3,)), dma((4,)), dma((7,)), dma((8,)), dma((2, 3)), dma((2, 3)),
                        pltpu.VMEM((w_head.shape[0], vocab), BF16), dma((2,)), dma((2,)),
                        dma((2,)), dma((2,))],
        compiler_params=pltpu.CompilerParams(collective_id=2, has_side_effects=True,
                                             vmem_limit_bytes=56 << 20),
        cost_estimate=pl.CostEstimate(flops=60 << 30, bytes_accessed=24 << 20, transcendentals=0),
        name="finish",
    )(attended, tokens, mlp_gain, w_out, final_gain, targets, w_gate, w_up, w_down, w_head, pair, other,
      from_back, from_ahead)


def results_kernel(share_ref, log_ref, share_out, log_out):
    share_out[...] = share_ref[...]
    log_out[...] = log_ref[0]


def results(share, logprob):
    return pl.pallas_call(
        results_kernel,
        in_specs=[vmem()] * 2,
        out_specs=[vmem()] * 2,
        out_shape=[jax.ShapeDtypeStruct(share.shape, BF16), jax.ShapeDtypeStruct(logprob.shape[1:], F32)],
        name="results",
    )(share, logprob)


def body(tokens, attn_gain, mlp_gain, final_gain, q_gain, k_gain, w_query, w_keyval, w_out, w_gate,
         w_up, w_down, w_head, targets, req_lengths, req_tenant, prefix_piece, prefix_kv):
    queries, own, pieces, pair, other = entry(
        req_lengths, tokens, attn_gain[None], q_gain[None], k_gain[None], w_query, w_keyval,
        prefix_kv, w_head)
    slab = pair.reshape(-1, pair.shape[2])
    ahead = [(2 * z + c, 2 * ((z + 1 + 2 * c) % RING) + c) for z in range(RING) for c in range(2)]
    from_back = lax.ppermute(slab, ("z", "c"), ahead)
    from_ahead = lax.ppermute(slab, ("z", "c"), [(b, a) for a, b in ahead])
    attended = attention(req_lengths, req_tenant, prefix_piece, queries, own, pieces)
    share, logprob = finish(attended, tokens, mlp_gain[None], w_out, final_gain[None], targets[None],
                            w_gate, w_up, w_down, w_head, pair, other, from_back, from_ahead)
    return tuple(results(share, logprob))


def solution(mesh):
    req = ("z", "y")
    mlp = ("x", "c")
    in_specs = (
        P(req, mlp), P(), P(), P(), P(), P(), P(None, mlp), P(None, mlp), P(mlp, None),
        P(None, mlp), P(None, mlp), P(mlp, None), P(req, mlp), P(req), P(req, None), P(req, None),
        P(), P(req, None, mlp),
    )
    out_specs = (P(req, mlp), P(req))
    split = Mesh(mesh.devices.reshape(RING, RING, RING, 2), ("z", "y", "x", "c"))
    return jax.shard_map(body, mesh=split, in_specs=in_specs, out_specs=out_specs, check_vma=False)
```

```python
import functools
import math

import jax
import jax.numpy as jnp
from jax import lax
from jax.experimental import pallas as pl
from jax.experimental.pallas import tpu as pltpu
from jax.sharding import Mesh
from jax.sharding import PartitionSpec as P

TENANTS = 4
PLEN = 4096
BLOCK = 64
EPS = 1e-05
LOG_THETA = math.log(1000000.0)
NEG = -1e30
RING = 4
MESH = pl.DeviceIdType.MESH
F32 = jnp.float32
BF16 = jnp.bfloat16


def dot(a, b):
    return jnp.dot(a, b, preferred_element_type=F32)


def dot_nt(a, b):
    return lax.dot_general(a, b, (((1,), (1,)), ((), ())), preferred_element_type=F32)


def remote(src, dst, send_sem, recv_sem, **device):
    return pltpu.make_async_remote_copy(
        src_ref=src, dst_ref=dst, send_sem=send_sem, recv_sem=recv_sem,
        device_id=device, device_id_type=MESH,
    )


def arrived(ref, sem):
    pltpu.make_async_copy(ref, ref, sem).wait()


def greet(peers):
    barrier = pltpu.get_barrier_semaphore()
    for peer in peers:
        pl.semaphore_signal(barrier, inc=1, device_id=peer, device_id_type=MESH)
    pl.semaphore_wait(barrier, len(peers))


def ring_of(axis, core):
    me = lax.axis_index(axis)
    ahead = lax.rem(me + 1 + 2 * core, RING)
    back = lax.rem(me + 3 + 2 * core, RING)
    far = lax.rem(me + 2, RING)
    return (me, ahead, back, far)


class Gather:
    def __init__(self, slots, send, recv):
        self.slots, self.send, self.recv, self.sent = slots, send, recv, []
        self.core = lax.axis_index("c")
        self.x, self.ahead, self.back, self.far = ring_of("x", self.core)

    def push(self, at, core, src=None, **device):
        slot = 2 * at + core
        copy = remote(self.slots.at[slot] if src is None else src, self.slots.at[slot],
                      self.send.at[len(self.sent)], self.recv.at[slot], **device)
        copy.start()
        self.sent.append(copy)

    def wait(self, at, core):
        slot = 2 * at + core
        arrived(self.slots.at[slot], self.recv.at[slot])

    def open(self, src=None):
        self.push(self.x, self.core, src, x=self.ahead)
        self.push(self.x, self.core, src, x=self.back)
        self.push(self.x, self.core, src, c=1 - self.core)

    def relay(self):
        self.wait(self.back, self.core)
        self.push(self.back, self.core, x=self.ahead)
        self.push(self.back, self.core, c=1 - self.core)
        self.wait(self.ahead, self.core)
        self.push(self.ahead, self.core, c=1 - self.core)

    def last(self):
        self.wait(self.far, self.core)
        self.push(self.far, self.core, c=1 - self.core)

    def close(self):
        self.last()
        self.rest()

    def rest(self):
        for x in (self.x, self.back, self.ahead, self.far):
            self.wait(x, 1 - self.core)

    def finish(self):
        for copy in self.sent:
            copy.wait_send()


def scatter_sum(partial, stage, paired, inbox, send, pair_sem, in_sem):
    core = lax.axis_index("c")
    x, ahead, back, far = ring_of("x", core)
    sent = []

    def push(value, dst, recv, **device):
        index = len(sent)
        stage[index] = value.astype(BF16)
        copy = remote(stage.at[index], dst, send.at[index], recv, **device)
        copy.start()
        sent.append(copy)

    def chip(to):
        mine = partial(2 * to + core)
        arrived(paired.at[to], pair_sem.at[to])
        return mine + paired[to].astype(F32)

    for to in (far, back, ahead, x):
        push(partial(2 * to + 1 - core), paired.at[to], pair_sem.at[to], c=1 - core)
    push(chip(far), inbox.at[2], in_sem.at[2], x=ahead)
    push(chip(back), inbox.at[1], in_sem.at[1], x=back)
    value = chip(ahead)
    arrived(inbox.at[2], in_sem.at[2])
    push(value + inbox[2].astype(F32), inbox.at[0], in_sem.at[0], x=ahead)
    value = chip(x)
    for slot in (1, 0):
        arrived(inbox.at[slot], in_sem.at[slot])
        value += inbox[slot].astype(F32)
    for copy in sent:
        copy.wait_send()
    return value


def normalise(blocks, gain_ref, normed):
    count, rows, width = blocks.shape
    square = jnp.zeros((rows, 1), F32)
    for m in range(count):
        value = blocks[m].astype(F32)
        square += jnp.sum(value * value, axis=1, keepdims=True)
    factor = lax.rsqrt(square / (count * width) + EPS)
    for m in range(count):
        columns = slice(m * width, (m + 1) * width)
        normed[:, columns] = (blocks[m].astype(F32) * factor * gain_ref[:, columns]).astype(BF16)


def x_peers():
    core = lax.axis_index("c")
    _, ahead, back, _ = ring_of("x", core)
    return [dict(x=ahead), dict(x=back), dict(c=1 - core)]


def entry_kernel(requests, scale, length_ref, tok_ref, gain_ref, qgain_ref, kgain_ref, wq_ref,
                 wkv_ref, prefix_ref, head_ref, q_out, own_out, pieces, pair_out, other_out, quarter, stream,
                 normed, send, recv, psend, precv, wsend, wrecv, local_sem):
    core = lax.axis_index("c")
    rows = tok_ref.shape[0]
    size = qgain_ref.shape[1]
    cut = prefix_ref.shape[1] * 23 // 32
    spans = (pl.ds(0, cut), pl.ds(cut, prefix_ref.shape[1] - cut))
    y, y_ahead, y_back, y_far = ring_of("y", core)
    z, z_ahead, z_back, z_far = ring_of("z", core)
    greet(x_peers() + [dict(y=y_ahead), dict(y=y_back), dict(z=z_ahead), dict(z=z_back)])

    sent = []

    def view(part, pz, py):
        return pieces.at[pz * RING + py, spans[part]]

    def push(part, pz, py, src=None, **device):
        slot = pz * RING + py
        copy = remote(view(part, pz, py) if src is None else src, view(part, pz, py),
                      psend.at[len(sent)], precv.at[part, slot], **device)
        copy.start()
        sent.append(copy)

    def wait(part, pz, py):
        arrived(view(part, pz, py), precv.at[part, pz * RING + py])

    first = [prefix_ref.at[0, spans[part]] for part in range(2)]
    gather = Gather(stream, send, recv)
    gather.open(tok_ref)
    push(0, z, y, first[0], y=y_ahead)
    push(0, z, y, first[0], y=y_back)
    push(1, z, y, first[1], z=z_ahead)
    push(1, z, y, first[1], z=z_back)
    push(0, z, y, first[0], z=z_ahead)
    push(0, z, y, first[0], z=z_back)
    push(1, z, y, first[1], y=y_ahead)
    push(1, z, y, first[1], y=y_back)

    given = []
    part_words = pair_out.shape[2]

    def words(index):
        return head_ref.at[:, pl.ds(pl.multiple_of(index * part_words, part_words), part_words)]

    def give(index, src, dst, **device):
        copy = remote(src, dst, wsend.at[index], wrecv.at[index], **device)
        copy.start()
        given.append(copy)

    keep = [pltpu.make_async_copy(prefix_ref.at[0], pieces.at[z * RING + y], local_sem.at[0]),
            pltpu.make_async_copy(tok_ref, stream.at[2 * gather.x + core], local_sem.at[1]),
            pltpu.make_async_copy(words(y), quarter, local_sem.at[2])]
    for copy in keep:
        copy.start()

    wait(0, z, y_back)
    push(0, z, y_back, y=y_ahead)
    push(0, z, y_back, z=z_ahead)
    push(0, z, y_back, z=z_back)
    wait(1, z_back, y)
    push(1, z_back, y, z=z_ahead)
    push(1, z_back, y, y=y_ahead)
    push(1, z_back, y, y=y_back)
    wait(0, z, y_ahead)
    push(0, z, y_ahead, z=z_ahead)
    push(0, z, y_ahead, z=z_back)
    wait(1, z_ahead, y)
    push(1, z_ahead, y, y=y_ahead)
    push(1, z_ahead, y, y=y_back)
    gather.relay()
    wait(0, z, y_far)
    push(0, z, y_far, z=z_ahead)
    push(0, z, y_far, z=z_back)
    wait(1, z_far, y)
    push(1, z_far, y, y=y_ahead)
    push(1, z_far, y, y=y_back)
    give(0, words(y_ahead), pair_out.at[1], y=y_ahead)
    give(1, words(y_back), other_out, y=y_back)
    keep[2].wait()
    keep.append(pltpu.make_async_copy(quarter, pair_out.at[0], local_sem.at[3]))
    keep[3].start()

    row = lax.broadcasted_iota(jnp.int32, (rows, 1), 0)
    offset = row
    end = 0
    for r in range(requests):
        end = end + length_ref[0, r]
        offset = offset - jnp.where(row >= end, length_ref[0, r], 0)
    lane = lax.broadcasted_iota(jnp.int32, (1, size), 1)
    freq = jnp.exp((lane & (size // 2 - 1)).astype(F32) * (-2.0 * LOG_THETA / size))
    angle = (PLEN + offset).astype(F32) * freq
    cosine, sine = jnp.cos(angle), jnp.sin(angle)

    def turned(value, gain):
        value = value * lax.rsqrt(jnp.mean(value * value, axis=1, keepdims=True) + EPS) * gain
        other = jnp.concatenate([-value[:, size // 2:], value[:, : size // 2]], axis=1)
        return (value * cosine + other * sine).astype(BF16)

    keep[1].wait()
    gather.close()
    normalise(stream, gain_ref, normed)

    far_z = [(py, z_back, z_ahead) for py in (y, y_far)] + [(py, z_ahead, z_back) for py in (y_back, y_ahead)]
    far_y = [(pz, y_back, y_ahead) for pz in (z, z_far)] + [(pz, y_ahead, y_back) for pz in (z_back, z_ahead)]
    order = (0, 2, 3, 1)
    for i in order:
        py, come, go = far_z[i]
        wait(0, come, py)
        push(0, come, py, z=go)
        pz, come, go = far_y[i]
        wait(1, pz, come)
        push(1, pz, come, y=go)

    query = dot(normed[...], wq_ref[...])
    keyval = dot(normed[...], wkv_ref[...])
    heads = query.shape[1] // size
    zero = jnp.zeros((rows, size), BF16)
    for h in range(heads):
        value = turned(query[:, h * size:(h + 1) * size], qgain_ref[...])
        value = jnp.concatenate([value * jnp.asarray(scale, BF16), zero], axis=1)
        for i in range(rows // BLOCK):
            q_out[i, h * BLOCK:(h + 1) * BLOCK, :] = value[i * BLOCK:(i + 1) * BLOCK]
    own_out[...] = jnp.concatenate(
        [turned(keyval[:, :size], kgain_ref[...]), keyval[:, size:].astype(BF16)], axis=1
    )

    for py, come, go in far_z:
        wait(0, go, py)
    for pz, come, go in far_y:
        wait(1, pz, go)
    for py, come, go in far_z:
        wait(0, z_far, py)
    for pz, come, go in far_y:
        wait(1, pz, y_far)
    arrived(pair_out.at[1], wrecv.at[0])
    arrived(other_out, wrecv.at[1])
    keep[0].wait()
    keep[3].wait()
    gather.finish()
    for copy in sent + given:
        copy.wait_send()


def vmem():
    return pl.BlockSpec(memory_space=pltpu.VMEM)


def hbm():
    return pl.BlockSpec(memory_space=pl.ANY)


def smem():
    return pl.BlockSpec(memory_space=pltpu.SMEM)


def entry(lengths, tokens, attn_gain, q_gain, k_gain, w_query, w_keyval, prefix_kv, w_head):
    rows, width = tokens.shape
    size = q_gain.shape[1]
    heads = w_query.shape[1] // size
    count = RING * RING
    quarter = (w_head.shape[0], w_head.shape[1] // RING)
    return pl.pallas_call(
        functools.partial(entry_kernel, lengths.shape[1], size ** (-0.5)),
        in_specs=[smem()] + [vmem()] * 7 + [hbm()],
        out_specs=[vmem(), vmem(), hbm(), hbm(), hbm()],
        out_shape=[jax.ShapeDtypeStruct((rows // BLOCK, heads * BLOCK, 2 * size), BF16),
                   jax.ShapeDtypeStruct((rows, 2 * size), BF16),
                   jax.ShapeDtypeStruct((count,) + prefix_kv.shape[1:], BF16),
                   jax.ShapeDtypeStruct((2,) + quarter, BF16),
                   jax.ShapeDtypeStruct(quarter, BF16)],
        scratch_shapes=[pltpu.VMEM(quarter, BF16), pltpu.VMEM((8, rows, width), BF16), pltpu.VMEM((rows, 8 * width), BF16),
                        pltpu.SemaphoreType.DMA((7,)), pltpu.SemaphoreType.DMA((8,)),
                        pltpu.SemaphoreType.DMA((30,)), pltpu.SemaphoreType.DMA((2, count)),
                        pltpu.SemaphoreType.DMA((2,)), pltpu.SemaphoreType.DMA((2,)),
                        pltpu.SemaphoreType.DMA((4,))],
        compiler_params=pltpu.CompilerParams(collective_id=1, has_side_effects=True),
        cost_estimate=pl.CostEstimate(flops=30 << 30, bytes_accessed=8 << 20, transcendentals=0),
        name="entry",
    )(lengths, tokens, attn_gain, q_gain, k_gain, w_query, w_keyval, prefix_kv, w_head)


def attention_kernel(requests, split, length_ref, tenant_ref, piece_ref,
                     q_ref, own_ref, kv_ref, out_ref, best_ref, total_ref, accum_ref, slot_ref):
    block = pl.program_id(0)
    queries = q_ref[0]
    count = queries.shape[0]
    rows = own_ref.shape[0]
    size = own_ref.shape[1] // 2
    for j in range(kv_ref.shape[0]):
        slot_ref[piece_ref[j]] = j
    row = (lax.broadcasted_iota(jnp.int32, (count, 1), 0) & (BLOCK - 1)) + block * BLOCK
    col = lax.broadcasted_iota(jnp.int32, (1, rows), 1)
    row_request = jnp.zeros((count, 1), jnp.int32)
    col_request = jnp.zeros((1, rows), jnp.int32)
    ends = []
    for r in range(requests):
        ends.append(length_ref[0, r] + (ends[-1] if ends else 0))
        row_request += (row >= ends[r]).astype(jnp.int32)
        col_request += (col >= ends[r]).astype(jnp.int32)
    seen = (row_request == col_request) & (col <= row)
    own = own_ref[...]
    scores = jnp.where(seen, dot_nt(queries, own), NEG)
    best = jnp.max(scores, axis=1, keepdims=True)
    weights = jnp.where(seen, jnp.exp(scores - best), 0.0)
    best_ref[...] = best
    total_ref[...] = jnp.sum(weights, axis=1, keepdims=True)
    accum_ref[...] = dot(weights.astype(BF16), own)
    for r in range(requests):
        begin = ends[r] - length_ref[0, r]

        @pl.when((ends[r] > block * BLOCK) & (begin < block * BLOCK + BLOCK))
        def _():
            inside = row_request == r
            tenant = tenant_ref[0, r]

            old = best_ref[...]
            keyvals = [kv_ref[slot_ref[tenant * split + index]] for index in range(split)]
            parts = [dot_nt(queries, keyval) for keyval in keyvals]
            new = old
            for part in parts:
                new = jnp.maximum(new, jnp.max(part, axis=1, keepdims=True))
            new = jnp.where(inside, new, old)
            keep = jnp.exp(old - new)
            shift = jnp.where(inside, new, -NEG)
            total = total_ref[...] * keep
            accum = accum_ref[...] * keep
            for part, keyval in zip(parts, keyvals):
                piece_weights = jnp.exp(part - shift)
                total += jnp.sum(piece_weights, axis=1, keepdims=True)
                accum += dot(piece_weights.astype(BF16), keyval)
            best_ref[...], total_ref[...], accum_ref[...] = new, total, accum

    out = accum_ref[...] / total_ref[...]
    heads = [out[h * BLOCK:(h + 1) * BLOCK, size:] for h in range(count // BLOCK)]
    out_ref[...] = jnp.concatenate(heads, axis=1).astype(BF16)


def attention(lengths, tenants, prefix_piece, queries, own, pieces):
    blocks, count, width = queries.shape
    rows = own.shape[0]
    columns = count // BLOCK * width // 2
    return pl.pallas_call(
        functools.partial(attention_kernel, lengths.shape[1], pieces.shape[0] // TENANTS),
        grid=(blocks,),
        in_specs=[smem(), smem(), smem(),
                  pl.BlockSpec((1, count, width), lambda i: (i, 0, 0)),
                  pl.BlockSpec(own.shape, lambda i: (0, 0)),
                  pl.BlockSpec(pieces.shape, lambda i: (0, 0, 0), pipeline_mode=pl.Buffered(1))],
        out_specs=pl.BlockSpec((BLOCK, columns), lambda i: (i, 0)),
        out_shape=jax.ShapeDtypeStruct((rows, columns), BF16),
        scratch_shapes=[pltpu.VMEM((count, 1), F32), pltpu.VMEM((count, 1), F32),
                        pltpu.VMEM((count, width), F32), pltpu.SMEM((pieces.shape[0],), jnp.int32)],
        cost_estimate=pl.CostEstimate(flops=24 << 30, bytes_accessed=5 << 20, transcendentals=0),
        name="attention",
    )(lengths, tenants, prefix_piece, queries, own, pieces)


def finish_kernel(att_ref, tok_ref, gain_ref, wo_ref, last_gain_ref, target_ref, wg_hbm, wu_hbm, wd_hbm,
                  head_hbm, pair_hbm, other_hbm, back_hbm, ahead_hbm, out_ref, log_ref,
                  wg, wu, wd, stage, paired, inbox, stage2, paired2, inbox2, mid, normed, inner,
                  weight, hidden, logits, wanted, stat, stat_y, stat_m,
                  load, send, pair_sem, in_sem, send2, pair_sem2, in_sem2, msend, mrecv,
                  gsend, grecv, ysend, tsend, trecv, ssend, srecv, ksend, krecv,
                  zsend, zrecv, passing, wsend, wrecv, fsend, frecv):
    core = lax.axis_index("c")
    rows, width = tok_ref.shape
    depth, vocab = other_hbm.shape
    x, x_ahead, x_back, x_far = ring_of("x", core)
    y, y_ahead, y_back, y_far = ring_of("y", core)
    z, z_ahead, z_back, z_far = ring_of("z", core)
    mine = 2 * x + core
    sent = []

    def push(src, dst, send_sem, recv_sem, **device):
        copy = remote(src, dst, send_sem, recv_sem, **device)
        copy.start()
        sent.append(copy)

    def columns(index, count):
        return pl.ds(pl.multiple_of(index * count, count), count)

    def place(pz, py):
        return weight.at[columns(pz * RING + py, depth)]

    loads = []

    def fetch(src, dst):
        copy = pltpu.make_async_copy(src, dst, load.at[len(loads)])
        copy.start()
        loads.append(copy)

    fetch(wg_hbm, wg)
    fetch(wu_hbm, wu)
    fetch(wd_hbm, wd)
    fetch(head_hbm.at[:, columns(y, vocab)], place(z, y))
    fetch(pair_hbm.at[1], place(z, y_back))
    fetch(other_hbm, place(z, y_ahead))
    for i, py in enumerate((y, y_back)):
        fetch(back_hbm.at[pl.ds(i * depth, depth)], place(z_back, py))
        fetch(ahead_hbm.at[pl.ds(i * depth, depth)], place(z_ahead, py))
    rest = (y_ahead, y_far)
    others = [dict(x=lax.rem(x + i // 2, RING), c=lax.rem(core + i % 2, 2)) for i in range(1, 8)]
    greet([dict(y=y_ahead), dict(y=y_back), dict(y=y_far), dict(z=z_ahead), dict(z=z_back)] + others)

    def head_open(i, source):
        to = place(z, rest[i])
        push(source, to, zsend.at[i, 0], zrecv.at[i, 0], z=z_ahead)
        push(source, to, zsend.at[i, 1], zrecv.at[i, 1], z=z_back)

    push(head_hbm.at[:, columns(y_far, vocab)], passing, wsend.at[0], wrecv.at[0], y=y_ahead)
    head_open(0, other_hbm)
    for i, py in enumerate((y, y_back)):
        push(back_hbm.at[pl.ds(i * depth, depth)], place(z_back, py), fsend.at[i], frecv.at[i], z=z_ahead)
    for i, to in enumerate((y_ahead, y_back, y_far)):
        push(target_ref, wanted.at[y], tsend.at[i], trecv.at[i], y=to)
    wanted[y] = target_ref[...]

    def head_relay(i):
        arrived(place(z_back, rest[i]), zrecv.at[i, 0])
        push(place(z_back, rest[i]), place(z_back, rest[i]), zsend.at[i, 2], zrecv.at[i, 2], z=z_ahead)

    att = att_ref[...]
    value = scatter_sum(lambda d: dot(att, wo_ref[:, columns(d, width)]),
                        stage, paired, inbox, send, pair_sem, in_sem)
    middle = Gather(mid, msend, mrecv)
    mid[mine] = (tok_ref[...].astype(F32) + value).astype(BF16)
    middle.open()
    arrived(passing, wrecv.at[0])
    push(passing, place(z, y_back), wsend.at[1], wrecv.at[1], y=y_ahead)
    middle.relay()
    middle.close()
    normalise(mid, gain_ref, normed)
    arrived(place(z, y_far), wrecv.at[1])
    head_open(1, place(z, y_far))
    head_relay(0)
    loads[0].wait()
    loads[1].wait()
    for t in range(inner.shape[1] // width):
        tile = slice(t * width, (t + 1) * width)
        gate = dot(normed[...], wg[:, tile])
        upper = dot(normed[...], wu[:, tile])
        inner[:, tile] = (gate / (1.0 + jnp.exp(-gate)) * upper).astype(BF16)
    loads[2].wait()
    value = scatter_sum(lambda d: dot(inner[...], wd[:, columns(d, width)]),
                        stage2, paired2, inbox2, send2, pair_sem2, in_sem2)
    share = (mid[mine].astype(F32) + value).astype(BF16)
    out_ref[...] = share
    hidden[y, mine] = share

    first = Gather(hidden.at[y], gsend.at[0], grecv.at[y])
    distant = Gather(hidden.at[y_far], gsend.at[1], grecv.at[y_far])
    y_down, y_up = lax.rem(y + 3, RING), lax.rem(y + 1, RING)
    moved = []

    def hand(group, slot, **device):
        push(hidden.at[group, slot], hidden.at[group, slot], ysend.at[len(moved)], grecv.at[group, slot],
             **device)
        moved.append(slot)

    def spread(to):
        hand(y, 2 * to + core, y=y_ahead)
        hand(y, 2 * to + core, y=y_back)

    def collect(group, to):
        arrived(hidden.at[group, 2 * to + core], grecv.at[group, 2 * to + core])
        hand(group, 2 * to + core, c=1 - core)

    first.open()
    spread(x)
    arrived(hidden.at[y_back, mine], grecv.at[y_back, mine])
    hand(y_back, mine, y=y_ahead)
    first.relay()
    spread(x_back)
    spread(x_ahead)
    hand(y_back, mine, c=1 - core)
    collect(y_ahead, x)
    head_relay(1)
    first.last()
    spread(x_far)
    arrived(hidden.at[y_far, mine], grecv.at[y_far, mine])
    distant.open()
    first.rest()
    for i, group in enumerate((y_back, y_ahead, y_far)):
        arrived(wanted.at[group], trecv.at[i])
    for copy in loads[3:]:
        copy.wait()
    for i, py in enumerate((y, y_back)):
        arrived(place(z_far, py), frecv.at[i])
    for i, py in enumerate(rest):
        arrived(place(z_ahead, py), zrecv.at[i, 1])
        arrived(place(z_far, py), zrecv.at[i, 2])

    tile = 512
    eye = (lax.broadcasted_iota(jnp.int32, (rows, rows), 0)
           == lax.broadcasted_iota(jnp.int32, (rows, rows), 1))
    start = (mine * RING + y) * vocab
    column = lax.broadcasted_iota(jnp.int32, (1, vocab), 1)

    def to_row(value):
        return jnp.sum(jnp.where(eye, value, 0.0), axis=0, keepdims=True)

    for index, group in enumerate((y, y_far, y_down, y_up)):
        if index > 1:
            for to in range(RING):
                slot = 2 * to + 1 - core
                arrived(hidden.at[group, slot], grecv.at[group, slot])
        if index == 1:
            distant.rest()
        normalise(hidden.at[group], last_gain_ref, normed)
        for t in range(vocab // tile):
            logits[:, t * tile:(t + 1) * tile] = dot(normed[...], weight[:, t * tile:(t + 1) * tile])
        if index == 0:
            for to in (x_back, x_ahead):
                collect(y_back, to)
                collect(y_ahead, to)
            distant.relay()
            collect(y_back, x_far)
            collect(y_ahead, x_far)
            distant.last()
        value = logits[...]
        top = jnp.max(value, axis=1, keepdims=True)
        total = jnp.sum(jnp.exp(value - top), axis=1, keepdims=True)
        target = jnp.sum(jnp.where(eye, wanted[group], 0), axis=1, keepdims=True)
        picked = jnp.sum(jnp.where(target - start == column, value, 0.0), axis=1, keepdims=True)
        stat[group, 0:1, :] = to_row(top)
        stat[group, 1:2, :] = to_row(total)
        stat[group, 2:3, :] = to_row(picked)
        if index:
            push(stat.at[group], stat_y.at[y], ssend.at[index - 1], srecv.at[y], y=group)

    stat_y[y] = stat[y]
    for group in (y_back, y_ahead, y_far):
        arrived(stat_y.at[group], srecv.at[group])

    def merge(parts, count):
        top = parts[0, 0:1, :]
        for i in range(1, count):
            top = jnp.maximum(top, parts[i, 0:1, :])
        total = jnp.zeros_like(top)
        picked = jnp.zeros_like(top)
        for i in range(count):
            total += parts[i, 1:2, :] * jnp.exp(parts[i, 0:1, :] - top)
            picked += parts[i, 2:3, :]
        return (top, total, picked)

    for i, value in enumerate(merge(stat_y, RING)):
        stat_m[mine, i:i + 1, :] = value
    for i, peer in enumerate(others):
        push(stat_m.at[mine], stat_m.at[mine], ksend.at[i], krecv.at[mine], **peer)
    for peer in others:
        slot = 2 * peer["x"] + peer["c"]
        arrived(stat_m.at[slot], krecv.at[slot])
    top, total, picked = merge(stat_m, 8)
    log_ref[...] = picked - top - jnp.log(total)
    middle.finish()
    first.finish()
    distant.finish()
    for copy in sent:
        copy.wait_send()


def finish(attended, tokens, mlp_gain, w_out, final_gain, targets, w_gate, w_up, w_down, w_head, pair, other,
           from_back, from_ahead):
    rows, width = tokens.shape
    units = w_gate.shape[1]
    block = (rows, width)
    vocab = other.shape[1]
    dma = pltpu.SemaphoreType.DMA
    stats = (8, rows)

    def blocks(n):
        return pltpu.VMEM((n,) + block, BF16)

    return pl.pallas_call(
        finish_kernel,
        in_specs=[vmem()] * 6 + [hbm()] * 8,
        out_specs=[vmem(), vmem()],
        out_shape=[jax.ShapeDtypeStruct(block, BF16), jax.ShapeDtypeStruct((1, rows), F32)],
        scratch_shapes=[pltpu.VMEM(w_gate.shape, BF16), pltpu.VMEM(w_up.shape, BF16),
                        pltpu.VMEM(w_down.shape, BF16),
                        blocks(7), blocks(4), blocks(3), blocks(7), blocks(4), blocks(3), blocks(8),
                        pltpu.VMEM((rows, 8 * width), BF16), pltpu.VMEM((rows, units), BF16),
                        pltpu.VMEM((8 * width, vocab), BF16), pltpu.VMEM((RING, 8) + block, BF16),
                        pltpu.VMEM((rows, vocab), F32),
                        pltpu.VMEM((RING, 1, rows), jnp.int32), pltpu.VMEM((RING,) + stats, F32),
                        pltpu.VMEM((RING,) + stats, F32), pltpu.VMEM((8,) + stats, F32),
                        dma((10,)), dma((7,)), dma((4,)), dma((3,)), dma((7,)), dma((4,)), dma((3,)),
                        dma((7,)), dma((8,)),
                        dma((2, 7)), dma((4, 8)), dma((17,)), dma((3,)), dma((3,)),
                        dma((3,)), dma((4,)), dma((7,)), dma((8,)), dma((2, 3)), dma((2, 3)),
                        pltpu.VMEM((w_head.shape[0], vocab), BF16), dma((2,)), dma((2,)),
                        dma((2,)), dma((2,))],
        compiler_params=pltpu.CompilerParams(collective_id=2, has_side_effects=True,
                                             vmem_limit_bytes=56 << 20),
        cost_estimate=pl.CostEstimate(flops=60 << 30, bytes_accessed=24 << 20, transcendentals=0),
        name="finish",
    )(attended, tokens, mlp_gain, w_out, final_gain, targets, w_gate, w_up, w_down, w_head, pair, other,
      from_back, from_ahead)


def results_kernel(share_ref, log_ref, share_out, log_out):
    share_out[...] = share_ref[...]
    log_out[...] = log_ref[0]


def results(share, logprob):
    return pl.pallas_call(
        results_kernel,
        in_specs=[vmem()] * 2,
        out_specs=[vmem()] * 2,
        out_shape=[jax.ShapeDtypeStruct(share.shape, BF16), jax.ShapeDtypeStruct(logprob.shape[1:], F32)],
        name="results",
    )(share, logprob)


def body(tokens, attn_gain, mlp_gain, final_gain, q_gain, k_gain, w_query, w_keyval, w_out, w_gate,
         w_up, w_down, w_head, targets, req_lengths, req_tenant, prefix_piece, prefix_kv):
    queries, own, pieces, pair, other = entry(
        req_lengths, tokens, attn_gain[None], q_gain[None], k_gain[None], w_query, w_keyval,
        prefix_kv, w_head)
    slab = pair.reshape(-1, pair.shape[2])
    ahead = [(2 * z + c, 2 * ((z + 1 + 2 * c) % RING) + c) for z in range(RING) for c in range(2)]
    from_back = lax.ppermute(slab, ("z", "c"), ahead)
    from_ahead = lax.ppermute(slab, ("z", "c"), [(b, a) for a, b in ahead])
    attended = attention(req_lengths, req_tenant, prefix_piece, queries, own, pieces)
    share, logprob = finish(attended, tokens, mlp_gain[None], w_out, final_gain[None], targets[None],
                            w_gate, w_up, w_down, w_head, pair, other, from_back, from_ahead)
    return tuple(results(share, logprob))


def solution(mesh):
    req = ("z", "y")
    mlp = ("x", "c")
    in_specs = (
        P(req, mlp), P(), P(), P(), P(), P(), P(None, mlp), P(None, mlp), P(mlp, None),
        P(None, mlp), P(None, mlp), P(mlp, None), P(req, mlp), P(req), P(req, None), P(req, None),
        P(), P(req, None, mlp),
    )
    out_specs = (P(req, mlp), P(req))
    split = Mesh(mesh.devices.reshape(RING, RING, RING, 2), ("z", "y", "x", "c"))
    return jax.shard_map(body, mesh=split, in_specs=in_specs, out_specs=out_specs, check_vma=False)
```
